32 devices in a mesh: tm: 8 (over z, core), space: 4 (over y, x).
Axes of the slice: x: 2, y: 2, z: 4, core: 2. Of those that a mesh axis runs over, the one named last changes fastest.
Arguments:
- snapshots: bfloat16 [4096, 1024], P('space', 'tm'), may hold values from -23 to 23
- energy: bfloat16 [32, 7, 128, 128], P('space'), may hold values from -0.375 to 0.375
- neighbours: int32 [32, 7], P('space'), may hold values from 0 to 31, as said below
- sketch: float32 [3, 256, 128], replicated, may hold values from -0.375 to 0.375
Outputs:
- modes: bfloat16 [4, 8, 4096, 128], P(None, 'tm', 'space')
The draws below stay inside these ranges and needn't reach their ends.
Inputs may be any that keep to these rules, and one draw needn't show every extreme that they name: `neighbours`: entry [b, k] lies within 2 blocks of b.
All inputs are finite; a program needn't handle non-finite values.
Results may differ from the reference program's by a relative error of at most 0.017.
Values may be sent and summed in bfloat16 or wider, within the bound.
No kernel may reach another device: no remote copies, remote signals or barrier semaphores. Data moves between devices by JAX's collectives and lax.ppermute only.
A program may use at most 64 MiB of HBM per device.

```python
import math
import jax
import jax.numpy as jnp
from jax import lax

K = 128
BLK = 128
HB = 2
LEVELS = 3
NBLK = 32
ROWS = 4096
SNAPS = 1024
N_TM = 8


def draw_snapshots(key, part):
    key_scale, key_base = jax.random.split(key, 2)
    position = jnp.arange(ROWS, dtype=jnp.float32) / ROWS
    rising = 3.0 ** (0.5 * position)
    roughness = jnp.exp(jax.random.uniform(key_scale, (ROWS,), jnp.float32, 0.0, math.log(10.0))) / 4.6
    values = jnp.clip(jax.random.normal(key_base, (ROWS, SNAPS), jnp.float32), -6.0, 6.0)
    return ((rising * roughness)[:, None] * values).astype(jnp.bfloat16)


def draw_neighbours(key, part):
    raw_offsets = jax.random.randint(key, (NBLK, 7), 0, 2 * HB)
    offsets = jnp.where(raw_offsets < HB, raw_offsets - HB, raw_offsets - HB + 1)
    own_block = jnp.arange(NBLK, dtype=jnp.int32)[:, None]
    return jnp.clip(own_block + offsets, 0, NBLK - 1).astype(jnp.int32)


def block_levels(stream_key, shape, cuts, least, top_value):
    loudness, own = 1.0, jax.random.fold_in(stream_key, 6)
    for dim, parts in cuts:
        heights = jnp.exp(jax.random.uniform(jax.random.fold_in(own, dim), (parts,), jnp.float32, least / len(cuts), top_value / len(cuts)))
        loudness = loudness * jnp.repeat(heights, shape[dim] // parts).reshape([-1 if axis == dim else 1 for axis in range(len(shape))])
    return loudness


def scatter_about(stream_key, shape, deviation, bound, pieces=(), held_as=jnp.bfloat16):
    values = deviation * jax.random.normal(stream_key, shape, jnp.float32)
    if pieces:
        values = values * block_levels(stream_key, shape, pieces, -0.22, 0.18)
    return jnp.clip(values, -bound, bound).astype(held_as)


def setup_inputs(seed: int = 0) -> dict:
    streams_of = jax.random.split(jax.random.key(seed), 5)
    return {
        "snapshots": draw_snapshots(jax.random.fold_in(streams_of[4], 71), 0),
        "energy": scatter_about(streams_of[1], (NBLK, 7, BLK, BLK), (2 * BLK) ** -0.5, 0.375, ((0, 4),)),
        "neighbours": draw_neighbours(jax.random.fold_in(streams_of[4], 71), 0),
        "sketch": scatter_about(streams_of[3], (LEVELS, 2 * K, K), (2 * K) ** -0.5, 0.375, (), jnp.float32),
    }


def energy_apply(source, energy, neighbours):
    blocks = source.reshape(NBLK, BLK, source.shape[1])
    running = 3.0 * blocks.astype(jnp.float32)
    for slot_index in range(energy.shape[1]):
        gathered = jnp.take(blocks, neighbours[:, slot_index], axis=0).astype(jnp.float32)
        running = running + jnp.einsum('nij,njw->niw', energy[:, slot_index].astype(jnp.float32), gathered)
    return running.astype(jnp.bfloat16).reshape(ROWS, source.shape[1])

def orthonormal_leaf(window, energy, neighbours):
    energy_image = energy_apply(window, energy, neighbours)
    gram_matrix = jnp.dot(energy_image.T.astype(jnp.float32), energy_image.astype(jnp.float32), preferred_element_type=jnp.float32) / ROWS
    lower_factor = jnp.linalg.cholesky(gram_matrix)
    identity = jnp.eye(K, dtype=jnp.float32)
    coefficients = jax.scipy.linalg.solve_triangular(lower_factor, identity, lower=True).T.astype(jnp.bfloat16)
    level_modes = jnp.dot(window.astype(jnp.float32), coefficients.astype(jnp.float32), preferred_element_type=jnp.float32).astype(jnp.bfloat16)
    level_image = jnp.dot(energy_image.astype(jnp.float32), coefficients.astype(jnp.float32), preferred_element_type=jnp.float32).astype(jnp.bfloat16)
    return (level_modes, level_image)

def merge_pair(joined, joined_image, sketch_level):
    gram_matrix = jnp.dot(joined_image.T.astype(jnp.float32), joined_image.astype(jnp.float32), preferred_element_type=jnp.float32) / ROWS
    columns = jnp.dot(gram_matrix, sketch_level, precision=lax.Precision.HIGHEST)
    inner_gram = jnp.dot(columns.T, jnp.dot(gram_matrix, columns, precision=lax.Precision.HIGHEST), precision=lax.Precision.HIGHEST)
    lower_factor = jnp.linalg.cholesky(inner_gram)
    coefficients = jax.scipy.linalg.solve_triangular(lower_factor, columns.T, lower=True).T.astype(jnp.bfloat16)
    level_modes = jnp.dot(joined.astype(jnp.float32), coefficients.astype(jnp.float32), preferred_element_type=jnp.float32).astype(jnp.bfloat16)
    level_image = jnp.dot(joined_image.astype(jnp.float32), coefficients.astype(jnp.float32), preferred_element_type=jnp.float32).astype(jnp.bfloat16)
    return (level_modes, level_image)

def reference(snapshots, energy, neighbours, sketch):
    windows = snapshots.reshape(ROWS, N_TM, K).transpose(1, 0, 2)
    current, images = lax.map(lambda window: orthonormal_leaf(window, energy, neighbours), windows)
    levels_kept = [current]
    for tree_level in range(LEVELS):
        joined = jnp.concatenate([current[0::2], current[1::2]], axis=2)
        joined_image = jnp.concatenate([images[0::2], images[1::2]], axis=2)
        sketch_level = sketch[tree_level]
        current, images = lax.map(lambda pair_items: merge_pair(pair_items[0], pair_items[1], sketch_level), (joined, joined_image))
        levels_kept.append(jnp.repeat(current, 2 ** (tree_level + 1), axis=0))
    return jnp.stack(levels_kept)
```

```python
import jax
import jax.numpy as jnp
from jax import lax
from jax.sharding import PartitionSpec as P

HB = 2


def padded_2(cells, sides, width):
    for axis, dim in sides:
        count = lax.axis_size(axis)
        ends = count - 1
        head = lax.slice_in_dim(cells, 0, width, axis=dim)
        tail = lax.slice_in_dim(cells, cells.shape[dim] - width, cells.shape[dim], axis=dim)
        cells = jnp.concatenate(
            [
                lax.ppermute(tail, axis, [(i, (i + 1) % count) for i in range(ends)]),
                cells,
                lax.ppermute(head, axis, [((i + 1) % count, i) for i in range(ends)]),
            ],
            axis=dim,
        )
    return cells


def from_partner(value, axis, bit):
    mask = 2**bit
    pairs = [(source, source ^ mask) for source in range(lax.axis_size(axis))]
    return lax.ppermute(value, axis, pairs)


def sum_over(value, axis):
    count = lax.axis_size(axis)
    done = 1
    while done < count:
        radix = 4 if count // done % 4 == 0 else 2
        parts = [value]
        for step in range(1, radix):
            mask = step * done
            pairs = [(source, source ^ mask) for source in range(count)]
            parts.append(lax.ppermute(value, axis, pairs))
        value = parts[0] + parts[1]
        if radix == 4:
            value = value + (parts[2] + parts[3])
        done *= radix
    return value


def blocked(matrix_rows, block_rows):
    return matrix_rows.reshape(matrix_rows.shape[0] // block_rows, block_rows, matrix_rows.shape[1])


def image_of(padded, source, energy, local_index):
    block_rows = energy.shape[2]
    running = 3.0 * blocked(source, block_rows).astype(jnp.float32)
    for slot_index in range(energy.shape[1]):
        gathered = jnp.take(padded, local_index[:, slot_index], axis=0)
        running = running + jnp.einsum(
            "nij,njw->niw", energy[:, slot_index], gathered, preferred_element_type=jnp.float32
        )
    return running.astype(jnp.bfloat16).reshape(source.shape[0], source.shape[1])


def gram_of(energy_image):
    return jnp.einsum("rc,rd->cd", energy_image, energy_image, preferred_element_type=jnp.float32)


def side_by_side(upper_half, first, second, axis_number):
    return jnp.where(
        upper_half,
        jnp.concatenate([second, first], axis_number),
        jnp.concatenate([first, second], axis_number),
    )


def on_device(snapshots, energy, neighbours, sketch):
    block_rows = energy.shape[2]
    block_count = energy.shape[0]
    rows_dev = snapshots.shape[0]
    total_rows = rows_dev * lax.axis_size("space")
    first_block = lax.axis_index("space") * block_count - HB
    local_index = neighbours - first_block
    window_index = lax.axis_index("tm")
    highest = lax.Precision.HIGHEST
    padded = padded_2(blocked(snapshots, block_rows), (("space", 0),), HB)
    energy_image = image_of(padded, snapshots, energy, local_index)
    gram_matrix = sum_over(gram_of(energy_image), "space") / total_rows
    lower_factor = jnp.linalg.cholesky(gram_matrix)
    identity = jnp.eye(snapshots.shape[1], dtype=jnp.float32)
    coefficients = jax.scipy.linalg.solve_triangular(lower_factor, identity, lower=True).T.astype(
        jnp.bfloat16
    )
    current = jnp.dot(snapshots, coefficients, preferred_element_type=jnp.float32).astype(
        jnp.bfloat16
    )
    images = jnp.dot(energy_image, coefficients, preferred_element_type=jnp.float32).astype(
        jnp.bfloat16
    )
    levels_kept = [current]
    for tree_level in range(sketch.shape[0]):
        upper_half = window_index // 2**tree_level % 2 == 1
        partner, partner_image = from_partner((current, images), "tm", tree_level)
        joined = side_by_side(upper_half, current, partner, 1)
        joined_image = side_by_side(upper_half, images, partner_image, 1)
        sketch_level = sketch[tree_level]
        gram_matrix = sum_over(gram_of(joined_image), "space") / total_rows
        columns = jnp.dot(gram_matrix, sketch_level, precision=highest)
        inner_gram = jnp.dot(
            columns.T, jnp.dot(gram_matrix, columns, precision=highest), precision=highest
        )
        lower_factor = jnp.linalg.cholesky(inner_gram)
        coefficients = jax.scipy.linalg.solve_triangular(
            lower_factor, columns.T, lower=True
        ).T.astype(jnp.bfloat16)
        new_modes = jnp.dot(joined, coefficients, preferred_element_type=jnp.float32).astype(
            jnp.bfloat16
        )
        new_image = jnp.dot(joined_image, coefficients, preferred_element_type=jnp.float32).astype(
            jnp.bfloat16
        )
        current = new_modes
        images = new_image
        levels_kept.append(current)
    return jnp.stack(levels_kept)[:, None]


def solution(mesh):
    placed = (P("space", "tm"), P("space", None, None, None), P("space", None), P())
    return jax.shard_map(
        on_device,
        mesh=mesh,
        in_specs=placed,
        out_specs=P(None, "tm", "space", None),
        check_vma=False,
    )
```

```python
import functools

import jax
import jax.numpy as jnp
from jax import lax
from jax.experimental import pallas as pl
from jax.experimental.pallas import tpu as pltpu
from jax.sharding import PartitionSpec as P

HB = 2
PANEL = 8
F32 = jnp.float32
BF16 = jnp.bfloat16


def swap(value, axis, mask):
    pairs = [(source, source ^ mask) for source in range(lax.axis_size(axis))]
    return lax.ppermute(value, axis, pairs)


def summands(value, axis):
    count = lax.axis_size(axis)
    done = 1
    parts = [value]
    while done < count:
        value = total_of(parts)
        radix = 4 if count // done % 4 == 0 else 2
        parts = [value] + [swap(value, axis, step * done) for step in range(1, radix)]
        done *= radix
    return parts


def total_of(parts):
    values = [part[...] for part in parts]
    while len(values) > 1:
        values = [a + b for a, b in zip(values[::2], values[1::2])]
    return values[0]


def dot_nn(a, b):
    return lax.dot_general(a, b, (((1,), (0,)), ((), ())), preferred_element_type=F32)


def dot_nt(a, b):
    return lax.dot_general(a, b, (((1,), (1,)), ((), ())), preferred_element_type=F32)


def dot_tn(a, b):
    return lax.dot_general(a, b, (((0,), (0,)), ((), ())), preferred_element_type=F32)


def halves_of(value):
    high = value.astype(BF16)
    return high, (value - high.astype(F32)).astype(BF16)


def full(dot, a, b):
    a_high, a_low = halves_of(a)
    b_high, b_low = halves_of(b)
    return dot(a_high, b_high) + (dot(a_high, b_low) + dot(a_low, b_high))


nn_full = functools.partial(full, dot_nn)
nt_full = functools.partial(full, dot_nt)


def inverse_factor(matrix):
    size = matrix.shape[0]
    panels = size // PANEL
    shape = (PANEL, size)
    lane = lax.broadcasted_iota(jnp.int32, shape, 1)
    sub = lax.broadcasted_iota(jnp.int32, shape, 0)

    def column(rows, index):
        return jnp.broadcast_to(rows[:, index : index + 1], shape)

    def row(rows, index):
        return jnp.broadcast_to(rows[index : index + 1, :], shape)

    rows_of = [matrix[PANEL * i : PANEL * (i + 1), :] for i in range(panels)]
    out = []
    block = [column(rows_of[0], j) for j in range(PANEL)]
    for k in range(panels):
        base = PANEL * k
        active = rows_of[k]
        ahead = (
            [column(active, base + PANEL + j) for j in range(PANEL)] if k + 1 < panels else []
        )
        here = (lane >= base) & (lane < base + PANEL)
        active = jnp.where(here, jnp.where(lane == sub + base, 1.0, 0.0), active)
        kept = active
        pivots = block[0]
        for j in range(PANEL):
            pivot = row(block[j], j)
            factor = jnp.where(sub == j, 0.0, block[j]) * (1.0 / pivot)
            kept = jnp.where(sub == j, active, kept)
            pivots = jnp.where(sub == j, pivot, pivots)
            active = active - factor * row(active, j)
            for q in range(j + 1, PANEL):
                block[q] = block[q] - factor * row(block[q], j)
            ahead = [item - factor * row(item, j) for item in ahead]
        out.append(jnp.where(lane < base + PANEL, kept * lax.rsqrt(pivots), 0.0))
        if k + 1 == panels:
            break
        scale = 1.0 / pivots
        solved = active * scale
        solved_rows = [row(solved, j) for j in range(PANEL)]
        block = []
        for i in range(k + 1, panels):
            old = rows_of[i]
            columns = [column(old, base + j) for j in range(PANEL)]
            if i == k + 1:
                for q in range(PANEL):
                    item = column(old, base + PANEL + q)
                    scaled = ahead[q] * scale
                    for j in range(PANEL):
                        item = item - columns[j] * row(scaled, j)
                    block.append(item)
            new = jnp.where(here, 0.0, old)
            for j in range(PANEL):
                new = new - columns[j] * solved_rows[j]
            rows_of[i] = new
    return jnp.concatenate(out, axis=0)


def run_kernel(body, outs, *operands):
    return pl.pallas_call(
        body,
        out_shape=outs,
        cost_estimate=pl.CostEstimate(flops=2_000_000_000, bytes_accessed=1_000_000, transcendentals=0),
    )(*operands)


def image_kernel(index_ref, energy_ref, padded_ref, image_ref, gram_ref):
    b = pl.program_id(0)
    own = padded_ref[b + HB]
    total = 3.0 * own.astype(F32)
    for slot in range(energy_ref.shape[1]):
        total = total + dot_nn(energy_ref[0, slot], padded_ref[index_ref[b, slot]])
    image = total.astype(BF16)
    image_ref[0] = image

    @pl.when(b == 0)
    def _():
        gram_ref[...] = jnp.zeros_like(gram_ref)

    gram_ref[...] += dot_tn(image, image)


def image_and_gram(local_index, energy, padded):
    blocks, slots, rows, _ = energy.shape
    width = padded.shape[2]
    grid_spec = pltpu.PrefetchScalarGridSpec(
        num_scalar_prefetch=1,
        grid=(blocks,),
        in_specs=[
            pl.BlockSpec((1, slots, rows, rows), lambda b, index: (b, 0, 0, 0)),
            pl.BlockSpec(padded.shape, lambda b, index: (0, 0, 0)),
        ],
        out_specs=[
            pl.BlockSpec((1, rows, width), lambda b, index: (b, 0, 0)),
            pl.BlockSpec((width, width), lambda b, index: (0, 0)),
        ],
    )
    image, gram = pl.pallas_call(
        image_kernel,
        out_shape=[
            jax.ShapeDtypeStruct((blocks, rows, width), BF16),
            jax.ShapeDtypeStruct((width, width), F32),
        ],
        grid_spec=grid_spec,
    )(local_index, energy, padded)
    return image.reshape(blocks * rows, width), gram


def leaf_kernel(total_rows, count, *refs):
    parts, (inverse_ref,) = refs[:count], refs[count:]
    inverse_ref[...] = inverse_factor(total_of(parts) / total_rows)


def merge(cross, sketch_own, sketch_other):
    columns_own = sketch_own + nt_full(sketch_other, cross)
    columns_other = nn_full(sketch_own, cross) + sketch_other
    image_own = columns_own + nt_full(columns_other, cross)
    image_other = nn_full(columns_own, cross) + columns_other
    inner = nt_full(columns_own, image_own) + nt_full(columns_other, image_other)
    inverse = inverse_factor(inner)
    return nn_full(inverse, columns_own), nn_full(inverse, columns_other)


def first_merge_kernel(total_rows, count, last, *refs):
    parts, refs = refs[:count], refs[count:]
    own_ref, other_ref, sketch_own, sketch_other, refs = *refs[:4], refs[4:]
    cross = nt_full(nn_full(own_ref[...], total_of(parts) / total_rows), other_ref[...])
    half_own, half_other = merge(cross, sketch_own[...], sketch_other[...])
    if not last:
        image_own, image_other, far_image, refs = *refs[:3], refs[3:]
        mine = nn_full(half_own, own_ref[...])
        theirs = nn_full(half_other, other_ref[...])
        image_t = dot_nt(mine.astype(BF16), image_own[...]) + dot_nt(
            theirs.astype(BF16), image_other[...]
        )
        image_t = image_t.astype(BF16)
        refs[2][...] = mine
        refs[3][...] = image_t
        refs[4][...] = dot_nn(image_t, far_image[...])
    refs[0][...] = half_own.astype(BF16)
    refs[1][...] = half_other.astype(BF16)


def later_merge_kernel(count, last, *refs):
    parts, refs = refs[:count], refs[count:]
    sketch_own, sketch_other, refs = *refs[:2], refs[2:]
    half_own, half_other = merge(total_of(parts), sketch_own[...], sketch_other[...])
    if not last:
        mine_ref, image_own, image_other, far_image, refs = *refs[:4], refs[4:]
        image_t = dot_nn(half_own.astype(BF16), image_own[...]) + dot_nn(
            half_other.astype(BF16), image_other[...]
        )
        image_t = image_t.astype(BF16)
        refs[2][...] = nn_full(half_own, mine_ref[...])
        refs[3][...] = image_t
        refs[4][...] = dot_nn(image_t, far_image[...])
    refs[0][...] = half_own.astype(BF16)
    refs[1][...] = half_other.astype(BF16)


def cross_kernel(total_rows, count, *refs):
    parts, (far_ref, out_ref) = refs[:count], refs[count:]
    out_ref[...] = nt_full(total_of(parts) / total_rows, far_ref[...])


def on_device(snapshots, energy, neighbours, sketch):
    block_count, _, block_rows, _ = energy.shape
    rows_dev, width = snapshots.shape
    space = lax.axis_size("space")
    total_rows = rows_dev * space
    levels = sketch.shape[0]
    window = lax.axis_index("tm")
    blocks = snapshots.reshape(block_count, block_rows, width)
    ends = space - 1
    before = lax.ppermute(blocks[-HB:], "space", [(i, i + 1) for i in range(ends)])
    after = lax.ppermute(blocks[:HB], "space", [(i + 1, i) for i in range(ends)])
    padded = jnp.concatenate([before, blocks, after], axis=0)
    local_index = neighbours - (lax.axis_index("space") * block_count - HB)
    sketch_t = jnp.swapaxes(sketch, 1, 2)

    def sketch_halves(level):
        lower, upper = sketch_t[level, :, :width], sketch_t[level, :, width:]
        is_upper = window // 2**level % 2 == 1
        return jnp.where(is_upper, upper, lower), jnp.where(is_upper, lower, upper)

    square = jax.ShapeDtypeStruct((width, width), F32)
    half = jax.ShapeDtypeStruct((width, width), BF16)
    long = jax.ShapeDtypeStruct((width, rows_dev), BF16)

    image, gram = image_and_gram(local_index, energy, padded)
    parts = summands(gram, "space")
    far_images = [swap(image, "tm", 2**level) for level in range(levels)]
    cross_parts = summands(dot_tn(image, far_images[0]), "space")
    inverse = run_kernel(
        functools.partial(leaf_kernel, total_rows, len(parts)), square, *parts
    )
    current = dot_nt(snapshots, inverse.astype(BF16)).astype(BF16)
    kept = [current]
    other_inverse = swap(inverse, "tm", 1)
    mine = image_t = None
    for level in range(levels):
        last = level + 1 == levels
        outs = [half, half] if last else [half, half, square, long, square]
        partner = swap(current, "tm", 2**level)
        halves = sketch_halves(level)
        if level == 0:
            operands = [*cross_parts, inverse, other_inverse, *halves]
            if not last:
                operands += [image, far_images[0], far_images[1]]
            body = functools.partial(first_merge_kernel, total_rows, len(cross_parts), last)
        else:
            far_mine = swap(mine, "tm", 2**level)
            if not last:
                far_image_t = swap(image_t, "tm", 2**level)
            parts = summands(probe, "space")
            cross = run_kernel(
                functools.partial(cross_kernel, total_rows, len(parts)), square, *parts, far_mine
            )
            for bit in range(level - 1):
                cross = cross + swap(cross, "tm", 2**bit)
            parts = [cross, swap(cross, "tm", 2 ** (level - 1))]
            operands = [*parts, *halves]
            if not last:
                operands += [mine, image_t, far_image_t, far_images[level + 1]]
            body = functools.partial(later_merge_kernel, len(parts), last)
        results = run_kernel(body, outs, *operands)
        half_own, half_other = results[:2]
        if not last:
            mine, image_t, probe = results[2:]
        current = (dot_nt(current, half_own) + dot_nt(partner, half_other)).astype(BF16)
        kept.append(current)
    return jnp.stack(kept)[:, None]


def solution(mesh):
    placed = (P("space", "tm"), P("space", None, None, None), P("space", None), P())
    return jax.shard_map(
        on_device,
        mesh=mesh,
        in_specs=placed,
        out_specs=P(None, "tm", "space", None),
        check_vma=False,
    )
```

```python
import functools

import jax
import jax.numpy as jnp
from jax import lax
from jax.experimental import pallas as pl
from jax.experimental.pallas import tpu as pltpu
from jax.sharding import PartitionSpec as P

HB = 2
PANEL = 8
F32 = jnp.float32
BF16 = jnp.bfloat16
PARAMS = pltpu.CompilerParams(vmem_limit_bytes=16 * 1024 * 1024)


def swap(value, axis, mask):
    pairs = [(source, source ^ mask) for source in range(lax.axis_size(axis))]
    return lax.ppermute(value, axis, pairs)


def summands(value, axis, count):
    done = 1
    parts = [value]
    while done < count:
        value = total_of(parts)
        radix = 4 if count // done % 4 == 0 else 2
        parts = [value] + [swap(value, axis, step * done) for step in range(1, radix)]
        done *= radix
    return parts


def total_of(parts):
    values = [part[...] for part in parts]
    while len(values) > 1:
        values = [a + b for a, b in zip(values[::2], values[1::2])]
    return values[0]


def dot_nn(a, b):
    return lax.dot_general(a, b, (((1,), (0,)), ((), ())), preferred_element_type=F32)


def dot_nt(a, b):
    return lax.dot_general(a, b, (((1,), (1,)), ((), ())), preferred_element_type=F32)


def split(value):
    high = value.astype(BF16)
    return high, (value - high.astype(F32)).astype(BF16)


def full(dot, axis, a, b):
    a_high, a_low = split(a)
    b_high, b_low = split(b)
    left = jnp.concatenate([a_high, a_high, a_low], axis=1)
    return dot(left, jnp.concatenate([b_high, b_low, b_high], axis=axis))


nn_full = functools.partial(full, dot_nn, 0)
nt_full = functools.partial(full, dot_nt, 1)


def inverse_factor(matrix):
    size = matrix.shape[0]
    panels = size // PANEL
    shape = (PANEL, size)
    lane = lax.broadcasted_iota(jnp.int32, shape, 1)
    sub = lax.broadcasted_iota(jnp.int32, shape, 0)

    def column(rows, index):
        return jnp.broadcast_to(rows[:, index : index + 1], shape)

    def row(rows, index):
        return jnp.broadcast_to(rows[index : index + 1, :], shape)

    rows_of = [matrix[PANEL * i : PANEL * (i + 1), :] for i in range(panels)]
    out = []
    block = [column(rows_of[0], j) for j in range(PANEL)]
    for k in range(panels):
        base = PANEL * k
        active = rows_of[k]
        ahead = (
            [column(active, base + PANEL + j) for j in range(PANEL)] if k + 1 < panels else []
        )
        here = (lane >= base) & (lane < base + PANEL)
        active = jnp.where(here, jnp.where(lane == sub + base, 1.0, 0.0), active)
        kept = active
        pivots = block[0]
        for j in range(PANEL):
            pivot = row(block[j], j)
            factor = jnp.where(sub == j, 0.0, block[j]) * (1.0 / pivot)
            kept = jnp.where(sub == j, active, kept)
            pivots = jnp.where(sub == j, pivot, pivots)
            active = active - factor * row(active, j)
            for q in range(j + 1, PANEL):
                block[q] = block[q] - factor * row(block[q], j)
            ahead = [item - factor * row(item, j) for item in ahead]
        out.append(jnp.where(lane < base + PANEL, kept * lax.rsqrt(pivots), 0.0))
        if k + 1 == panels:
            break
        scale = 1.0 / pivots
        solved = active * scale
        solved_rows = [row(solved, j) for j in range(PANEL)]
        block = []
        for i in range(k + 1, panels):
            old = rows_of[i]
            columns = [column(old, base + j) for j in range(PANEL)]
            if i == k + 1:
                for q in range(PANEL):
                    item = column(old, base + PANEL + q)
                    scaled = ahead[q] * scale
                    for j in range(PANEL):
                        item = item - columns[j] * row(scaled, j)
                    block.append(item)
            new = jnp.where(here, 0.0, old)
            for j in range(PANEL):
                new = new - columns[j] * solved_rows[j]
            rows_of[i] = new
    return jnp.concatenate(out, axis=0)


def run_kernel(body, outs, *operands):
    cost = pl.CostEstimate(flops=2_000_000_000, bytes_accessed=1_000_000, transcendentals=0)
    return pl.pallas_call(
        body, out_shape=outs, cost_estimate=cost, compiler_params=PARAMS
    )(*operands)


def coupled(energy_ref, place, slots, lookup):
    left = jnp.concatenate([energy_ref[place, slot] for slot in range(slots)], axis=1)
    right = jnp.concatenate([lookup(slot) for slot in range(slots)], axis=0)
    return dot_nn(left, right)


def interior_kernel(index_ref, energy_ref, blocks_ref, sketch_ref, image_ref, sketch_out):
    count, slots = energy_ref.shape[:2]
    first = lax.axis_index("space") * blocks_ref.shape[0]
    width = sketch_out.shape[2]
    window = lax.axis_index("tm")
    step = pl.program_id(0)
    for place in range(count):
        b = (step + 1) * count + place
        value = 3.0 * blocks_ref[b].astype(F32) + coupled(
            energy_ref, place, slots, lambda slot: blocks_ref[index_ref[b, slot] - first]
        )
        image_ref[place] = value.astype(BF16)

    @pl.when(step == 0)
    def _():
        for level in range(sketch_ref.shape[0]):
            upper = window // 2**level % 2
            for half in range(2):
                start = pl.multiple_of((upper ^ half) * width, width)
                sketch_out[level, half] = sketch_ref[level, pl.ds(start, width), :].T


def edge_kernel(
    index_ref, energy_ref, before_ref, blocks_ref, after_ref, inner_ref,
    image_ref, image_t_ref, gram_ref, padded_ref,
):
    count, slots = energy_ref.shape[:2]
    blocks = blocks_ref.shape[0]
    step = pl.program_id(0)
    first = lax.axis_index("space") * blocks - HB + step * (blocks - HB)

    @pl.when(step == 0)
    def _():
        padded_ref[:HB] = before_ref[...]
        padded_ref[HB:] = blocks_ref[: 2 * HB]
        image_ref[HB : blocks - HB] = inner_ref[...]

    @pl.when(step == 1)
    def _():
        padded_ref[: 2 * HB] = blocks_ref[blocks - 2 * HB :]
        padded_ref[2 * HB :] = after_ref[...]

    for place in range(count):
        b = step * (blocks - HB) + place
        value = 3.0 * blocks_ref[b].astype(F32) + coupled(
            energy_ref, place, slots, lambda slot: padded_ref[index_ref[b, slot] - first]
        )
        image_ref[b] = value.astype(BF16)

    @pl.when(step == 1)
    def _():
        image = image_ref[...].reshape(image_t_ref.shape[1], image_t_ref.shape[0])
        image_t = image.T
        image_t_ref[...] = image_t
        gram_ref[...] = dot_nn(image_t, image)


def images_of(neighbours, energy, before, blocks, after, sketch):
    count, slots, rows, _ = energy.shape
    width = blocks.shape[2]
    levels = sketch.shape[0]

    def whole(array):
        return pl.BlockSpec(array.shape, lambda i, index: (0,) * array.ndim)

    inner_shape = jax.ShapeDtypeStruct((count - 2 * HB, rows, width), BF16)
    sketch_shape = jax.ShapeDtypeStruct((levels, 2, width, width), F32)
    energy_block = (HB, slots, rows, rows)
    steps = count // HB
    inner, sketch_t = pl.pallas_call(
        interior_kernel,
        out_shape=[inner_shape, sketch_shape],
        grid_spec=pltpu.PrefetchScalarGridSpec(
            num_scalar_prefetch=1,
            grid=(steps - 2,),
            in_specs=[
                pl.BlockSpec(energy_block, lambda i, index: (i + 1, 0, 0, 0)),
                whole(blocks),
                whole(sketch),
            ],
            out_specs=[
                pl.BlockSpec((HB, rows, width), lambda i, index: (i, 0, 0)),
                whole(sketch_shape),
            ],
        ),
        compiler_params=PARAMS,
    )(neighbours, energy, blocks, sketch)
    outs = [
        jax.ShapeDtypeStruct((count, rows, width), BF16),
        jax.ShapeDtypeStruct((width, count * rows), BF16),
        jax.ShapeDtypeStruct((width, width), F32),
    ]
    image, image_t, gram = pl.pallas_call(
        edge_kernel,
        out_shape=outs,
        grid_spec=pltpu.PrefetchScalarGridSpec(
            num_scalar_prefetch=1,
            grid=(2,),
            in_specs=[
                pl.BlockSpec(energy_block, lambda i, index: (i * (steps - 1), 0, 0, 0)),
                whole(before),
                whole(blocks),
                whole(after),
                whole(inner),
            ],
            out_specs=[whole(item) for item in outs],
            scratch_shapes=[pltpu.VMEM((3 * HB, rows, width), BF16)],
        ),
        compiler_params=PARAMS,
    )(neighbours, energy, before, blocks, after, inner)
    return image.reshape(count * rows, width), image_t, gram, sketch_t


def pair_kernel(gram_ref, image_t_ref, other_ref, out_ref):
    width = gram_ref.shape[0]
    out_ref[:width] = gram_ref[...]
    out_ref[width:] = dot_nn(image_t_ref[...], other_ref[...])


def leaf_kernel(total_rows, count, *refs):
    parts, refs = refs[:count], refs[count:]
    snapshots_ref, inverse_ref, cross_ref, modes_ref = refs
    width = inverse_ref.shape[0]
    grams = total_of(parts) / total_rows
    cross_ref[...] = grams[width:]
    inverse = inverse_factor(grams[:width])
    inverse_ref[...] = inverse
    modes_ref[...] = dot_nt(snapshots_ref[...], inverse.astype(BF16)).astype(BF16)


def merge(cross_t, sketch_ref):
    sketch_own, sketch_other = sketch_ref[0], sketch_ref[1]
    columns_own = sketch_own + nn_full(sketch_other, cross_t)
    columns_other = nt_full(sketch_own, cross_t) + sketch_other
    image_own = columns_own + nn_full(columns_other, cross_t)
    image_other = nt_full(columns_own, cross_t) + columns_other
    inner = nt_full(
        jnp.concatenate([columns_own, columns_other], axis=1),
        jnp.concatenate([image_own, image_other], axis=1),
    )
    inverse = inverse_factor(inner)
    return nn_full(inverse, columns_own), nn_full(inverse, columns_other)


def combined(own, other, half_own, half_other):
    joined = jnp.concatenate([own, other], axis=1)
    halves = jnp.concatenate([half_own.astype(BF16), half_other.astype(BF16)], axis=1)
    return dot_nt(joined, halves).astype(BF16)


def first_merge_kernel(
    cross_ref, own_ref, other_ref, sketch_ref, modes_own, modes_other,
    image_own, image_other, far_image_t, mine_ref, probe_ref, bulk_ref,
):
    rows = modes_own.shape[0]
    cross_t = nt_full(other_ref[...], nn_full(own_ref[...], cross_ref[...]))
    half_own, half_other = merge(cross_t, sketch_ref)
    mine = nn_full(half_own, own_ref[...])
    theirs = nn_full(half_other, other_ref[...])
    mine_ref[...] = mine
    image = combined(image_own[...], image_other[...], mine, theirs)
    probe_ref[...] = dot_nn(far_image_t[...], image)
    bulk_ref[:rows] = combined(modes_own[...], modes_other[...], half_own, half_other)
    bulk_ref[rows:] = image


def later_merge_kernel(
    count, *refs,
):
    parts, refs = refs[:count], refs[count:]
    sketch_ref, old_ref, bulk_own, bulk_other, far_image_t, mine_ref, probe_ref, bulk_ref = refs
    rows = far_image_t.shape[1]
    half_own, half_other = merge(total_of(parts), sketch_ref)
    mine_ref[...] = nn_full(half_own, old_ref[...])
    image = combined(bulk_own[rows:], bulk_other[rows:], half_own, half_other)
    probe_ref[...] = dot_nn(far_image_t[...], image)
    bulk_ref[:rows] = combined(bulk_own[:rows], bulk_other[:rows], half_own, half_other)
    if bulk_ref.shape[0] > rows:
        bulk_ref[rows:] = image


def last_merge_kernel(count, *refs):
    parts, refs = refs[:count], refs[count:]
    sketch_ref, own_ref, other_ref, refs = *refs[:3], refs[3:]
    *earlier, out_ref = refs
    half_own, half_other = merge(total_of(parts), sketch_ref)
    rows = out_ref.shape[1]
    for level, modes_ref in enumerate(earlier):
        out_ref[level] = modes_ref[:rows]
    out_ref[len(earlier)] = own_ref[:rows]
    out_ref[len(earlier) + 1] = combined(
        own_ref[:rows], other_ref[:rows], half_own, half_other
    )


def cross_kernel(total_rows, count, *refs):
    parts, (far_ref, out_ref) = refs[:count], refs[count:]
    out_ref[...] = nn_full(far_ref[...], total_of(parts) / total_rows)


def on_device(snapshots, energy, neighbours, sketch):
    block_count, _, block_rows, _ = energy.shape
    rows_dev, width = snapshots.shape
    space = lax.axis_size("space")
    total_rows = rows_dev * space
    levels = sketch.shape[0]
    blocks = snapshots.reshape(block_count, block_rows, width)
    ends = space - 1
    before = lax.ppermute(blocks[-HB:], "space", [(i, i + 1) for i in range(ends)])
    after = lax.ppermute(blocks[:HB], "space", [(i + 1, i) for i in range(ends)])
    square = jax.ShapeDtypeStruct((width, width), F32)

    image, image_t, gram, sketch_t = images_of(
        neighbours, energy, before, blocks, after, sketch
    )
    other_image = swap(image, "tm", 1)
    pair = run_kernel(
        pair_kernel,
        jax.ShapeDtypeStruct((2 * width, width), F32),
        gram, image_t, other_image,
    )
    parts = summands(pair, "space", space)
    far_images = [swap(image_t, "tm", 2**level) for level in range(1, levels)]
    modes_shape = jax.ShapeDtypeStruct((rows_dev, width), BF16)
    inverse, cross, current = run_kernel(
        functools.partial(leaf_kernel, total_rows, len(parts)),
        [square, square, modes_shape],
        *parts, snapshots,
    )
    other_inverse = swap(inverse, "tm", 1)
    other = swap(current, "tm", 1)
    kept = [current]
    for level in range(levels):
        bulk_shape = jax.ShapeDtypeStruct(
            (rows_dev * (2 if level + 2 < levels else 1), width), BF16
        )
        outs = [square, square, bulk_shape]
        if level == 0:
            mine, probe, current = run_kernel(
                first_merge_kernel, outs,
                cross, inverse, other_inverse, sketch_t[level],
                current, other, image, other_image, far_images[level],
            )
        else:
            far_mine = swap(mine, "tm", 2**level)
            parts = summands(probe, "space", space)
            other = swap(current, "tm", 2**level)
            cross = run_kernel(
                functools.partial(cross_kernel, total_rows, len(parts)), square, *parts, far_mine
            )
            parts = summands(cross, "tm", 2**level)
            if level + 1 < levels:
                mine, probe, current = run_kernel(
                    functools.partial(later_merge_kernel, len(parts)), outs,
                    *parts, sketch_t[level], mine, current, other, far_images[level],
                )
            else:
                out = run_kernel(
                    functools.partial(last_merge_kernel, len(parts)),
                    jax.ShapeDtypeStruct((levels + 1, rows_dev, width), BF16),
                    *parts, sketch_t[level], current, other, *kept[:-1],
                )
        kept.append(current)
    return out[:, None]


def solution(mesh):
    placed = (P("space", "tm"), P("space", None, None, None), P("space", None), P())
    return jax.shard_map(
        on_device,
        mesh=mesh,
        in_specs=placed,
        out_specs=P(None, "tm", "space", None),
        check_vma=False,
    )
```

```python
import functools

import jax
import jax.numpy as jnp
from jax import lax
from jax.experimental import pallas as pl
from jax.experimental.pallas import tpu as pltpu
from jax.sharding import PartitionSpec as P


HB = 2
PANEL = 8
F32 = jnp.float32
BF16 = jnp.bfloat16
PARAMS = pltpu.CompilerParams(vmem_limit_bytes=16 * 1024 * 1024)
WIDE = pltpu.CompilerParams(vmem_limit_bytes=62_000_000)


def swap(value, axis, mask):
    pairs = [(source, source ^ mask) for source in range(lax.axis_size(axis))]
    return lax.ppermute(value, axis, pairs)


def summands(value, axis, count, widest):
    done = 1
    parts = [value]
    while done < count:
        if len(parts) > 1:
            value = run_kernel(add_kernel, jax.ShapeDtypeStruct(value.shape, F32), *parts)
        radix = 4 if widest == 4 and count // done % 4 == 0 else 2
        parts = [value]
        for step in range(1, radix):
            parts.append(swap(value, axis, step * done))
        done *= radix
    return parts


def add_kernel(*refs):
    refs[-1][...] = total_of(refs[:-1])


def total_of(parts):
    values = [part[...] for part in parts]
    while len(values) > 1:
        values = [a + b for a, b in zip(values[::2], values[1::2])]
    return values[0]


def dot_nn(a, b):
    return lax.dot_general(a, b, (((1,), (0,)), ((), ())), preferred_element_type=F32)


def dot_nt(a, b):
    return lax.dot_general(a, b, (((1,), (1,)), ((), ())), preferred_element_type=F32)


def split(value):
    high = value.astype(BF16)
    return high, (value - high.astype(F32)).astype(BF16)


def full(dot, axis, a, b):
    a_high, a_low = split(a)
    b_high, b_low = split(b)
    left = jnp.concatenate([a_high, a_high, a_low], axis=1)
    return dot(left, jnp.concatenate([b_high, b_low, b_high], axis=axis))


nn_full = functools.partial(full, dot_nn, 0)
nt_full = functools.partial(full, dot_nt, 1)


def inverse_factor(matrix):
    size = matrix.shape[0]
    panels = size // PANEL
    shape = (PANEL, size)
    lane = lax.broadcasted_iota(jnp.int32, shape, 1)
    sub = lax.broadcasted_iota(jnp.int32, shape, 0)

    def column(rows, index):
        return jnp.broadcast_to(rows[:, index : index + 1], shape)

    def row(rows, index):
        return jnp.broadcast_to(rows[index : index + 1, :], shape)

    rows_of = [matrix[PANEL * i : PANEL * (i + 1), :] for i in range(panels)]
    out = []
    block = [column(rows_of[0], j) for j in range(PANEL)]
    for k in range(panels):
        base = PANEL * k
        active = rows_of[k]
        ahead = (
            [column(active, base + PANEL + j) for j in range(PANEL)] if k + 1 < panels else []
        )
        here = (lane >= base) & (lane < base + PANEL)
        active = jnp.where(here, jnp.where(lane == sub + base, 1.0, 0.0), active)
        kept = active
        pivots = block[0]
        for j in range(PANEL):
            pivot = row(block[j], j)
            factor = jnp.where(sub == j, 0.0, block[j]) * (1.0 / pivot)
            kept = jnp.where(sub == j, active, kept)
            pivots = jnp.where(sub == j, pivot, pivots)
            active = active - factor * row(active, j)
            for q in range(j + 1, PANEL):
                block[q] = block[q] - factor * row(block[q], j)
            ahead = [item - factor * row(item, j) for item in ahead]
        out.append(jnp.where(lane < base + PANEL, kept * lax.rsqrt(pivots), 0.0))
        if k + 1 == panels:
            break
        scale = 1.0 / pivots
        solved = active * scale
        solved_rows = [row(solved, j) for j in range(PANEL)]
        block = []
        for i in range(k + 1, panels):
            old = rows_of[i]
            columns = [column(old, base + j) for j in range(PANEL)]
            if i == k + 1:
                for q in range(PANEL):
                    item = column(old, base + PANEL + q)
                    scaled = ahead[q] * scale
                    for j in range(PANEL):
                        item = item - columns[j] * row(scaled, j)
                    block.append(item)
            new = jnp.where(here, 0.0, old)
            for j in range(PANEL):
                new = new - columns[j] * solved_rows[j]
            rows_of[i] = new
    return jnp.concatenate(out, axis=0)


def run_kernel(body, outs, *operands):
    cost = pl.CostEstimate(flops=2_000_000_000, bytes_accessed=1_000_000, transcendentals=0)
    return pl.pallas_call(
        body, out_shape=outs, cost_estimate=cost, compiler_params=PARAMS
    )(*operands)


def coupled(energy_ref, place, slots, lookup):
    left = jnp.concatenate([energy_ref[place, slot] for slot in range(slots)], axis=1)
    right = jnp.concatenate([lookup(slot) for slot in range(slots)], axis=0)
    return dot_nn(left, right)


def interior_kernel(
    index_hbm, energy_hbm, blocks_hbm, sketch_hbm,
    image_ref, sketch_out, edges_ref, blocks_ref, index_ref, energy_ref, sketch_ref, sems,
):
    count = blocks_ref.shape[0]
    inner, slots = energy_ref.shape[:2]
    width = sketch_out.shape[2]
    copies = [
        pltpu.make_async_copy(source, target, sems.at[place])
        for place, (source, target) in enumerate(
            [
                (index_hbm, index_ref),
                (blocks_hbm, blocks_ref),
                (energy_hbm.at[pl.ds(HB, inner)], energy_ref),
                (sketch_hbm, sketch_ref),
                (energy_hbm.at[pl.ds(0, HB)], edges_ref.at[0]),
                (energy_hbm.at[pl.ds(count - HB, HB)], edges_ref.at[1]),
            ]
        )
    ]
    for copy in copies:
        copy.start()
    first = lax.axis_index("space") * count
    window = lax.axis_index("tm")
    for copy in copies[:3]:
        copy.wait()
    for place in range(inner):
        b = HB + place
        value = 3.0 * blocks_ref[b].astype(F32) + coupled(
            energy_ref, place, slots, lambda slot: blocks_ref[index_ref[b, slot] - first]
        )
        image_ref[place] = value.astype(BF16)
    copies[3].wait()
    for level in range(sketch_ref.shape[0]):
        upper = window // 2**level % 2
        for half in range(2):
            start = pl.multiple_of((upper ^ half) * width, width)
            sketch_out[level, half] = sketch_ref[level, pl.ds(start, width), :].T
    for copy in copies[4:]:
        copy.wait()


def edge_kernel(
    index_ref, edges_ref, before_ref, blocks_ref, after_ref, inner_ref,
    image_ref, image_t_ref, gram_ref, padded_ref,
):
    slots = edges_ref.shape[2]
    blocks = blocks_ref.shape[0]
    padded_ref[0, :HB] = before_ref[...]
    padded_ref[0, HB:] = blocks_ref[: 2 * HB]
    padded_ref[1, : 2 * HB] = blocks_ref[blocks - 2 * HB :]
    padded_ref[1, 2 * HB :] = after_ref[...]
    image_ref[HB : blocks - HB] = inner_ref[...]
    for side in range(2):
        first = lax.axis_index("space") * blocks - HB + side * (blocks - HB)
        for place in range(HB):
            b = side * (blocks - HB) + place
            value = 3.0 * blocks_ref[b].astype(F32) + coupled(
                edges_ref.at[side], place, slots,
                lambda slot: padded_ref[side, index_ref[b, slot] - first],
            )
            image_ref[b] = value.astype(BF16)
    image = image_ref[...].reshape(image_t_ref.shape[1], image_t_ref.shape[0])
    image_t = image.T
    image_t_ref[...] = image_t
    gram_ref[...] = dot_nn(image_t, image)


def interior_of(neighbours, energy, blocks, sketch):
    count, slots, rows, _ = energy.shape
    width = blocks.shape[2]
    levels = sketch.shape[0]
    inner = count - 2 * HB
    return pl.pallas_call(
        interior_kernel,
        out_shape=[
            jax.ShapeDtypeStruct((inner, rows, width), BF16),
            jax.ShapeDtypeStruct((levels, 2, width, width), F32),
            jax.ShapeDtypeStruct((2, HB, slots, rows, rows), BF16),
            jax.ShapeDtypeStruct(blocks.shape, BF16),
        ],
        in_specs=[pl.BlockSpec(memory_space=pltpu.HBM)] * 4,
        scratch_shapes=[
            pltpu.SMEM(neighbours.shape, jnp.int32),
            pltpu.VMEM((inner, slots, rows, rows), BF16),
            pltpu.VMEM(sketch.shape, F32),
            pltpu.SemaphoreType.DMA((6,)),
        ],
        compiler_params=WIDE,
    )(neighbours, energy, blocks, sketch)


def edge_of(neighbours, edges, before, blocks, after, inner):
    count, rows, width = blocks.shape
    image, image_t, gram = pl.pallas_call(
        edge_kernel,
        out_shape=[
            jax.ShapeDtypeStruct((count, rows, width), BF16),
            jax.ShapeDtypeStruct((width, count * rows), BF16),
            jax.ShapeDtypeStruct((width, width), F32),
        ],
        in_specs=[pl.BlockSpec(memory_space=pltpu.SMEM)]
        + [pl.BlockSpec(memory_space=pltpu.VMEM)] * 5,
        scratch_shapes=[pltpu.VMEM((2, 3 * HB, rows, width), BF16)],
        compiler_params=PARAMS,
    )(neighbours, edges, before, blocks, after, inner)
    return image.reshape(count * rows, width), image_t, gram


def pair_kernel(gram_ref, image_t_ref, other_ref, out_ref):
    width = gram_ref.shape[0]
    out_ref[:width] = gram_ref[...]
    out_ref[width:] = dot_nn(image_t_ref[...], other_ref[...])


def leaf_kernel(total_rows, count, *refs):
    parts, refs = refs[:count], refs[count:]
    snapshots_ref, inverse_ref, cross_ref, modes_ref = refs
    width = inverse_ref.shape[0]
    grams = total_of(parts) / total_rows
    cross_ref[...] = grams[width:]
    inverse = inverse_factor(grams[:width])
    inverse_ref[...] = inverse
    modes_ref[...] = dot_nt(snapshots_ref[...], inverse.astype(BF16)).astype(BF16)


def merge(cross_t, sketch_ref):
    sketch_own, sketch_other = sketch_ref[0], sketch_ref[1]
    columns_own = sketch_own + nn_full(sketch_other, cross_t)
    columns_other = nt_full(sketch_own, cross_t) + sketch_other
    image_own = columns_own + nn_full(columns_other, cross_t)
    image_other = nt_full(columns_own, cross_t) + columns_other
    inner = nt_full(
        jnp.concatenate([columns_own, columns_other], axis=1),
        jnp.concatenate([image_own, image_other], axis=1),
    )
    inverse = inverse_factor(inner)
    return nn_full(inverse, columns_own), nn_full(inverse, columns_other)


def combined(own, other, half_own, half_other):
    joined = jnp.concatenate([own, other], axis=1)
    halves = jnp.concatenate([half_own.astype(BF16), half_other.astype(BF16)], axis=1)
    return dot_nt(joined, halves).astype(BF16)


def choose(first, second):
    odd = lax.axis_index("tm") % 2 == 1
    return jnp.where(odd, second, first), jnp.where(odd, first, second)


def write_bulk(refs, modes, image):
    modes_ref, *image_ref, outgoing_ref = refs
    modes_ref[...] = modes
    if image_ref:
        image_ref[0][...] = image
        outgoing_ref[...] = choose(modes, image)[0]
    else:
        part = outgoing_ref.shape[0]
        outgoing_ref[...] = choose(modes[:part], modes[part:])[0]


def read_modes(came_ref, shared_ref, rows):
    first, second = choose(came_ref[...], shared_ref[...])
    if first.shape[0] == rows:
        return first
    return jnp.concatenate([first, second], axis=0)


def first_merge_kernel(
    cross_ref, own_ref, other_ref, sketch_ref, modes_own, modes_other,
    image_own, image_other, far_image_t, mine_ref, probe_ref, *bulk_refs,
):
    cross_t = nt_full(other_ref[...], nn_full(own_ref[...], cross_ref[...]))
    half_own, half_other = merge(cross_t, sketch_ref)
    mine = nn_full(half_own, own_ref[...])
    theirs = nn_full(half_other, other_ref[...])
    mine_ref[...] = mine
    image = combined(image_own[...], image_other[...], mine, theirs)
    probe_ref[...] = dot_nn(far_image_t[...], image)
    modes = combined(modes_own[...], modes_other[...], half_own, half_other)
    write_bulk(bulk_refs, modes, image)


def merge_kernel(count, *refs):
    parts, (sketch_ref, old_ref, halves_ref, mine_ref) = refs[:count], refs[count:]
    half_own, half_other = merge(total_of(parts), sketch_ref)
    halves_ref[0] = half_own.astype(BF16)
    halves_ref[1] = half_other.astype(BF16)
    mine_ref[...] = nn_full(half_own, old_ref[...])


def apply_kernel(
    halves_ref, modes_own, image_own, came_ref, shared_ref, far_image_t, probe_ref, *bulk_refs
):
    modes_other, image_other = choose(came_ref[...], shared_ref[...])
    image = combined(image_own[...], image_other, halves_ref[0], halves_ref[1])
    probe_ref[...] = dot_nn(far_image_t[...], image)
    modes = combined(modes_own[...], modes_other, halves_ref[0], halves_ref[1])
    write_bulk(bulk_refs, modes, image)


def output_kernel(halves_ref, came_ref, shared_ref, *refs):
    *earlier, out_ref = refs
    for level, modes_ref in enumerate(earlier):
        out_ref[level] = modes_ref[...]
    modes_other = read_modes(came_ref, shared_ref, out_ref.shape[1])
    out_ref[len(earlier)] = combined(
        earlier[-1][...], modes_other, halves_ref[0], halves_ref[1]
    )


def cross_kernel(total_rows, count, *refs):
    parts, (far_ref, out_ref) = refs[:count], refs[count:]
    out_ref[...] = nn_full(far_ref[...], total_of(parts) / total_rows)


def modes_of(snapshots, energy, neighbours, sketch):
    block_count, _, block_rows, _ = energy.shape
    rows_dev, width = snapshots.shape
    space = lax.axis_size("space")
    total_rows = rows_dev * space
    levels = sketch.shape[0]
    blocks = snapshots.reshape(block_count, block_rows, width)
    ends = space - 1
    before = lax.ppermute(blocks[-HB:], "space", [(i, i + 1) for i in range(ends)])
    after = lax.ppermute(blocks[:HB], "space", [(i + 1, i) for i in range(ends)])
    square = jax.ShapeDtypeStruct((width, width), F32)
    modes_shape = jax.ShapeDtypeStruct((rows_dev, width), BF16)
    half_shape = jax.ShapeDtypeStruct((rows_dev // 2, width), BF16)
    halves_shape = jax.ShapeDtypeStruct((2, width, width), BF16)

    inner, sketch_t, edges, blocks = interior_of(neighbours, energy, blocks, sketch)
    image, image_t, gram = edge_of(neighbours, edges, before, blocks, after, inner)
    other_image = swap(image, "tm", 1)
    pair = run_kernel(
        pair_kernel,
        jax.ShapeDtypeStruct((2 * width, width), F32),
        gram, image_t, other_image,
    )
    parts = summands(pair, "space", space, 4)
    far_images = [swap(image_t, "tm", 2**level) for level in range(1, levels)]
    inverse, cross, modes = run_kernel(
        functools.partial(leaf_kernel, total_rows, len(parts)),
        [square, square, modes_shape],
        *parts, blocks.reshape(rows_dev, width),
    )
    other_inverse = swap(inverse, "tm", 1)
    other = swap(modes, "tm", 1)
    kept = [modes]
    for level in range(levels):
        deep = level + 2 < levels
        outs = [square, square, modes_shape] + ([modes_shape] * 2 if deep else [half_shape])
        if level == 0:
            mine, probe, *bulk = run_kernel(
                first_merge_kernel, outs,
                cross, inverse, other_inverse, sketch_t[level],
                modes, other, image, other_image, far_images[level],
            )
        else:
            far_mine = swap(mine, "tm", 2**level)
            parts = summands(probe, "space", space, 4)
            came = swap(bulk[-1], "tm", 2**level)
            shared = swap(came, "tm", 1)
            cross = run_kernel(
                functools.partial(cross_kernel, total_rows, len(parts)),
                square, *parts, far_mine,
            )
            parts = summands(cross, "tm", 2**level, 2)
            halves, mine = run_kernel(
                functools.partial(merge_kernel, len(parts)), [halves_shape, square],
                *parts, sketch_t[level], mine,
            )
            if level + 1 < levels:
                probe, *bulk = run_kernel(
                    apply_kernel, outs[1:],
                    halves, *bulk[:2], came, shared, far_images[level],
                )
            else:
                out = run_kernel(
                    output_kernel,
                    jax.ShapeDtypeStruct((levels + 1, rows_dev, width), BF16),
                    halves, came, shared, *kept,
                )
        kept.append(bulk[0])
    return out[:, None]


def solution(mesh):
    placed = (P("space", "tm"), P("space", None, None, None), P("space", None), P())
    return jax.shard_map(
        modes_of,
        mesh=mesh,
        in_specs=placed,
        out_specs=P(None, "tm", "space", None),
        check_vma=False,
    )
```

```python
import functools

import jax
import jax.numpy as jnp
from jax import lax
from jax.experimental import pallas as pl
from jax.experimental.pallas import tpu as pltpu
from jax.sharding import PartitionSpec as P


HB = 2
PANEL = 8
F32 = jnp.float32
BF16 = jnp.bfloat16
PARAMS = pltpu.CompilerParams(vmem_limit_bytes=16 * 1024 * 1024)


def swap(value, axis, mask):
    pairs = [(source, source ^ mask) for source in range(lax.axis_size(axis))]
    return lax.ppermute(value, axis, pairs)


def summands(value, axis, count, widest):
    done = 1
    parts = [value]
    while done < count:
        if len(parts) > 1:
            value = run_kernel(add_kernel, jax.ShapeDtypeStruct(value.shape, F32), *parts)
        radix = 4 if widest == 4 and count // done % 4 == 0 else 2
        parts = [value]
        for step in range(1, radix):
            parts.append(swap(value, axis, step * done))
        done *= radix
    return parts


def add_kernel(*refs):
    refs[-1][...] = total_of(refs[:-1])


def total_of(parts):
    values = [part[...] for part in parts]
    while len(values) > 1:
        values = [a + b for a, b in zip(values[::2], values[1::2])]
    return values[0]


def dot_nn(a, b):
    return lax.dot_general(a, b, (((1,), (0,)), ((), ())), preferred_element_type=F32)


def dot_nt(a, b):
    return lax.dot_general(a, b, (((1,), (1,)), ((), ())), preferred_element_type=F32)


def split(value):
    high = value.astype(BF16)
    return high, (value - high.astype(F32)).astype(BF16)


def full(dot, axis, a, b):
    a_high, a_low = split(a)
    b_high, b_low = split(b)
    left = jnp.concatenate([a_high, a_high, a_low], axis=1)
    return dot(left, jnp.concatenate([b_high, b_low, b_high], axis=axis))


nn_full = functools.partial(full, dot_nn, 0)
nt_full = functools.partial(full, dot_nt, 1)


def inverse_factor(matrix):
    size = matrix.shape[0]
    panels = size // PANEL
    shape = (PANEL, size)
    lane = lax.broadcasted_iota(jnp.int32, shape, 1)
    sub = lax.broadcasted_iota(jnp.int32, shape, 0)

    def column(rows, index):
        return jnp.broadcast_to(rows[:, index : index + 1], shape)

    def row(rows, index):
        return jnp.broadcast_to(rows[index : index + 1, :], shape)

    rows_of = [matrix[PANEL * i : PANEL * (i + 1), :] for i in range(panels)]
    out = []
    block = [column(rows_of[0], j) for j in range(PANEL)]
    for k in range(panels):
        base = PANEL * k
        active = rows_of[k]
        ahead = (
            [column(active, base + PANEL + j) for j in range(PANEL)] if k + 1 < panels else []
        )
        here = (lane >= base) & (lane < base + PANEL)
        active = jnp.where(here, jnp.where(lane == sub + base, 1.0, 0.0), active)
        kept = active
        pivots = block[0]
        for j in range(PANEL):
            pivot = row(block[j], j)
            factor = jnp.where(sub == j, 0.0, block[j]) * (1.0 / pivot)
            kept = jnp.where(sub == j, active, kept)
            pivots = jnp.where(sub == j, pivot, pivots)
            active = active - factor * row(active, j)
            for q in range(j + 1, PANEL):
                block[q] = block[q] - factor * row(block[q], j)
            ahead = [item - factor * row(item, j) for item in ahead]
        out.append(jnp.where(lane < base + PANEL, kept * lax.rsqrt(pivots), 0.0))
        if k + 1 == panels:
            break
        scale = 1.0 / pivots
        solved = active * scale
        solved_rows = [row(solved, j) for j in range(PANEL)]
        block = []
        for i in range(k + 1, panels):
            old = rows_of[i]
            columns = [column(old, base + j) for j in range(PANEL)]
            if i == k + 1:
                for q in range(PANEL):
                    item = column(old, base + PANEL + q)
                    scaled = ahead[q] * scale
                    for j in range(PANEL):
                        item = item - columns[j] * row(scaled, j)
                    block.append(item)
            new = jnp.where(here, 0.0, old)
            for j in range(PANEL):
                new = new - columns[j] * solved_rows[j]
            rows_of[i] = new
    return jnp.concatenate(out, axis=0)


def run_kernel(body, outs, *operands):
    cost = pl.CostEstimate(flops=2_000_000_000, bytes_accessed=1_000_000, transcendentals=0)
    return pl.pallas_call(
        body, out_shape=outs, cost_estimate=cost, compiler_params=PARAMS
    )(*operands)


def coupled(energy_ref, place, slots, lookup):
    left = jnp.concatenate([energy_ref[place, slot] for slot in range(slots)], axis=1)
    right = jnp.concatenate([lookup(slot) for slot in range(slots)], axis=0)
    return dot_nn(left, right)


def interior_kernel(
    index_hbm, energy_hbm, blocks_hbm, sketch_hbm,
    image_ref, sketch_out, edges_ref, blocks_ref, index_ref, energy_ref, sketch_ref, sems,
):
    count = blocks_ref.shape[0]
    inner, slots = energy_ref.shape[:2]
    width = sketch_out.shape[2]
    copies = [
        pltpu.make_async_copy(source, target, sems.at[place])
        for place, (source, target) in enumerate(
            [
                (index_hbm, index_ref),
                (blocks_hbm, blocks_ref),
                (energy_hbm.at[pl.ds(HB, inner)], energy_ref),
                (sketch_hbm, sketch_ref),
                (energy_hbm.at[pl.ds(0, HB)], edges_ref.at[0]),
                (energy_hbm.at[pl.ds(count - HB, HB)], edges_ref.at[1]),
            ]
        )
    ]
    for copy in copies:
        copy.start()
    first = lax.axis_index("space") * count
    window = lax.axis_index("tm")
    for copy in copies[:3]:
        copy.wait()
    for place in range(inner):
        b = HB + place
        value = 3.0 * blocks_ref[b].astype(F32) + coupled(
            energy_ref, place, slots, lambda slot: blocks_ref[index_ref[b, slot] - first]
        )
        image_ref[place] = value.astype(BF16)
    copies[3].wait()
    for level in range(sketch_ref.shape[0]):
        upper = window // 2**level % 2
        for half in range(2):
            start = pl.multiple_of((upper ^ half) * width, width)
            sketch_out[level, half] = sketch_ref[level, pl.ds(start, width), :].T
    for copy in copies[4:]:
        copy.wait()


def edge_kernel(
    index_ref, edges_ref, near_ref, blocks_ref, wide_ref, inner_ref,
    image_ref, image_t_ref, gram_ref, padded_ref,
):
    slots = edges_ref.shape[2]
    blocks = blocks_ref.shape[0]
    before, after = choose("space", wide_ref[...], near_ref[...])
    padded_ref[0, :HB] = before
    padded_ref[0, HB:] = blocks_ref[: 2 * HB]
    padded_ref[1, : 2 * HB] = blocks_ref[blocks - 2 * HB :]
    padded_ref[1, 2 * HB :] = after
    image_ref[HB : blocks - HB] = inner_ref[...]
    for side in range(2):
        first = lax.axis_index("space") * blocks - HB + side * (blocks - HB)
        for place in range(HB):
            b = side * (blocks - HB) + place
            value = 3.0 * blocks_ref[b].astype(F32) + coupled(
                edges_ref.at[side], place, slots,
                lambda slot: padded_ref[side, index_ref[b, slot] - first],
            )
            image_ref[b] = value.astype(BF16)
    image = image_ref[...].reshape(image_t_ref.shape[1], image_t_ref.shape[0])
    image_t = image.T
    image_t_ref[...] = image_t
    gram_ref[...] = dot_nn(image_t, image)


def interior_of(neighbours, energy, blocks, sketch):
    count, slots, rows, _ = energy.shape
    width = blocks.shape[2]
    levels = sketch.shape[0]
    inner = count - 2 * HB
    return pl.pallas_call(
        interior_kernel,
        out_shape=[
            jax.ShapeDtypeStruct((inner, rows, width), BF16),
            jax.ShapeDtypeStruct((levels, 2, width, width), F32),
            jax.ShapeDtypeStruct((2, HB, slots, rows, rows), BF16),
            jax.ShapeDtypeStruct(blocks.shape, BF16),
        ],
        in_specs=[pl.BlockSpec(memory_space=pltpu.HBM)] * 4,
        scratch_shapes=[
            pltpu.SMEM(neighbours.shape, jnp.int32),
            pltpu.VMEM((inner, slots, rows, rows), BF16),
            pltpu.VMEM(sketch.shape, F32),
            pltpu.SemaphoreType.DMA((6,)),
        ],
        compiler_params=PARAMS,
    )(*[pltpu.with_memory_space_constraint(item, pltpu.HBM) for item in (neighbours, energy, blocks, sketch)])


def edge_of(neighbours, edges, came_near, blocks, came_wide, inner):
    count, rows, width = blocks.shape
    image, image_t, gram = pl.pallas_call(
        edge_kernel,
        out_shape=[
            jax.ShapeDtypeStruct((count, rows, width), BF16),
            jax.ShapeDtypeStruct((width, count * rows), BF16),
            jax.ShapeDtypeStruct((width, width), F32),
        ],
        in_specs=[pl.BlockSpec(memory_space=pltpu.SMEM)]
        + [pl.BlockSpec(memory_space=pltpu.VMEM)] * 5,
        scratch_shapes=[pltpu.VMEM((2, 3 * HB, rows, width), BF16)],
        compiler_params=PARAMS,
    )(neighbours, edges, came_near, blocks, came_wide, inner)
    return image.reshape(count * rows, width), image_t, gram


def pair_kernel(gram_ref, image_t_ref, other_ref, out_ref):
    width = gram_ref.shape[0]
    out_ref[:width] = gram_ref[...]
    cross = dot_nn(image_t_ref[...], other_ref[...])
    odd = lax.axis_index("tm") % 2 == 1
    out_ref[width:] = jnp.where(odd, cross.T[width // 2 :], cross[: width // 2])


def leaf_kernel(total_rows, count, *refs):
    parts, (snapshots_ref, factor_ref, modes_ref) = refs[:count], refs[count:]
    width = snapshots_ref.shape[1]
    grams = total_of(parts) / total_rows
    factor_ref[width:] = grams[width:]
    inverse = inverse_factor(grams[:width])
    factor_ref[:width] = inverse
    modes_ref[...] = dot_nt(snapshots_ref[...], inverse.astype(BF16)).astype(BF16)


def merge(cross_t, sketch_ref):
    sketch_own, sketch_other = sketch_ref[0], sketch_ref[1]
    columns_own = sketch_own + nn_full(sketch_other, cross_t)
    columns_other = nt_full(sketch_own, cross_t) + sketch_other
    image_own = columns_own + nn_full(columns_other, cross_t)
    image_other = nt_full(columns_own, cross_t) + columns_other
    inner = nt_full(
        jnp.concatenate([columns_own, columns_other], axis=1),
        jnp.concatenate([image_own, image_other], axis=1),
    )
    inverse = inverse_factor(inner)
    return nn_full(inverse, columns_own), nn_full(inverse, columns_other)


def combined(own, other, half_own, half_other):
    joined = jnp.concatenate([own, other], axis=1)
    halves = jnp.concatenate([half_own.astype(BF16), half_other.astype(BF16)], axis=1)
    return dot_nt(joined, halves).astype(BF16)


def choose(axis, first, second):
    odd = (lax.axis_index(axis) & 1) == 1
    return jnp.where(odd, second, first), jnp.where(odd, first, second)


def write_bulk(refs, modes, image):
    modes_ref, *image_ref, outgoing_ref = refs
    modes_ref[...] = modes
    if image_ref:
        image_ref[0][...] = image
        outgoing_ref[...] = choose("tm", modes, image)[0]
    else:
        part = outgoing_ref.shape[0]
        outgoing_ref[...] = choose("tm", modes[:part], modes[part:])[0]


def read_modes(came_ref, shared_ref, rows):
    first, second = choose("tm", came_ref[...], shared_ref[...])
    if first.shape[0] == rows:
        return first
    return jnp.concatenate([first, second], axis=0)


def first_merge_kernel(
    own_ref, other_ref, sketch_ref, modes_own, modes_other,
    image_own, image_other, far_image_t, mine_ref, probe_ref, *bulk_refs,
):
    width = own_ref.shape[1]
    own, other = own_ref[:width], other_ref[:width]
    even, odd = choose("tm", own, other)
    pair_gram = jnp.concatenate(choose("tm", own_ref[width:], other_ref[width:]), axis=0)
    cross = nt_full(nn_full(even, pair_gram), odd)
    cross_t = jnp.where(lax.axis_index("tm") % 2 == 1, cross, cross.T)
    half_own, half_other = merge(cross_t, sketch_ref)
    mine = nn_full(half_own, own)
    theirs = nn_full(half_other, other)
    mine_ref[...] = mine
    image = combined(image_own[...], image_other[...], mine, theirs)
    probe_ref[...] = dot_nn(far_image_t[...], image)
    modes = combined(modes_own[...], modes_other[...], half_own, half_other)
    write_bulk(bulk_refs, modes, image)


def merge_kernel(count, *refs):
    parts, (sketch_ref, old_ref, halves_ref, mine_ref) = refs[:count], refs[count:]
    half_own, half_other = merge(total_of(parts), sketch_ref)
    halves_ref[0] = half_own.astype(BF16)
    halves_ref[1] = half_other.astype(BF16)
    mine_ref[...] = nn_full(half_own, old_ref[...])


def apply_kernel(
    halves_ref, modes_own, image_own, came_ref, shared_ref, far_image_t, probe_ref, *bulk_refs
):
    modes_other, image_other = choose("tm", came_ref[...], shared_ref[...])
    image = combined(image_own[...], image_other, halves_ref[0], halves_ref[1])
    probe_ref[...] = dot_nn(far_image_t[...], image)
    modes = combined(modes_own[...], modes_other, halves_ref[0], halves_ref[1])
    write_bulk(bulk_refs, modes, image)


def output_kernel(halves_ref, came_ref, shared_ref, *refs):
    *earlier, out_ref = refs
    for level, modes_ref in enumerate(earlier):
        out_ref[level] = modes_ref[...]
    modes_other = read_modes(came_ref, shared_ref, out_ref.shape[1])
    out_ref[len(earlier)] = combined(
        earlier[-1][...], modes_other, halves_ref[0], halves_ref[1]
    )


def cross_kernel(total_rows, count, *refs):
    parts, (far_ref, out_ref) = refs[:count], refs[count:]
    out_ref[...] = nn_full(far_ref[...], total_of(parts) / total_rows)


def modes_of(snapshots, energy, neighbours, sketch):
    block_count, _, block_rows, _ = energy.shape
    rows_dev, width = snapshots.shape
    space = lax.axis_size("space")
    total_rows = rows_dev * space
    levels = sketch.shape[0]
    blocks = snapshots.reshape(block_count, block_rows, width)
    head, tail = blocks[:HB], blocks[block_count - HB :]
    odd = (lax.axis_index("space") & 1) == 1
    near = [(i, i ^ 1) for i in range(space)]
    wide = [(i, (i + 2 * (i % 2) - 1) % space) for i in range(space)]
    came_near = lax.ppermute(jnp.where(odd, head, tail), "space", near)
    came_wide = lax.ppermute(jnp.where(odd, tail, head), "space", wide)
    square = jax.ShapeDtypeStruct((width, width), F32)
    modes_shape = jax.ShapeDtypeStruct((rows_dev, width), BF16)
    half_shape = jax.ShapeDtypeStruct((rows_dev // 2, width), BF16)
    factor_shape = jax.ShapeDtypeStruct((width + width // 2, width), F32)
    halves_shape = jax.ShapeDtypeStruct((2, width, width), BF16)

    inner, sketch_t, edges, blocks = interior_of(neighbours, energy, blocks, sketch)
    image, image_t, gram = edge_of(neighbours, edges, came_near, blocks, came_wide, inner)
    other_image = swap(image, "tm", 1)
    pair = run_kernel(
        pair_kernel,
        factor_shape, gram, image_t, other_image,
    )
    parts = summands(pair, "space", space, 4)
    far_images = [swap(image_t, "tm", 2**level) for level in range(1, levels)]
    factor, modes = run_kernel(
        functools.partial(leaf_kernel, total_rows, len(parts)),
        [factor_shape, modes_shape],
        *parts, blocks.reshape(rows_dev, width),
    )
    other_factor = swap(factor, "tm", 1)
    other = swap(modes, "tm", 1)
    kept = [modes]
    for level in range(levels):
        deep = level + 2 < levels
        outs = [square, square, modes_shape] + ([modes_shape] * 2 if deep else [half_shape])
        if level == 0:
            mine, probe, *bulk = run_kernel(
                first_merge_kernel, outs,
                factor, other_factor, sketch_t[level],
                modes, other, image, other_image, far_images[level],
            )
        else:
            far_mine = swap(mine, "tm", 2**level)
            parts = summands(probe, "space", space, 4)
            came = swap(bulk[-1], "tm", 2**level)
            shared = swap(came, "tm", 1)
            cross = run_kernel(
                functools.partial(cross_kernel, total_rows, len(parts)),
                square, *parts, far_mine,
            )
            parts = summands(cross, "tm", 2**level, 2)
            halves, mine = run_kernel(
                functools.partial(merge_kernel, len(parts)), [halves_shape, square],
                *parts, sketch_t[level], mine,
            )
            if level + 1 < levels:
                probe, *bulk = run_kernel(
                    apply_kernel, outs[1:],
                    halves, *bulk[:2], came, shared, far_images[level],
                )
            else:
                out = run_kernel(
                    output_kernel,
                    jax.ShapeDtypeStruct((levels + 1, rows_dev, width), BF16),
                    halves, came, shared, *kept,
                )
        kept.append(bulk[0])
    return out[:, None]


def solution(mesh):
    placed = (P("space", "tm"), P("space", None, None, None), P("space", None), P())
    return jax.shard_map(
        modes_of,
        mesh=mesh,
        in_specs=placed,
        out_specs=P(None, "tm", "space", None),
        check_vma=False,
    )
```

```python
import functools

import jax
import jax.numpy as jnp
from jax import lax
from jax.experimental import pallas as pl
from jax.experimental.pallas import tpu as pltpu
from jax.sharding import PartitionSpec as P


HB = 2
PANEL = 8
F32 = jnp.float32
BF16 = jnp.bfloat16
PARAMS = pltpu.CompilerParams(vmem_limit_bytes=16 * 1024 * 1024)


def swap(value, axis, mask):
    pairs = [(source, source ^ mask) for source in range(lax.axis_size(axis))]
    return lax.ppermute(value, axis, pairs)


def summands(value, axis, count, widest):
    done = 1
    parts = [value]
    while done < count:
        if len(parts) > 1:
            value = run_kernel(add_kernel, jax.ShapeDtypeStruct(value.shape, F32), *parts)
        radix = 4 if widest == 4 and count // done % 4 == 0 else 2
        parts = [value]
        for step in range(1, radix):
            parts.append(swap(value, axis, step * done))
        done *= radix
    return parts


def add_kernel(*refs):
    refs[-1][...] = total_of(refs[:-1])


def total_of(parts):
    values = [part[...] for part in parts]
    while len(values) > 1:
        values = [a + b for a, b in zip(values[::2], values[1::2])]
    return values[0]


def dot_nn(a, b):
    return lax.dot_general(a, b, (((1,), (0,)), ((), ())), preferred_element_type=F32)


def dot_nt(a, b):
    return lax.dot_general(a, b, (((1,), (1,)), ((), ())), preferred_element_type=F32)


def split(value):
    high = value.astype(BF16)
    return high, (value - high.astype(F32)).astype(BF16)


def full(dot, axis, a, b):
    a_high, a_low = split(a)
    b_high, b_low = split(b)
    left = jnp.concatenate([a_high, a_high, a_low], axis=1)
    return dot(left, jnp.concatenate([b_high, b_low, b_high], axis=axis))


nn_full = functools.partial(full, dot_nn, 0)
nt_full = functools.partial(full, dot_nt, 1)


def inverse_factor(matrix):
    size = matrix.shape[0]
    panels = size // PANEL
    shape = (PANEL, size)
    lane = lax.broadcasted_iota(jnp.int32, shape, 1)
    sub = lax.broadcasted_iota(jnp.int32, shape, 0)

    def column(rows, index):
        return jnp.broadcast_to(rows[:, index : index + 1], shape)

    def row(rows, index):
        return jnp.broadcast_to(rows[index : index + 1, :], shape)

    rows_of = [matrix[PANEL * i : PANEL * (i + 1), :] for i in range(panels)]
    out = []
    block = [column(rows_of[0], j) for j in range(PANEL)]
    for k in range(panels):
        base = PANEL * k
        active = rows_of[k]
        ahead = (
            [column(active, base + PANEL + j) for j in range(PANEL)] if k + 1 < panels else []
        )
        here = (lane >= base) & (lane < base + PANEL)
        active = jnp.where(here, jnp.where(lane == sub + base, 1.0, 0.0), active)
        kept = active
        pivots = block[0]
        for j in range(PANEL):
            pivot = row(block[j], j)
            factor = jnp.where(sub == j, 0.0, block[j]) * (1.0 / pivot)
            kept = jnp.where(sub == j, active, kept)
            pivots = jnp.where(sub == j, pivot, pivots)
            active = active - factor * row(active, j)
            for q in range(j + 1, PANEL):
                block[q] = block[q] - factor * row(block[q], j)
            ahead = [item - factor * row(item, j) for item in ahead]
        out.append(jnp.where(lane < base + PANEL, kept * lax.rsqrt(pivots), 0.0))
        if k + 1 == panels:
            break
        scale = 1.0 / pivots
        solved = active * scale
        solved_rows = [row(solved, j) for j in range(PANEL)]
        block = []
        for i in range(k + 1, panels):
            old = rows_of[i]
            columns = [column(old, base + j) for j in range(PANEL)]
            if i == k + 1:
                for q in range(PANEL):
                    item = column(old, base + PANEL + q)
                    scaled = ahead[q] * scale
                    for j in range(PANEL):
                        item = item - columns[j] * row(scaled, j)
                    block.append(item)
            new = jnp.where(here, 0.0, old)
            for j in range(PANEL):
                new = new - columns[j] * solved_rows[j]
            rows_of[i] = new
    return jnp.concatenate(out, axis=0)


def run_kernel(body, outs, *operands):
    cost = pl.CostEstimate(flops=2_000_000_000, bytes_accessed=1_000_000, transcendentals=0)
    return pl.pallas_call(
        body, out_shape=outs, cost_estimate=cost, compiler_params=PARAMS
    )(*operands)


def coupled(energy_ref, place, slots, lookup):
    left = jnp.concatenate([energy_ref[place, slot] for slot in range(slots)], axis=1)
    right = jnp.concatenate([lookup(slot) for slot in range(slots)], axis=0)
    return dot_nn(left, right)


def interior_kernel(
    index_hbm, energy_hbm, blocks_hbm, sketch_hbm,
    image_ref, sketch_out, edges_ref, blocks_ref, index_ref, energy_ref, sketch_ref, sems,
):
    count = blocks_ref.shape[0]
    inner, slots = energy_ref.shape[:2]
    width = sketch_out.shape[2]
    copies = [
        pltpu.make_async_copy(source, target, sems.at[place])
        for place, (source, target) in enumerate(
            [
                (index_hbm, index_ref),
                (blocks_hbm, blocks_ref),
                (energy_hbm.at[pl.ds(HB, inner)], energy_ref),
                (sketch_hbm, sketch_ref),
                (energy_hbm.at[pl.ds(0, HB)], edges_ref.at[0]),
                (energy_hbm.at[pl.ds(count - HB, HB)], edges_ref.at[1]),
            ]
        )
    ]
    for copy in copies:
        copy.start()
    first = lax.axis_index("space") * count
    window = lax.axis_index("tm")
    for copy in copies[:3]:
        copy.wait()
    for place in range(inner):
        b = HB + place
        value = 3.0 * blocks_ref[b].astype(F32) + coupled(
            energy_ref, place, slots, lambda slot: blocks_ref[index_ref[b, slot] - first]
        )
        image_ref[place] = value.astype(BF16)
    copies[3].wait()
    for level in range(sketch_ref.shape[0]):
        upper = window // 2**level % 2
        for half in range(2):
            start = pl.multiple_of((upper ^ half) * width, width)
            sketch_out[level, half] = sketch_ref[level, pl.ds(start, width), :].T
    for copy in copies[4:]:
        copy.wait()


def edge_kernel(
    index_ref, edges_ref, near_ref, blocks_ref, wide_ref, inner_ref,
    image_ref, image_t_ref, gram_ref, padded_ref,
):
    slots = edges_ref.shape[2]
    blocks = blocks_ref.shape[0]
    before, after = choose("space", wide_ref[...], near_ref[...])
    padded_ref[0, :HB] = before
    padded_ref[0, HB:] = blocks_ref[: 2 * HB]
    padded_ref[1, : 2 * HB] = blocks_ref[blocks - 2 * HB :]
    padded_ref[1, 2 * HB :] = after
    image_ref[HB : blocks - HB] = inner_ref[...]
    for side in range(2):
        first = lax.axis_index("space") * blocks - HB + side * (blocks - HB)
        for place in range(HB):
            b = side * (blocks - HB) + place
            value = 3.0 * blocks_ref[b].astype(F32) + coupled(
                edges_ref.at[side], place, slots,
                lambda slot: padded_ref[side, index_ref[b, slot] - first],
            )
            image_ref[b] = value.astype(BF16)
    image = image_ref[...].reshape(image_t_ref.shape[1], image_t_ref.shape[0])
    image_t = image.T
    image_t_ref[...] = image_t
    gram_ref[...] = dot_nn(image_t, image)


def interior_of(neighbours, energy, blocks, sketch):
    count, slots, rows, _ = energy.shape
    width = blocks.shape[2]
    levels = sketch.shape[0]
    inner = count - 2 * HB
    return pl.pallas_call(
        interior_kernel,
        out_shape=[
            jax.ShapeDtypeStruct((inner, rows, width), BF16),
            jax.ShapeDtypeStruct((levels, 2, width, width), F32),
            jax.ShapeDtypeStruct((2, HB, slots, rows, rows), BF16),
            jax.ShapeDtypeStruct(blocks.shape, BF16),
        ],
        in_specs=[pl.BlockSpec(memory_space=pltpu.HBM)] * 4,
        scratch_shapes=[
            pltpu.SMEM(neighbours.shape, jnp.int32),
            pltpu.VMEM((inner, slots, rows, rows), BF16),
            pltpu.VMEM(sketch.shape, F32),
            pltpu.SemaphoreType.DMA((6,)),
        ],
        compiler_params=PARAMS,
    )(*[pltpu.with_memory_space_constraint(item, pltpu.HBM) for item in (neighbours, energy, blocks, sketch)])


def edge_of(neighbours, edges, came_near, blocks, came_wide, inner):
    count, rows, width = blocks.shape
    image, image_t, gram = pl.pallas_call(
        edge_kernel,
        out_shape=[
            jax.ShapeDtypeStruct((count, rows, width), BF16),
            jax.ShapeDtypeStruct((width, count * rows), BF16),
            jax.ShapeDtypeStruct((width, width), F32),
        ],
        in_specs=[pl.BlockSpec(memory_space=pltpu.SMEM)]
        + [pl.BlockSpec(memory_space=pltpu.VMEM)] * 5,
        scratch_shapes=[pltpu.VMEM((2, 3 * HB, rows, width), BF16)],
        compiler_params=PARAMS,
    )(neighbours, edges, came_near, blocks, came_wide, inner)
    return image.reshape(count * rows, width), image_t, gram


def pair_kernel(gram_ref, image_t_ref, other_ref, out_ref):
    width = gram_ref.shape[0]
    out_ref[:width] = gram_ref[...]
    cross = dot_nn(image_t_ref[...], other_ref[...])
    odd = lax.axis_index("tm") % 2 == 1
    out_ref[width:] = jnp.where(odd, cross.T[width // 2 :], cross[: width // 2])


def leaf_kernel(total_rows, count, *refs):
    parts, (snapshots_ref, factor_ref, modes_ref) = refs[:count], refs[count:]
    width = snapshots_ref.shape[1]
    grams = total_of(parts) / total_rows
    factor_ref[width:] = grams[width:]
    inverse = inverse_factor(grams[:width])
    factor_ref[:width] = inverse
    modes_ref[...] = dot_nt(snapshots_ref[...], inverse.astype(BF16)).astype(BF16)


def merge(cross_t, sketch_ref):
    sketch_own, sketch_other = sketch_ref[0], sketch_ref[1]
    columns_own = sketch_own + nn_full(sketch_other, cross_t)
    columns_other = nt_full(sketch_own, cross_t) + sketch_other
    image_own = columns_own + nn_full(columns_other, cross_t)
    image_other = nt_full(columns_own, cross_t) + columns_other
    inner = nt_full(
        jnp.concatenate([columns_own, columns_other], axis=1),
        jnp.concatenate([image_own, image_other], axis=1),
    )
    inverse = inverse_factor(inner)
    return nn_full(inverse, columns_own), nn_full(inverse, columns_other)


def combined(own, other, half_own, half_other):
    joined = jnp.concatenate([own, other], axis=1)
    halves = jnp.concatenate([half_own.astype(BF16), half_other.astype(BF16)], axis=1)
    return dot_nt(joined, halves).astype(BF16)


def choose(axis, first, second):
    odd = (lax.axis_index(axis) & 1) == 1
    return jnp.where(odd, second, first), jnp.where(odd, first, second)


def write_bulk(refs, modes, image):
    modes_ref, *image_ref, outgoing_ref = refs
    modes_ref[...] = modes
    if image_ref:
        image_ref[0][...] = image
        outgoing_ref[...] = choose("tm", modes, image)[0]
    else:
        part = outgoing_ref.shape[0]
        outgoing_ref[...] = choose("tm", modes[:part], modes[part:])[0]


def read_modes(came_ref, shared_ref, rows):
    first, second = choose("tm", came_ref[...], shared_ref[...])
    if first.shape[0] == rows:
        return first
    return jnp.concatenate([first, second], axis=0)


def first_merge_kernel(own_ref, other_ref, sketch_ref, halves_ref, mine_ref, slices_ref):
    width = own_ref.shape[1]
    own, other = own_ref[:width], other_ref[:width]
    even, odd = choose("tm", own, other)
    pair_gram = jnp.concatenate(choose("tm", own_ref[width:], other_ref[width:]), axis=0)
    cross = nt_full(nn_full(even, pair_gram), odd)
    cross_t = jnp.where(lax.axis_index("tm") % 2 == 1, cross, cross.T)
    half_own, half_other = merge(cross_t, sketch_ref)
    halves_ref[0] = half_own.astype(BF16)
    halves_ref[1] = half_other.astype(BF16)
    mine = nn_full(half_own, own)
    mine_ref[...] = mine
    slices_ref[0] = mine.astype(BF16)
    slices_ref[1] = nn_full(half_other, other).astype(BF16)


def first_apply_kernel(
    halves_ref, slices_ref, modes_own, modes_other, image_own, image_other, far_image_t,
    probe_ref, *bulk_refs,
):
    image = combined(image_own[...], image_other[...], slices_ref[0], slices_ref[1])
    probe_ref[...] = dot_nn(far_image_t[...], image)
    modes = combined(modes_own[...], modes_other[...], halves_ref[0], halves_ref[1])
    write_bulk(bulk_refs, modes, image)


def merge_kernel(count, *refs):
    parts, (sketch_ref, old_ref, halves_ref, mine_ref) = refs[:count], refs[count:]
    half_own, half_other = merge(total_of(parts), sketch_ref)
    halves_ref[0] = half_own.astype(BF16)
    halves_ref[1] = half_other.astype(BF16)
    mine_ref[...] = nn_full(half_own, old_ref[...])


def last_merge_kernel(count, *refs):
    parts, (sketch_ref, *kept, halves_ref, out_ref, sems) = refs[:count], refs[count:]
    copies = [
        pltpu.make_async_copy(modes_ref, out_ref.at[level], sems.at[level])
        for level, modes_ref in enumerate(kept)
    ]
    for copy in copies:
        copy.start()
    half_own, half_other = merge(total_of(parts), sketch_ref)
    halves_ref[0] = half_own.astype(BF16)
    halves_ref[1] = half_other.astype(BF16)
    for copy in copies:
        copy.wait()


def apply_kernel(
    halves_ref, modes_own, image_own, came_ref, shared_ref, far_image_t, probe_ref, *bulk_refs
):
    modes_other, image_other = choose("tm", came_ref[...], shared_ref[...])
    image = combined(image_own[...], image_other, halves_ref[0], halves_ref[1])
    probe_ref[...] = dot_nn(far_image_t[...], image)
    modes = combined(modes_own[...], modes_other, halves_ref[0], halves_ref[1])
    write_bulk(bulk_refs, modes, image)


def output_kernel(halves_ref, modes_own, came_ref, shared_ref, _, out_ref, modes_ref, sems):
    rows = modes_own.shape[0]
    modes_other = read_modes(came_ref, shared_ref, rows)
    part = rows // 2
    copies = []
    for half in range(2):
        span = slice(half * part, (half + 1) * part)
        modes_ref[span] = combined(
            modes_own[span], modes_other[span], halves_ref[0], halves_ref[1]
        )
        copies.append(
            pltpu.make_async_copy(
                modes_ref.at[pl.ds(half * part, part)],
                out_ref.at[out_ref.shape[0] - 1, pl.ds(half * part, part)],
                sems.at[half],
            )
        )
        copies[-1].start()
    for copy in copies:
        copy.wait()


def last_level(parts, sketch_t, kept, halves_shape):
    rows, width = kept[0].shape
    levels = len(kept)
    vmem = pl.BlockSpec(memory_space=pltpu.VMEM)
    hbm = pl.BlockSpec(memory_space=pltpu.HBM)
    return pl.pallas_call(
        functools.partial(last_merge_kernel, len(parts)),
        out_shape=[halves_shape, jax.ShapeDtypeStruct((levels + 1, rows, width), BF16)],
        in_specs=[vmem] * (len(parts) + 1 + levels),
        out_specs=[vmem, hbm],
        scratch_shapes=[pltpu.SemaphoreType.DMA((levels,))],
        compiler_params=PARAMS,
    )(*parts, sketch_t, *kept)


def last_modes(halves, modes, came, shared, out):
    vmem = pl.BlockSpec(memory_space=pltpu.VMEM)
    hbm = pl.BlockSpec(memory_space=pltpu.HBM)
    return pl.pallas_call(
        output_kernel,
        out_shape=jax.ShapeDtypeStruct(out.shape, BF16),
        in_specs=[vmem] * 4 + [hbm],
        out_specs=hbm,
        scratch_shapes=[pltpu.VMEM(modes.shape, BF16), pltpu.SemaphoreType.DMA((2,))],
        input_output_aliases={4: 0},
        compiler_params=PARAMS,
    )(halves, modes, came, shared, out)


def cross_kernel(total_rows, count, *refs):
    parts, (far_ref, out_ref) = refs[:count], refs[count:]
    out_ref[...] = nn_full(far_ref[...], total_of(parts) / total_rows)


def modes_of(snapshots, energy, neighbours, sketch):
    block_count, _, block_rows, _ = energy.shape
    rows_dev, width = snapshots.shape
    space = lax.axis_size("space")
    total_rows = rows_dev * space
    levels = sketch.shape[0]
    blocks = snapshots.reshape(block_count, block_rows, width)
    head, tail = blocks[:HB], blocks[block_count - HB :]
    odd = (lax.axis_index("space") & 1) == 1
    near = [(i, i ^ 1) for i in range(space)]
    wide = [(i, (i + 2 * (i % 2) - 1) % space) for i in range(space)]
    came_near = lax.ppermute(jnp.where(odd, head, tail), "space", near)
    came_wide = lax.ppermute(jnp.where(odd, tail, head), "space", wide)
    square = jax.ShapeDtypeStruct((width, width), F32)
    modes_shape = jax.ShapeDtypeStruct((rows_dev, width), BF16)
    half_shape = jax.ShapeDtypeStruct((rows_dev // 2, width), BF16)
    factor_shape = jax.ShapeDtypeStruct((width + width // 2, width), F32)
    halves_shape = jax.ShapeDtypeStruct((2, width, width), BF16)

    inner, sketch_t, edges, blocks = interior_of(neighbours, energy, blocks, sketch)
    image, image_t, gram = edge_of(neighbours, edges, came_near, blocks, came_wide, inner)
    other_image = swap(image, "tm", 1)
    pair = run_kernel(
        pair_kernel,
        factor_shape, gram, image_t, other_image,
    )
    parts = summands(pair, "space", space, 4)
    far_images = [swap(image_t, "tm", 2**level) for level in range(1, levels)]
    factor, modes = run_kernel(
        functools.partial(leaf_kernel, total_rows, len(parts)),
        [factor_shape, modes_shape],
        *parts, blocks.reshape(rows_dev, width),
    )
    other_factor = swap(factor, "tm", 1)
    other = swap(modes, "tm", 1)
    kept = [modes]
    for level in range(levels):
        deep = level + 2 < levels
        outs = [square, square, modes_shape] + ([modes_shape] * 2 if deep else [half_shape])
        if level == 0:
            halves, mine, slices = run_kernel(
                first_merge_kernel, [halves_shape, square, halves_shape],
                factor, other_factor, sketch_t[level],
            )
            probe, *bulk = run_kernel(
                first_apply_kernel, outs[1:],
                halves, slices, modes, other, image, other_image, far_images[level],
            )
        else:
            far_mine = swap(mine, "tm", 2**level)
            parts = summands(probe, "space", space, 4)
            came = swap(bulk[-1], "tm", 2**level)
            shared = swap(came, "tm", 1)
            cross = run_kernel(
                functools.partial(cross_kernel, total_rows, len(parts)),
                square, *parts, far_mine,
            )
            parts = summands(cross, "tm", 2**level, 2)
            if level + 1 < levels:
                halves, mine = run_kernel(
                    functools.partial(merge_kernel, len(parts)), [halves_shape, square],
                    *parts, sketch_t[level], mine,
                )
                probe, *bulk = run_kernel(
                    apply_kernel, outs[1:],
                    halves, *bulk[:2], came, shared, far_images[level],
                )
            else:
                halves, out = last_level(parts, sketch_t[level], kept, halves_shape)
                out = last_modes(halves, bulk[0], came, shared, out)
        kept.append(bulk[0])
    return out[:, None]


def solution(mesh):
    placed = (P("space", "tm"), P("space", None, None, None), P("space", None), P())
    return jax.shard_map(
        modes_of,
        mesh=mesh,
        in_specs=placed,
        out_specs=P(None, "tm", "space", None),
        check_vma=False,
    )
```

```python
import functools

import jax
import jax.numpy as jnp
from jax import lax
from jax.experimental import pallas as pl
from jax.experimental.pallas import tpu as pltpu
from jax.sharding import PartitionSpec as P


HB = 2
PANEL = 8
F32 = jnp.float32
BF16 = jnp.bfloat16
PARAMS = pltpu.CompilerParams(vmem_limit_bytes=16 * 1024 * 1024)


def swap(value, axis, mask):
    pairs = [(source, source ^ mask) for source in range(lax.axis_size(axis))]
    return lax.ppermute(value, axis, pairs)


def summands(value, axis, count, widest):
    done = 1
    parts = [value]
    while done < count:
        if len(parts) > 1:
            value = run_kernel(add_kernel, jax.ShapeDtypeStruct(value.shape, value.dtype), *parts)
        radix = 4 if widest == 4 and count // done % 4 == 0 else 2
        parts = [value]
        for step in range(1, radix):
            parts.append(swap(value, axis, step * done))
        done *= radix
    return parts


def add_kernel(*refs):
    refs[-1][...] = total_of(refs[:-1]).astype(refs[-1].dtype)


def total_of(parts):
    values = [part[...].astype(F32) for part in parts]
    while len(values) > 1:
        values = [a + b for a, b in zip(values[::2], values[1::2])]
    return values[0]


def dot_nn(a, b):
    return lax.dot_general(a, b, (((1,), (0,)), ((), ())), preferred_element_type=F32)


def dot_nt(a, b):
    return lax.dot_general(a, b, (((1,), (1,)), ((), ())), preferred_element_type=F32)


def split(value):
    high = value.astype(BF16)
    return high, (value - high.astype(F32)).astype(BF16)


def full(dot, axis, a, b):
    a_high, a_low = split(a)
    b_high, b_low = split(b)
    left = jnp.concatenate([a_high, a_high, a_low], axis=1)
    return dot(left, jnp.concatenate([b_high, b_low, b_high], axis=axis))


nn_full = functools.partial(full, dot_nn, 0)
nt_full = functools.partial(full, dot_nt, 1)


def inverse_factor(matrix):
    size = matrix.shape[0]
    panels = size // PANEL
    shape = (PANEL, size)
    lane = lax.broadcasted_iota(jnp.int32, shape, 1)
    sub = lax.broadcasted_iota(jnp.int32, shape, 0)

    def column(rows, index):
        return jnp.broadcast_to(rows[:, index : index + 1], shape)

    def row(rows, index):
        return jnp.broadcast_to(rows[index : index + 1, :], shape)

    rows_of = [matrix[PANEL * i : PANEL * (i + 1), :] for i in range(panels)]
    out = []
    block = [column(rows_of[0], j) for j in range(PANEL)]
    for k in range(panels):
        base = PANEL * k
        active = rows_of[k]
        ahead = (
            [column(active, base + PANEL + j) for j in range(PANEL)] if k + 1 < panels else []
        )
        here = (lane >= base) & (lane < base + PANEL)
        active = jnp.where(here, jnp.where(lane == sub + base, 1.0, 0.0), active)
        kept = active
        pivots = block[0]
        for j in range(PANEL):
            pivot = row(block[j], j)
            factor = jnp.where(sub == j, 0.0, block[j]) * (1.0 / pivot)
            kept = jnp.where(sub == j, active, kept)
            pivots = jnp.where(sub == j, pivot, pivots)
            active = active - factor * row(active, j)
            for q in range(j + 1, PANEL):
                block[q] = block[q] - factor * row(block[q], j)
            ahead = [item - factor * row(item, j) for item in ahead]
        out.append(jnp.where(lane < base + PANEL, kept * lax.rsqrt(pivots), 0.0))
        if k + 1 == panels:
            break
        scale = 1.0 / pivots
        solved = active * scale
        solved_rows = [row(solved, j) for j in range(PANEL)]
        block = []
        for i in range(k + 1, panels):
            old = rows_of[i]
            columns = [column(old, base + j) for j in range(PANEL)]
            if i == k + 1:
                for q in range(PANEL):
                    item = column(old, base + PANEL + q)
                    scaled = ahead[q] * scale
                    for j in range(PANEL):
                        item = item - columns[j] * row(scaled, j)
                    block.append(item)
            new = jnp.where(here, 0.0, old)
            for j in range(PANEL):
                new = new - columns[j] * solved_rows[j]
            rows_of[i] = new
    return jnp.concatenate(out, axis=0)


def run_kernel(body, outs, *operands):
    cost = pl.CostEstimate(flops=2_000_000_000, bytes_accessed=1_000_000, transcendentals=0)
    return pl.pallas_call(
        body, out_shape=outs, cost_estimate=cost, compiler_params=PARAMS
    )(*operands)


def coupled(energy_ref, place, slots, lookup):
    left = jnp.concatenate([energy_ref[place, slot] for slot in range(slots)], axis=1)
    right = jnp.concatenate([lookup(slot) for slot in range(slots)], axis=0)
    return dot_nn(left, right)


def interior_kernel(
    index_hbm, energy_hbm, blocks_hbm, sketch_hbm,
    image_ref, sketch_out, edges_ref, blocks_ref, index_ref, energy_ref, sketch_ref, sems,
):
    count = blocks_ref.shape[0]
    inner, slots = energy_ref.shape[:2]
    width = sketch_out.shape[2]
    copies = [
        pltpu.make_async_copy(source, target, sems.at[place])
        for place, (source, target) in enumerate(
            [
                (index_hbm, index_ref),
                (blocks_hbm, blocks_ref),
                (energy_hbm.at[pl.ds(HB, inner)], energy_ref),
                (sketch_hbm, sketch_ref),
                (energy_hbm.at[pl.ds(0, HB)], edges_ref.at[0]),
                (energy_hbm.at[pl.ds(count - HB, HB)], edges_ref.at[1]),
            ]
        )
    ]
    for copy in copies:
        copy.start()
    first = lax.axis_index("space") * count
    window = lax.axis_index("tm")
    for copy in copies[:3]:
        copy.wait()
    for place in range(inner):
        b = HB + place
        value = 3.0 * blocks_ref[b].astype(F32) + coupled(
            energy_ref, place, slots, lambda slot: blocks_ref[index_ref[b, slot] - first]
        )
        image_ref[place] = value.astype(BF16)
    copies[3].wait()
    for level in range(sketch_ref.shape[0]):
        upper = window // 2**level % 2
        for half in range(2):
            start = pl.multiple_of((upper ^ half) * width, width)
            sketch_out[level, half] = sketch_ref[level, pl.ds(start, width), :].T
    for copy in copies[4:]:
        copy.wait()


def edge_kernel(
    index_ref, edges_ref, near_ref, blocks_ref, wide_ref, inner_ref,
    image_ref, image_t_ref, gram_ref, padded_ref,
):
    slots = edges_ref.shape[2]
    blocks = blocks_ref.shape[0]
    before, after = choose("space", wide_ref[...], near_ref[...])
    padded_ref[0, :HB] = before
    padded_ref[0, HB:] = blocks_ref[: 2 * HB]
    padded_ref[1, : 2 * HB] = blocks_ref[blocks - 2 * HB :]
    padded_ref[1, 2 * HB :] = after
    image_ref[HB : blocks - HB] = inner_ref[...]
    for side in range(2):
        first = lax.axis_index("space") * blocks - HB + side * (blocks - HB)
        for place in range(HB):
            b = side * (blocks - HB) + place
            value = 3.0 * blocks_ref[b].astype(F32) + coupled(
                edges_ref.at[side], place, slots,
                lambda slot: padded_ref[side, index_ref[b, slot] - first],
            )
            image_ref[b] = value.astype(BF16)
    image = image_ref[...].reshape(image_t_ref.shape[1], image_t_ref.shape[0])
    image_t = image.T
    image_t_ref[...] = image_t
    gram_ref[...] = dot_nn(image_t, image)


def interior_of(neighbours, energy, blocks, sketch):
    count, slots, rows, _ = energy.shape
    width = blocks.shape[2]
    levels = sketch.shape[0]
    inner = count - 2 * HB
    return pl.pallas_call(
        interior_kernel,
        out_shape=[
            jax.ShapeDtypeStruct((inner, rows, width), BF16),
            jax.ShapeDtypeStruct((levels, 2, width, width), F32),
            jax.ShapeDtypeStruct((2, HB, slots, rows, rows), BF16),
            jax.ShapeDtypeStruct(blocks.shape, BF16),
        ],
        in_specs=[pl.BlockSpec(memory_space=pltpu.HBM)] * 4,
        scratch_shapes=[
            pltpu.SMEM(neighbours.shape, jnp.int32),
            pltpu.VMEM((inner, slots, rows, rows), BF16),
            pltpu.VMEM(sketch.shape, F32),
            pltpu.SemaphoreType.DMA((6,)),
        ],
        compiler_params=PARAMS,
    )(*[pltpu.with_memory_space_constraint(item, pltpu.HBM) for item in (neighbours, energy, blocks, sketch)])


def edge_of(neighbours, edges, came_near, blocks, came_wide, inner):
    count, rows, width = blocks.shape
    image, image_t, gram = pl.pallas_call(
        edge_kernel,
        out_shape=[
            jax.ShapeDtypeStruct((count, rows, width), BF16),
            jax.ShapeDtypeStruct((width, count * rows), BF16),
            jax.ShapeDtypeStruct((width, width), F32),
        ],
        in_specs=[pl.BlockSpec(memory_space=pltpu.SMEM)]
        + [pl.BlockSpec(memory_space=pltpu.VMEM)] * 5,
        scratch_shapes=[pltpu.VMEM((2, 3 * HB, rows, width), BF16)],
        compiler_params=PARAMS,
    )(neighbours, edges, came_near, blocks, came_wide, inner)
    return image.reshape(count * rows, width), image_t, gram


def pair_kernel(gram_ref, image_t_ref, other_ref, out_ref):
    width = gram_ref.shape[0]
    out_ref[:width] = gram_ref[...]
    cross = dot_nn(image_t_ref[...], other_ref[...])
    odd = lax.axis_index("tm") % 2 == 1
    out_ref[width:] = jnp.where(odd, cross.T[width // 2 :], cross[: width // 2])


def leaf_kernel(total_rows, count, *refs):
    parts, (factor_ref,) = refs[:count], refs[count:]
    width = factor_ref.shape[1]
    grams = total_of(parts) / total_rows
    factor_ref[width:] = grams[width:]
    inverse = inverse_factor(grams[:width])
    factor_ref[:width] = inverse


def leaf_modes_kernel(snapshots_ref, factor_ref, modes_ref):
    inverse = factor_ref[: factor_ref.shape[1]]
    modes_ref[...] = dot_nt(snapshots_ref[...], inverse.astype(BF16)).astype(BF16)


def merge(cross_t, sketch_ref):
    sketch_own, sketch_other = sketch_ref[0], sketch_ref[1]
    columns_own = sketch_own + nn_full(sketch_other, cross_t)
    columns_other = nt_full(sketch_own, cross_t) + sketch_other
    image_own = columns_own + nn_full(columns_other, cross_t)
    image_other = nt_full(columns_own, cross_t) + columns_other
    inner = nt_full(
        jnp.concatenate([columns_own, columns_other], axis=1),
        jnp.concatenate([image_own, image_other], axis=1),
    )
    inverse = inverse_factor(inner)
    return nn_full(inverse, columns_own), nn_full(inverse, columns_other)


def combined(own, other, half_own, half_other):
    joined = jnp.concatenate([own, other], axis=1)
    halves = jnp.concatenate([half_own.astype(BF16), half_other.astype(BF16)], axis=1)
    return dot_nt(joined, halves).astype(BF16)


def choose(axis, first, second):
    odd = (lax.axis_index(axis) & 1) == 1
    return jnp.where(odd, second, first), jnp.where(odd, first, second)


def write_bulk(refs, modes, image_ref):
    modes_ref, outgoing_ref = refs
    modes_ref[...] = modes
    if image_ref is not None:
        outgoing_ref[...] = choose("tm", modes, image_ref[...])[0]
    else:
        part = outgoing_ref.shape[0]
        outgoing_ref[...] = choose("tm", modes[:part], modes[part:])[0]


def read_modes(came_ref, shared_ref, rows):
    first, second = choose("tm", came_ref[...], shared_ref[...])
    if first.shape[0] == rows:
        return first
    return jnp.concatenate([first, second], axis=0)


def first_merge_kernel(own_ref, other_ref, sketch_ref, halves_ref, mine_ref, slices_ref):
    width = own_ref.shape[1]
    own, other = own_ref[:width], other_ref[:width]
    even, odd = choose("tm", own, other)
    pair_gram = jnp.concatenate(choose("tm", own_ref[width:], other_ref[width:]), axis=0)
    cross = nt_full(nn_full(even, pair_gram), odd)
    cross_t = jnp.where(lax.axis_index("tm") % 2 == 1, cross, cross.T)
    half_own, half_other = merge(cross_t, sketch_ref)
    halves_ref[0] = half_own.astype(BF16)
    halves_ref[1] = half_other.astype(BF16)
    mine = nn_full(half_own, own)
    mine_ref[...] = mine
    slices_ref[0] = mine.astype(BF16)
    slices_ref[1] = nn_full(half_other, other).astype(BF16)


def write_probe(refs, far_image_t, image):
    refs[0][...] = dot_nn(far_image_t[...], image).astype(BF16)
    if len(refs) > 1:
        refs[1][...] = image


def first_apply_kernel(slices_ref, image_own, image_other, far_image_t, *refs):
    image = combined(image_own[...], image_other[...], slices_ref[0], slices_ref[1])
    write_probe(refs, far_image_t, image)


def first_modes_kernel(halves_ref, modes_own, modes_other, *refs):
    *image_ref, modes_ref, outgoing_ref = refs
    modes = combined(modes_own[...], modes_other[...], halves_ref[0], halves_ref[1])
    write_bulk((modes_ref, outgoing_ref), modes, image_ref[0] if image_ref else None)


def merge_kernel(count, *refs):
    parts, (sketch_ref, old_ref, halves_ref, mine_ref) = refs[:count], refs[count:]
    half_own, half_other = merge(total_of(parts), sketch_ref)
    halves_ref[0] = half_own.astype(BF16)
    halves_ref[1] = half_other.astype(BF16)
    mine_ref[...] = nn_full(half_own, old_ref[...])


def last_merge_kernel(count, *refs):
    parts, (sketch_ref, *kept, halves_ref, out_ref, sems) = refs[:count], refs[count:]
    copies = [
        pltpu.make_async_copy(modes_ref, out_ref.at[level], sems.at[level])
        for level, modes_ref in enumerate(kept)
    ]
    for copy in copies:
        copy.start()
    half_own, half_other = merge(total_of(parts), sketch_ref)
    halves_ref[0] = half_own.astype(BF16)
    halves_ref[1] = half_other.astype(BF16)
    for copy in copies:
        copy.wait()


def apply_kernel(halves_ref, image_own, came_ref, shared_ref, far_image_t, *refs):
    image_other = choose("tm", came_ref[...], shared_ref[...])[1]
    image = combined(image_own[...], image_other, halves_ref[0], halves_ref[1])
    write_probe(refs, far_image_t, image)


def modes_kernel(halves_ref, modes_own, came_ref, shared_ref, *refs):
    *image_ref, modes_ref, outgoing_ref = refs
    modes_other = choose("tm", came_ref[...], shared_ref[...])[0]
    modes = combined(modes_own[...], modes_other, halves_ref[0], halves_ref[1])
    write_bulk((modes_ref, outgoing_ref), modes, image_ref[0] if image_ref else None)


def output_kernel(halves_ref, modes_own, came_ref, shared_ref, _, out_ref, modes_ref, sems):
    rows = modes_own.shape[0]
    modes_other = read_modes(came_ref, shared_ref, rows)
    part = rows // 2
    copies = []
    for half in range(2):
        span = slice(half * part, (half + 1) * part)
        modes_ref[span] = combined(
            modes_own[span], modes_other[span], halves_ref[0], halves_ref[1]
        )
        copies.append(
            pltpu.make_async_copy(
                modes_ref.at[pl.ds(half * part, part)],
                out_ref.at[out_ref.shape[0] - 1, pl.ds(half * part, part)],
                sems.at[half],
            )
        )
        copies[-1].start()
    for copy in copies:
        copy.wait()


def last_level(parts, sketch_t, kept, halves_shape):
    rows, width = kept[0].shape
    levels = len(kept)
    vmem = pl.BlockSpec(memory_space=pltpu.VMEM)
    hbm = pl.BlockSpec(memory_space=pltpu.HBM)
    return pl.pallas_call(
        functools.partial(last_merge_kernel, len(parts)),
        out_shape=[halves_shape, jax.ShapeDtypeStruct((levels + 1, rows, width), BF16)],
        in_specs=[vmem] * (len(parts) + 1 + levels),
        out_specs=[vmem, hbm],
        scratch_shapes=[pltpu.SemaphoreType.DMA((levels,))],
        compiler_params=PARAMS,
    )(*parts, sketch_t, *kept)


def last_modes(halves, modes, came, shared, out):
    vmem = pl.BlockSpec(memory_space=pltpu.VMEM)
    hbm = pl.BlockSpec(memory_space=pltpu.HBM)
    return pl.pallas_call(
        output_kernel,
        out_shape=jax.ShapeDtypeStruct(out.shape, BF16),
        in_specs=[vmem] * 4 + [hbm],
        out_specs=hbm,
        scratch_shapes=[pltpu.VMEM(modes.shape, BF16), pltpu.SemaphoreType.DMA((2,))],
        input_output_aliases={4: 0},
        compiler_params=PARAMS,
    )(halves, modes, came, shared, out)


def cross_kernel(total_rows, count, *refs):
    parts, (far_ref, out_ref) = refs[:count], refs[count:]
    out_ref[...] = nn_full(far_ref[...], total_of(parts) / total_rows).astype(BF16)


def modes_of(snapshots, energy, neighbours, sketch):
    block_count, _, block_rows, _ = energy.shape
    rows_dev, width = snapshots.shape
    space = lax.axis_size("space")
    total_rows = rows_dev * space
    levels = sketch.shape[0]
    blocks = snapshots.reshape(block_count, block_rows, width)
    head, tail = blocks[:HB], blocks[block_count - HB :]
    odd = (lax.axis_index("space") & 1) == 1
    near = [(i, i ^ 1) for i in range(space)]
    wide = [(i, (i + 2 * (i % 2) - 1) % space) for i in range(space)]
    came_near = lax.ppermute(jnp.where(odd, head, tail), "space", near)
    came_wide = lax.ppermute(jnp.where(odd, tail, head), "space", wide)
    square = jax.ShapeDtypeStruct((width, width), F32)
    modes_shape = jax.ShapeDtypeStruct((rows_dev, width), BF16)
    half_shape = jax.ShapeDtypeStruct((rows_dev // 2, width), BF16)
    factor_shape = jax.ShapeDtypeStruct((width + width // 2, width), F32)
    half_square = jax.ShapeDtypeStruct((width, width), BF16)
    halves_shape = jax.ShapeDtypeStruct((2, width, width), BF16)

    inner, sketch_t, edges, blocks = interior_of(neighbours, energy, blocks, sketch)
    image, image_t, gram = edge_of(neighbours, edges, came_near, blocks, came_wide, inner)
    other_image = swap(image, "tm", 1)
    pair = run_kernel(
        pair_kernel,
        factor_shape, gram, image_t, other_image,
    )
    parts = summands(pair, "space", space, 4)
    far_images = [swap(image_t, "tm", 2**level) for level in range(1, levels)]
    factor = run_kernel(
        functools.partial(leaf_kernel, total_rows, len(parts)), factor_shape, *parts
    )
    other_factor = swap(factor, "tm", 1)
    modes = run_kernel(
        leaf_modes_kernel, modes_shape, blocks.reshape(rows_dev, width), factor
    )
    other = swap(modes, "tm", 1)
    kept = [modes]
    for level in range(levels):
        last = level + 1 == levels
        deep = level + 2 < levels
        probe_outs = [half_square] + ([modes_shape] if deep else [])
        modes_outs = [modes_shape, modes_shape if deep else half_shape]
        if level > 0:
            far_mine = swap(mine, "tm", 2**level)
            parts = summands(probe, "space", space, 4)
            came = swap(outgoing, "tm", 2**level)
            shared = swap(came, "tm", 1)
            cross = run_kernel(
                functools.partial(cross_kernel, total_rows, len(parts)),
                half_square, *parts, far_mine,
            )
            parts = summands(cross, "tm", 2**level, 2)
        if level == 0:
            halves, mine, slices = run_kernel(
                first_merge_kernel, [halves_shape, square, halves_shape],
                factor, other_factor, sketch_t[level],
            )
        elif last:
            halves, out = last_level(parts, sketch_t[level], kept, halves_shape)
        else:
            halves, mine = run_kernel(
                functools.partial(merge_kernel, len(parts)), [halves_shape, square],
                *parts, sketch_t[level], mine,
            )
        if last:
            out = last_modes(halves, modes, came, shared, out)
            break
        if level == 0:
            probe, *image = run_kernel(
                first_apply_kernel, probe_outs,
                slices, image, other_image, far_images[level],
            )
        else:
            probe, *image = run_kernel(
                apply_kernel, probe_outs,
                halves, image[0], came, shared, far_images[level],
            )
        if level == 0:
            modes, outgoing = run_kernel(
                first_modes_kernel, modes_outs, halves, modes, other, *image
            )
        else:
            modes, outgoing = run_kernel(
                modes_kernel, modes_outs, halves, modes, came, shared, *image
            )
        kept.append(modes)
    return out[:, None]


def solution(mesh):
    placed = (P("space", "tm"), P("space", None, None, None), P("space", None), P())
    return jax.shard_map(
        modes_of,
        mesh=mesh,
        in_specs=placed,
        out_specs=P(None, "tm", "space", None),
        check_vma=False,
    )
```

```python
import functools

import jax
import jax.numpy as jnp
from jax import lax
from jax.experimental import pallas as pl
from jax.experimental.pallas import tpu as pltpu
from jax.sharding import PartitionSpec as P


HB = 2
PANEL = 8
F32 = jnp.float32
BF16 = jnp.bfloat16
PARAMS = pltpu.CompilerParams(vmem_limit_bytes=16 * 1024 * 1024)


def swap(value, axis, mask):
    pairs = [(source, source ^ mask) for source in range(lax.axis_size(axis))]
    return lax.ppermute(value, axis, pairs)


def mixed_swap(value, even, odd):
    space = lax.axis_size("space")
    pairs = []
    for t in range(lax.axis_size("tm")):
        masks = odd if t % 2 else even
        for place in range(space):
            target = (t ^ masks[0]) * space + (place ^ masks[1])
            pairs.append((t * space + place, target))
    return lax.ppermute(value, ("tm", "space"), pairs)


def summands(value, axis, count, widest, done=1):
    parts = [value]
    while done < count:
        if len(parts) > 1:
            value = run_kernel(add_kernel, jax.ShapeDtypeStruct(value.shape, value.dtype), *parts)
        radix = 4 if widest == 4 and count // done % 4 == 0 else 2
        parts = [value]
        for step in range(1, radix):
            parts.append(swap(value, axis, step * done))
        done *= radix
    return parts


def add_kernel(*refs):
    refs[-1][...] = total_of(refs[:-1]).astype(refs[-1].dtype)


def total_of(parts):
    values = [part[...].astype(F32) for part in parts]
    while len(values) > 1:
        values = [a + b for a, b in zip(values[::2], values[1::2])]
    return values[0]


def dot_nn(a, b):
    return lax.dot_general(a, b, (((1,), (0,)), ((), ())), preferred_element_type=F32)


def dot_nt(a, b):
    return lax.dot_general(a, b, (((1,), (1,)), ((), ())), preferred_element_type=F32)


def split(value):
    high = value.astype(BF16)
    return high, (value - high.astype(F32)).astype(BF16)


def full(dot, axis, a, b):
    a_high, a_low = split(a)
    b_high, b_low = split(b)
    left = jnp.concatenate([a_high, a_high, a_low], axis=1)
    return dot(left, jnp.concatenate([b_high, b_low, b_high], axis=axis))


nn_full = functools.partial(full, dot_nn, 0)
nt_full = functools.partial(full, dot_nt, 1)


def inverse_factor(matrix):
    size = matrix.shape[0]
    panels = size // PANEL
    shape = (PANEL, size)
    lane = lax.broadcasted_iota(jnp.int32, shape, 1)
    sub = lax.broadcasted_iota(jnp.int32, shape, 0)

    def column(rows, index):
        return jnp.broadcast_to(rows[:, index : index + 1], shape)

    def row(rows, index):
        return jnp.broadcast_to(rows[index : index + 1, :], shape)

    rows_of = [matrix[PANEL * i : PANEL * (i + 1), :] for i in range(panels)]
    out = []
    block = [column(rows_of[0], j) for j in range(PANEL)]
    for k in range(panels):
        base = PANEL * k
        active = rows_of[k]
        ahead = (
            [column(active, base + PANEL + j) for j in range(PANEL)] if k + 1 < panels else []
        )
        here = (lane >= base) & (lane < base + PANEL)
        active = jnp.where(here, jnp.where(lane == sub + base, 1.0, 0.0), active)
        kept = active
        pivots = block[0]
        for j in range(PANEL):
            pivot = row(block[j], j)
            factor = jnp.where(sub == j, 0.0, block[j]) * (1.0 / pivot)
            kept = jnp.where(sub == j, active, kept)
            pivots = jnp.where(sub == j, pivot, pivots)
            active = active - factor * row(active, j)
            for q in range(j + 1, PANEL):
                block[q] = block[q] - factor * row(block[q], j)
            ahead = [item - factor * row(item, j) for item in ahead]
        out.append(jnp.where(lane < base + PANEL, kept * lax.rsqrt(pivots), 0.0))
        if k + 1 == panels:
            break
        scale = 1.0 / pivots
        solved = active * scale
        solved_rows = [row(solved, j) for j in range(PANEL)]
        block = []
        for i in range(k + 1, panels):
            old = rows_of[i]
            columns = [column(old, base + j) for j in range(PANEL)]
            if i == k + 1:
                for q in range(PANEL):
                    item = column(old, base + PANEL + q)
                    scaled = ahead[q] * scale
                    for j in range(PANEL):
                        item = item - columns[j] * row(scaled, j)
                    block.append(item)
            new = jnp.where(here, 0.0, old)
            for j in range(PANEL):
                new = new - columns[j] * solved_rows[j]
            rows_of[i] = new
    return jnp.concatenate(out, axis=0)


def run_kernel(body, outs, *operands):
    cost = pl.CostEstimate(flops=2_000_000_000, bytes_accessed=1_000_000, transcendentals=0)
    return pl.pallas_call(
        body, out_shape=outs, cost_estimate=cost, compiler_params=PARAMS
    )(*operands)


def coupled(energy_ref, place, slots, lookup):
    left = jnp.concatenate([energy_ref[place, slot] for slot in range(slots)], axis=1)
    right = jnp.concatenate([lookup(slot) for slot in range(slots)], axis=0)
    return dot_nn(left, right)


def interior_kernel(
    index_hbm, energy_hbm, blocks_hbm, sketch_hbm,
    image_ref, sketch_out, edges_ref, blocks_ref, index_ref, energy_ref, sketch_ref, sems,
):
    count = blocks_ref.shape[0]
    inner, slots = energy_ref.shape[:2]
    width = sketch_out.shape[2]
    copies = [
        pltpu.make_async_copy(source, target, sems.at[place])
        for place, (source, target) in enumerate(
            [
                (index_hbm, index_ref),
                (blocks_hbm, blocks_ref),
                (energy_hbm.at[pl.ds(HB, inner)], energy_ref),
                (sketch_hbm, sketch_ref),
                (energy_hbm.at[pl.ds(0, HB)], edges_ref.at[0]),
                (energy_hbm.at[pl.ds(count - HB, HB)], edges_ref.at[1]),
            ]
        )
    ]
    for copy in copies:
        copy.start()
    first = lax.axis_index("space") * count
    window = lax.axis_index("tm")
    for copy in copies[:3]:
        copy.wait()
    for place in range(inner):
        b = HB + place
        value = 3.0 * blocks_ref[b].astype(F32) + coupled(
            energy_ref, place, slots, lambda slot: blocks_ref[index_ref[b, slot] - first]
        )
        image_ref[place] = value.astype(BF16)
    copies[3].wait()
    for level in range(sketch_ref.shape[0]):
        upper = window // 2**level % 2
        for half in range(2):
            start = pl.multiple_of((upper ^ half) * width, width)
            sketch_out[level, half] = sketch_ref[level, pl.ds(start, width), :].T
    for copy in copies[4:]:
        copy.wait()


def edge_kernel(
    index_ref, edges_ref, near_ref, blocks_ref, wide_ref, inner_ref,
    image_ref, image_t_ref, gram_ref, padded_ref,
):
    slots = edges_ref.shape[2]
    blocks = blocks_ref.shape[0]
    before, after = choose("space", wide_ref[...], near_ref[...])
    padded_ref[0, :HB] = before
    padded_ref[0, HB:] = blocks_ref[: 2 * HB]
    padded_ref[1, : 2 * HB] = blocks_ref[blocks - 2 * HB :]
    padded_ref[1, 2 * HB :] = after
    image_ref[HB : blocks - HB] = inner_ref[...]
    for side in range(2):
        first = lax.axis_index("space") * blocks - HB + side * (blocks - HB)
        for place in range(HB):
            b = side * (blocks - HB) + place
            value = 3.0 * blocks_ref[b].astype(F32) + coupled(
                edges_ref.at[side], place, slots,
                lambda slot: padded_ref[side, index_ref[b, slot] - first],
            )
            image_ref[b] = value.astype(BF16)
    image = image_ref[...].reshape(image_t_ref.shape[1], image_t_ref.shape[0])
    image_t = image.T
    image_t_ref[...] = image_t
    gram_ref[...] = dot_nn(image_t, image)


def interior_of(neighbours, energy, blocks, sketch):
    count, slots, rows, _ = energy.shape
    width = blocks.shape[2]
    levels = sketch.shape[0]
    inner = count - 2 * HB
    return pl.pallas_call(
        interior_kernel,
        out_shape=[
            jax.ShapeDtypeStruct((inner, rows, width), BF16),
            jax.ShapeDtypeStruct((levels, 2, width, width), F32),
            jax.ShapeDtypeStruct((2, HB, slots, rows, rows), BF16),
            jax.ShapeDtypeStruct(blocks.shape, BF16),
        ],
        in_specs=[pl.BlockSpec(memory_space=pltpu.HBM)] * 4,
        scratch_shapes=[
            pltpu.SMEM(neighbours.shape, jnp.int32),
            pltpu.VMEM((inner, slots, rows, rows), BF16),
            pltpu.VMEM(sketch.shape, F32),
            pltpu.SemaphoreType.DMA((6,)),
        ],
        compiler_params=PARAMS,
    )(*[pltpu.with_memory_space_constraint(item, pltpu.HBM) for item in (neighbours, energy, blocks, sketch)])


def edge_of(neighbours, edges, came_near, blocks, came_wide, inner):
    count, rows, width = blocks.shape
    image, image_t, gram = pl.pallas_call(
        edge_kernel,
        out_shape=[
            jax.ShapeDtypeStruct((count, rows, width), BF16),
            jax.ShapeDtypeStruct((width, count * rows), BF16),
            jax.ShapeDtypeStruct((width, width), F32),
        ],
        in_specs=[pl.BlockSpec(memory_space=pltpu.SMEM)]
        + [pl.BlockSpec(memory_space=pltpu.VMEM)] * 5,
        scratch_shapes=[pltpu.VMEM((2, 3 * HB, rows, width), BF16)],
        compiler_params=PARAMS,
    )(neighbours, edges, came_near, blocks, came_wide, inner)
    return image.reshape(count * rows, width), image_t, gram


def pair_kernel(gram_ref, image_t_ref, other_ref, out_ref):
    width = gram_ref.shape[0]
    out_ref[:width] = gram_ref[...]
    cross = dot_nn(image_t_ref[...], other_ref[...])
    odd = lax.axis_index("tm") % 2 == 1
    out_ref[width:] = jnp.where(odd, cross.T[width // 2 :], cross[: width // 2])


def leaf_kernel(total_rows, count, *refs):
    parts, (factor_ref,) = refs[:count], refs[count:]
    width = factor_ref.shape[1]
    grams = total_of(parts) / total_rows
    factor_ref[width:] = grams[width:]
    inverse = inverse_factor(grams[:width])
    factor_ref[:width] = inverse


def leaf_modes_kernel(snapshots_ref, factor_ref, modes_ref):
    inverse = factor_ref[: factor_ref.shape[1]]
    modes_ref[...] = dot_nt(snapshots_ref[...], inverse.astype(BF16)).astype(BF16)


def merge(cross_t, sketch_ref):
    sketch_own, sketch_other = sketch_ref[0], sketch_ref[1]
    columns_own = sketch_own + nn_full(sketch_other, cross_t)
    columns_other = nt_full(sketch_own, cross_t) + sketch_other
    image_own = columns_own + nn_full(columns_other, cross_t)
    image_other = nt_full(columns_own, cross_t) + columns_other
    inner = nt_full(
        jnp.concatenate([columns_own, columns_other], axis=1),
        jnp.concatenate([image_own, image_other], axis=1),
    )
    inverse = inverse_factor(inner)
    return nn_full(inverse, columns_own), nn_full(inverse, columns_other)


def combined(own, other, half_own, half_other):
    joined = jnp.concatenate([own, other], axis=1)
    halves = jnp.concatenate([half_own.astype(BF16), half_other.astype(BF16)], axis=1)
    return dot_nt(joined, halves).astype(BF16)


def choose(axis, first, second):
    odd = (lax.axis_index(axis) & 1) == 1
    return jnp.where(odd, second, first), jnp.where(odd, first, second)


def write_bulk(refs, modes, image_ref):
    modes_ref, outgoing_ref = refs
    modes_ref[...] = modes
    if image_ref is not None:
        outgoing_ref[...] = choose("tm", modes, image_ref[...])[0]
    else:
        part = outgoing_ref.shape[0]
        outgoing_ref[...] = choose("tm", modes[:part], modes[part:])[0]


def read_modes(came_ref, shared_ref, rows):
    first, second = choose("tm", came_ref[...], shared_ref[...])
    if first.shape[0] == rows:
        return first
    return jnp.concatenate([first, second], axis=0)


def first_merge_kernel(own_ref, other_ref, sketch_ref, halves_ref, slices_ref):
    width = own_ref.shape[1]
    own, other = own_ref[:width], other_ref[:width]
    even, odd = choose("tm", own, other)
    pair_gram = jnp.concatenate(choose("tm", own_ref[width:], other_ref[width:]), axis=0)
    cross = nt_full(nn_full(even, pair_gram), odd)
    cross_t = jnp.where(lax.axis_index("tm") % 2 == 1, cross, cross.T)
    half_own, half_other = merge(cross_t, sketch_ref)
    halves_ref[0] = half_own.astype(BF16)
    halves_ref[1] = half_other.astype(BF16)
    slices = choose("tm", nn_full(half_own, own), nn_full(half_other, other))
    slices_ref[:width] = slices[0]
    slices_ref[width:] = slices[1]


def write_probes(refs, slices, far_t, shared_t, image):
    probes_ref, second_ref, *image_ref = refs
    probes = jnp.concatenate(
        [dot_nn(far, image) for far in choose("tm", far_t[...], shared_t[...])], axis=0
    ).astype(BF16)
    probes_ref[...] = probes
    second_ref[...] = choose("tm", probes, slices)[0]
    if image_ref:
        image_ref[0][...] = image


def first_apply_kernel(slices_ref, image_own, image_other, far_t, shared_t, *refs):
    slices = slices_ref[...].astype(BF16)
    width = slices.shape[1]
    own, other = choose("tm", slices[:width], slices[width:])
    image = combined(image_own[...], image_other[...], own, other)
    write_probes(refs, slices, far_t, shared_t, image)


def pick_kernel(probes_ref, slices_ref, out_ref):
    out_ref[...] = choose("tm", probes_ref[...], slices_ref[...].astype(BF16))[0]


def first_modes_kernel(halves_ref, modes_own, modes_other, *refs):
    *image_ref, modes_ref, outgoing_ref = refs
    modes = combined(modes_own[...], modes_other[...], halves_ref[0], halves_ref[1])
    write_bulk((modes_ref, outgoing_ref), modes, image_ref[0] if image_ref else None)


def cross_of(total_rows, own_ref, one_ref, two_ref, shared_one, shared_two):
    first, second = choose("tm", one_ref[...], shared_one[...])
    third, slices = choose("tm", two_ref[...], shared_two[...])
    probes = (own_ref[...].astype(F32) + first.astype(F32)) + (
        second.astype(F32) + third.astype(F32)
    )
    high, low = split(probes / total_rows)
    width = slices.shape[1]
    left = jnp.concatenate([slices[:width], slices[width:]] * 2, axis=1)
    return dot_nn(left, jnp.concatenate([high, low], axis=0))


def write_coefficients(halves_ref, slices_ref, old_ref, half_own, half_other):
    halves_ref[0] = half_own.astype(BF16)
    halves_ref[1] = half_other.astype(BF16)
    width = old_ref.shape[1]
    slices_ref[:width] = nn_full(half_own, old_ref[:width])
    slices_ref[width:] = nn_full(half_own, old_ref[width:])


def near_merge_kernel(total_rows, *refs):
    *arrivals, sketch_ref, old_ref, halves_ref, slices_ref = refs
    half_own, half_other = merge(cross_of(total_rows, *arrivals), sketch_ref)
    write_coefficients(halves_ref, slices_ref, old_ref, half_own, half_other)


def merge_kernel(count, *refs):
    parts, (sketch_ref, old_ref, halves_ref, slices_ref) = refs[:count], refs[count:]
    half_own, half_other = merge(total_of(parts), sketch_ref)
    write_coefficients(halves_ref, slices_ref, old_ref, half_own, half_other)


def last_merge_kernel(count, *refs):
    parts, (sketch_ref, *kept, halves_ref, out_ref, sems) = refs[:count], refs[count:]
    copies = [
        pltpu.make_async_copy(modes_ref, out_ref.at[level], sems.at[level])
        for level, modes_ref in enumerate(kept)
    ]
    for copy in copies:
        copy.start()
    half_own, half_other = merge(total_of(parts), sketch_ref)
    halves_ref[0] = half_own.astype(BF16)
    halves_ref[1] = half_other.astype(BF16)
    for copy in copies:
        copy.wait()


def apply_kernel(halves_ref, slices_ref, image_own, came_ref, shared_ref, far_t, shared_t, *refs):
    image_other = choose("tm", came_ref[...], shared_ref[...])[1]
    image = combined(image_own[...], image_other, halves_ref[0], halves_ref[1])
    write_probes(refs, slices_ref[...].astype(BF16), far_t, shared_t, image)


def modes_kernel(halves_ref, modes_own, came_ref, shared_ref, *refs):
    *image_ref, modes_ref, outgoing_ref = refs
    modes_other = choose("tm", came_ref[...], shared_ref[...])[0]
    modes = combined(modes_own[...], modes_other, halves_ref[0], halves_ref[1])
    write_bulk((modes_ref, outgoing_ref), modes, image_ref[0] if image_ref else None)


def output_kernel(halves_ref, modes_own, came_ref, shared_ref, _, out_ref, modes_ref, sems):
    rows = modes_own.shape[0]
    modes_other = read_modes(came_ref, shared_ref, rows)
    part = rows // 2
    copies = []
    for half in range(2):
        span = slice(half * part, (half + 1) * part)
        modes_ref[span] = combined(
            modes_own[span], modes_other[span], halves_ref[0], halves_ref[1]
        )
        copies.append(
            pltpu.make_async_copy(
                modes_ref.at[pl.ds(half * part, part)],
                out_ref.at[out_ref.shape[0] - 1, pl.ds(half * part, part)],
                sems.at[half],
            )
        )
        copies[-1].start()
    for copy in copies:
        copy.wait()


def last_level(parts, sketch_t, kept, halves_shape):
    rows, width = kept[0].shape
    levels = len(kept)
    vmem = pl.BlockSpec(memory_space=pltpu.VMEM)
    hbm = pl.BlockSpec(memory_space=pltpu.HBM)
    return pl.pallas_call(
        functools.partial(last_merge_kernel, len(parts)),
        out_shape=[halves_shape, jax.ShapeDtypeStruct((levels + 1, rows, width), BF16)],
        in_specs=[vmem] * (len(parts) + 1 + levels),
        out_specs=[vmem, hbm],
        scratch_shapes=[pltpu.SemaphoreType.DMA((levels,))],
        compiler_params=PARAMS,
    )(*parts, sketch_t, *kept)


def last_modes(halves, modes, came, shared, out):
    vmem = pl.BlockSpec(memory_space=pltpu.VMEM)
    hbm = pl.BlockSpec(memory_space=pltpu.HBM)
    return pl.pallas_call(
        output_kernel,
        out_shape=jax.ShapeDtypeStruct(out.shape, BF16),
        in_specs=[vmem] * 4 + [hbm],
        out_specs=hbm,
        scratch_shapes=[pltpu.VMEM(modes.shape, BF16), pltpu.SemaphoreType.DMA((2,))],
        input_output_aliases={4: 0},
        compiler_params=PARAMS,
    )(halves, modes, came, shared, out)


def cross_kernel(total_rows, *refs):
    *arrivals, out_ref = refs
    out_ref[...] = cross_of(total_rows, *arrivals).astype(BF16)


def modes_of(snapshots, energy, neighbours, sketch):
    block_count, _, block_rows, _ = energy.shape
    rows_dev, width = snapshots.shape
    space = lax.axis_size("space")
    total_rows = rows_dev * space
    levels = sketch.shape[0]
    blocks = snapshots.reshape(block_count, block_rows, width)
    head, tail = blocks[:HB], blocks[block_count - HB :]
    odd = (lax.axis_index("space") & 1) == 1
    near = [(i, i ^ 1) for i in range(space)]
    wide = [(i, (i + 2 * (i % 2) - 1) % space) for i in range(space)]
    came_near = lax.ppermute(jnp.where(odd, head, tail), "space", near)
    came_wide = lax.ppermute(jnp.where(odd, tail, head), "space", wide)
    modes_shape = jax.ShapeDtypeStruct((rows_dev, width), BF16)
    half_shape = jax.ShapeDtypeStruct((rows_dev // 2, width), BF16)
    factor_shape = jax.ShapeDtypeStruct((width + width // 2, width), F32)
    half_square = jax.ShapeDtypeStruct((width, width), BF16)
    pair_square = jax.ShapeDtypeStruct((2 * width, width), BF16)
    slices_shape = jax.ShapeDtypeStruct((2 * width, width), F32)
    halves_shape = jax.ShapeDtypeStruct((2, width, width), BF16)

    inner, sketch_t, edges, blocks = interior_of(neighbours, energy, blocks, sketch)
    image, image_t, gram = edge_of(neighbours, edges, came_near, blocks, came_wide, inner)
    other_image = swap(image, "tm", 1)
    pair = run_kernel(
        pair_kernel,
        factor_shape, gram, image_t, other_image,
    )
    parts = summands(pair, "space", space, 4)
    far_images = [swap(image_t, "tm", 2**level) for level in range(1, levels)]
    factor = run_kernel(
        functools.partial(leaf_kernel, total_rows, len(parts)), factor_shape, *parts
    )
    other_factor = swap(factor, "tm", 1)
    modes = run_kernel(
        leaf_modes_kernel, modes_shape, blocks.reshape(rows_dev, width), factor
    )
    other = swap(modes, "tm", 1)
    kept = [modes]
    for level in range(levels):
        last = level + 1 == levels
        deep = level + 2 < levels
        probe_outs = [pair_square] * 2 + ([modes_shape] if deep else [])
        modes_outs = [modes_shape, modes_shape if deep else half_shape]
        if level > 0:
            quarter = space // 4
            if quarter > 1:
                parts = summands(probes, "space", quarter, 4)
                probes = run_kernel(add_kernel, pair_square, *parts)
                second = run_kernel(pick_kernel, pair_square, probes, slices)
            one = mixed_swap(probes, (0, quarter), (0, 2 * quarter))
            two = mixed_swap(second, (0, 3 * quarter), (2**level, 0))
            came = swap(outgoing, "tm", 2**level)
            shared = swap(came, "tm", 1)
            arrivals = [
                probes, one, two,
                swap(one, "tm", 1), swap(two, "tm", 1),
            ]
            if level > 1:
                cross = run_kernel(
                    functools.partial(cross_kernel, total_rows), half_square, *arrivals
                )
                parts = summands(cross, "tm", 2**level, 2, done=2)
        outs = [halves_shape, slices_shape]
        if level == 0:
            halves, slices = run_kernel(
                first_merge_kernel, outs, factor, other_factor, sketch_t[level]
            )
        elif last:
            halves, out = last_level(parts, sketch_t[level], kept, halves_shape)
        elif level == 1:
            halves, slices = run_kernel(
                functools.partial(near_merge_kernel, total_rows), outs,
                *arrivals, sketch_t[level], slices,
            )
        else:
            halves, slices = run_kernel(
                functools.partial(merge_kernel, len(parts)), outs,
                *parts, sketch_t[level], slices,
            )
        if last:
            out = last_modes(halves, modes, came, shared, out)
            break
        far = far_images[level]
        far_shared = swap(far, "tm", 1)
        if level == 0:
            probes, second, *image = run_kernel(
                first_apply_kernel, probe_outs,
                slices, image, other_image, far, far_shared,
            )
        else:
            probes, second, *image = run_kernel(
                apply_kernel, probe_outs,
                halves, slices, image[0], came, shared, far, far_shared,
            )
        if level == 0:
            modes, outgoing = run_kernel(
                first_modes_kernel, modes_outs, halves, modes, other, *image
            )
        else:
            modes, outgoing = run_kernel(
                modes_kernel, modes_outs, halves, modes, came, shared, *image
            )
        kept.append(modes)
    return out[:, None]


def solution(mesh):
    placed = (P("space", "tm"), P("space", None, None, None), P("space", None), P())
    return jax.shard_map(
        modes_of,
        mesh=mesh,
        in_specs=placed,
        out_specs=P(None, "tm", "space", None),
        check_vma=False,
    )
```

```python
import functools

import jax
import jax.numpy as jnp
from jax import lax
from jax.experimental import pallas as pl
from jax.experimental.pallas import tpu as pltpu
from jax.sharding import PartitionSpec as P


HB = 2
PANEL = 8
F32 = jnp.float32
BF16 = jnp.bfloat16
PARAMS = pltpu.CompilerParams(vmem_limit_bytes=16 * 1024 * 1024)


def swap(value, axis, mask):
    pairs = [(source, source ^ mask) for source in range(lax.axis_size(axis))]
    return lax.ppermute(value, axis, pairs)


def mixed_swap(value, even, odd):
    space = lax.axis_size("space")
    pairs = []
    for t in range(lax.axis_size("tm")):
        masks = odd if t % 2 else even
        for place in range(space):
            target = (t ^ masks[0]) * space + (place ^ masks[1])
            pairs.append((t * space + place, target))
    return lax.ppermute(value, ("tm", "space"), pairs)


def summands(value, axis, count, widest, done=1):
    parts = [value]
    while done < count:
        if len(parts) > 1:
            value = run_kernel(add_kernel, jax.ShapeDtypeStruct(value.shape, value.dtype), *parts)
        radix = 4 if widest == 4 and count // done % 4 == 0 else 2
        parts = [value]
        for step in range(1, radix):
            parts.append(swap(value, axis, step * done))
        done *= radix
    return parts


def add_kernel(*refs):
    refs[-1][...] = total_of(refs[:-1]).astype(refs[-1].dtype)


def total_of(parts):
    values = [part[...].astype(F32) for part in parts]
    while len(values) > 1:
        values = [a + b for a, b in zip(values[::2], values[1::2])]
    return values[0]


def dot_nn(a, b):
    return lax.dot_general(a, b, (((1,), (0,)), ((), ())), preferred_element_type=F32)


def dot_nt(a, b):
    return lax.dot_general(a, b, (((1,), (1,)), ((), ())), preferred_element_type=F32)


def split(value):
    high = value.astype(BF16)
    return high, (value - high.astype(F32)).astype(BF16)


def full(dot, axis, a, b):
    a_high, a_low = split(a)
    b_high, b_low = split(b)
    left = jnp.concatenate([a_high, a_high, a_low], axis=1)
    return dot(left, jnp.concatenate([b_high, b_low, b_high], axis=axis))


nn_full = functools.partial(full, dot_nn, 0)
nt_full = functools.partial(full, dot_nt, 1)


def inverse_factor(matrix, exact=False):
    size = matrix.shape[0]
    panels = size // PANEL
    shape = (PANEL, size)
    lane = lax.broadcasted_iota(jnp.int32, shape, 1)
    sub = lax.broadcasted_iota(jnp.int32, shape, 0)

    def column(rows, index):
        return jnp.broadcast_to(rows[:, index : index + 1], shape)

    def row(rows, index):
        return jnp.broadcast_to(rows[index : index + 1, :], shape)

    rows_of = [matrix[PANEL * i : PANEL * (i + 1), :] for i in range(panels)]
    zero = jnp.zeros(shape, F32)
    out = []
    block = [column(rows_of[0], j) for j in range(PANEL)]
    for k in range(panels):
        base = PANEL * k
        final = k + 1 == panels
        active = rows_of[k]
        here = (lane >= base) & (lane < base + PANEL)
        if not final:
            below = rows_of[k + 1]
            under = [column(below, base + j) for j in range(PANEL)]
            ahead = [column(active, base + PANEL + q) for q in range(PANEL)]
            following = [column(below, base + PANEL + q) for q in range(PANEL)]
            below = jnp.where(here, 0.0, below)
        active = jnp.where(here, jnp.where(lane == sub + base, 1.0, 0.0), active)
        kept = active
        pivots = block[0]
        for j in range(PANEL):
            pivot = row(block[j], j)
            inverse = 1.0 / pivot
            factor = jnp.where(sub == j, 0.0, block[j]) * inverse
            leading = row(active, j)
            kept = jnp.where(sub == j, active, kept)
            pivots = jnp.where(sub == j, pivot, pivots)
            active = active - factor * leading
            if not final:
                lower = under[j] * inverse
                below = below - lower * leading
            for q in range(j + 1, PANEL):
                item = row(block[q], j)
                block[q] = block[q] - factor * item
                if not final:
                    under[q] = under[q] - lower * item
            if not final:
                for q in range(PANEL):
                    item = row(ahead[q], j)
                    ahead[q] = ahead[q] - factor * item
                    following[q] = following[q] - lower * item
        out.append(jnp.where(lane < base + PANEL, kept * lax.rsqrt(pivots), 0.0))
        if final:
            break
        rows_of[k + 1] = below
        block = following
        if k + 2 < panels:
            solved = active * (1.0 / pivots)
            solved_rows = [row(solved, j) for j in range(PANEL)]
            for i in range(k + 2, panels if exact else k + 3):
                old = rows_of[i]
                new = jnp.where(here, 0.0, old)
                for j in range(PANEL):
                    new = new - column(old, base + j) * solved_rows[j]
                rows_of[i] = new
        if k + 3 < panels and not exact:
            rest = rows_of[k + 3 :]
            spread = jnp.concatenate([zero] * k + [solved] + [zero] * (panels - k - 1), axis=0)
            change = nn_full(jnp.concatenate(rest, axis=0), spread)
            for i, old in enumerate(rest):
                part = change[PANEL * i : PANEL * (i + 1)]
                rows_of[k + 3 + i] = jnp.where(here, 0.0, old) - part
    return jnp.concatenate(out, axis=0)


def run_kernel(body, outs, *operands):
    cost = pl.CostEstimate(flops=2_000_000_000, bytes_accessed=1_000_000, transcendentals=0)
    return pl.pallas_call(
        body, out_shape=outs, cost_estimate=cost, compiler_params=PARAMS
    )(*operands)


def coupled(energy_ref, place, slots, lookup):
    left = jnp.concatenate([energy_ref[place, slot] for slot in range(slots)], axis=1)
    right = jnp.concatenate([lookup(slot) for slot in range(slots)], axis=0)
    return dot_nn(left, right)


def interior_kernel(
    index_hbm, energy_hbm, blocks_hbm, sketch_hbm,
    image_ref, sketch_out, edges_ref, blocks_ref, index_ref, energy_ref, sketch_ref, sems,
):
    count = blocks_ref.shape[0]
    inner, slots = energy_ref.shape[:2]
    width = sketch_out.shape[2]
    copies = [
        pltpu.make_async_copy(source, target, sems.at[place])
        for place, (source, target) in enumerate(
            [
                (index_hbm, index_ref),
                (blocks_hbm, blocks_ref),
                (energy_hbm.at[pl.ds(HB, inner)], energy_ref),
                (sketch_hbm, sketch_ref),
                (energy_hbm.at[pl.ds(0, HB)], edges_ref.at[0]),
                (energy_hbm.at[pl.ds(count - HB, HB)], edges_ref.at[1]),
            ]
        )
    ]
    for copy in copies:
        copy.start()
    first = lax.axis_index("space") * count
    window = lax.axis_index("tm")
    for copy in copies[:3]:
        copy.wait()
    for place in range(inner):
        b = HB + place
        value = 3.0 * blocks_ref[b].astype(F32) + coupled(
            energy_ref, place, slots, lambda slot: blocks_ref[index_ref[b, slot] - first]
        )
        image_ref[place] = value.astype(BF16)
    copies[3].wait()
    for level in range(sketch_ref.shape[0]):
        upper = window // 2**level % 2
        for half in range(2):
            start = pl.multiple_of((upper ^ half) * width, width)
            sketch_out[level, half] = sketch_ref[level, pl.ds(start, width), :].T
    for copy in copies[4:]:
        copy.wait()


def edge_kernel(
    index_ref, edges_ref, near_ref, blocks_ref, wide_ref, inner_ref,
    image_ref, image_t_ref, gram_ref, padded_ref,
):
    slots = edges_ref.shape[2]
    blocks = blocks_ref.shape[0]
    before, after = choose("space", wide_ref[...], near_ref[...])
    padded_ref[0, :HB] = before
    padded_ref[0, HB:] = blocks_ref[: 2 * HB]
    padded_ref[1, : 2 * HB] = blocks_ref[blocks - 2 * HB :]
    padded_ref[1, 2 * HB :] = after
    image_ref[HB : blocks - HB] = inner_ref[...]
    for side in range(2):
        first = lax.axis_index("space") * blocks - HB + side * (blocks - HB)
        for place in range(HB):
            b = side * (blocks - HB) + place
            value = 3.0 * blocks_ref[b].astype(F32) + coupled(
                edges_ref.at[side], place, slots,
                lambda slot: padded_ref[side, index_ref[b, slot] - first],
            )
            image_ref[b] = value.astype(BF16)
    image = image_ref[...].reshape(image_t_ref.shape[1], image_t_ref.shape[0])
    image_t = image.T
    image_t_ref[...] = image_t
    gram_ref[...] = dot_nn(image_t, image)


def interior_of(neighbours, energy, blocks, sketch):
    count, slots, rows, _ = energy.shape
    width = blocks.shape[2]
    levels = sketch.shape[0]
    inner = count - 2 * HB
    return pl.pallas_call(
        interior_kernel,
        out_shape=[
            jax.ShapeDtypeStruct((inner, rows, width), BF16),
            jax.ShapeDtypeStruct((levels, 2, width, width), F32),
            jax.ShapeDtypeStruct((2, HB, slots, rows, rows), BF16),
            jax.ShapeDtypeStruct(blocks.shape, BF16),
        ],
        in_specs=[pl.BlockSpec(memory_space=pltpu.HBM)] * 4,
        scratch_shapes=[
            pltpu.SMEM(neighbours.shape, jnp.int32),
            pltpu.VMEM((inner, slots, rows, rows), BF16),
            pltpu.VMEM(sketch.shape, F32),
            pltpu.SemaphoreType.DMA((6,)),
        ],
        compiler_params=PARAMS,
    )(*[pltpu.with_memory_space_constraint(item, pltpu.HBM) for item in (neighbours, energy, blocks, sketch)])


def edge_of(neighbours, edges, came_near, blocks, came_wide, inner):
    count, rows, width = blocks.shape
    image, image_t, gram = pl.pallas_call(
        edge_kernel,
        out_shape=[
            jax.ShapeDtypeStruct((count, rows, width), BF16),
            jax.ShapeDtypeStruct((width, count * rows), BF16),
            jax.ShapeDtypeStruct((width, width), F32),
        ],
        in_specs=[pl.BlockSpec(memory_space=pltpu.SMEM)]
        + [pl.BlockSpec(memory_space=pltpu.VMEM)] * 5,
        scratch_shapes=[pltpu.VMEM((2, 3 * HB, rows, width), BF16)],
        compiler_params=PARAMS,
    )(neighbours, edges, came_near, blocks, came_wide, inner)
    return image.reshape(count * rows, width), image_t, gram


def pair_kernel(gram_ref, image_t_ref, other_ref, out_ref):
    width = gram_ref.shape[0]
    out_ref[:width] = gram_ref[...]
    cross = dot_nn(image_t_ref[...], other_ref[...])
    odd = lax.axis_index("tm") % 2 == 1
    out_ref[width:] = jnp.where(odd, cross.T[width // 2 :], cross[: width // 2])


def leaf_kernel(total_rows, count, *refs):
    parts, (factor_ref,) = refs[:count], refs[count:]
    width = factor_ref.shape[1]
    grams = total_of(parts) / total_rows
    factor_ref[width:] = grams[width:]
    inverse = inverse_factor(grams[:width], exact=True)
    factor_ref[:width] = inverse


def leaf_modes_kernel(snapshots_ref, factor_ref, modes_ref):
    inverse = factor_ref[: factor_ref.shape[1]]
    modes_ref[...] = dot_nt(snapshots_ref[...], inverse.astype(BF16)).astype(BF16)


def merge(cross_t, sketch_ref):
    sketch_own, sketch_other = sketch_ref[0], sketch_ref[1]
    columns_own = sketch_own + nn_full(sketch_other, cross_t)
    columns_other = nt_full(sketch_own, cross_t) + sketch_other
    image_own = columns_own + nn_full(columns_other, cross_t)
    image_other = nt_full(columns_own, cross_t) + columns_other
    inner = nt_full(
        jnp.concatenate([columns_own, columns_other], axis=1),
        jnp.concatenate([image_own, image_other], axis=1),
    )
    inverse = inverse_factor(inner)
    return nn_full(inverse, columns_own), nn_full(inverse, columns_other)


def combined(own, other, half_own, half_other):
    joined = jnp.concatenate([own, other], axis=1)
    halves = jnp.concatenate([half_own.astype(BF16), half_other.astype(BF16)], axis=1)
    return dot_nt(joined, halves).astype(BF16)


def choose(axis, first, second):
    odd = (lax.axis_index(axis) & 1) == 1
    return jnp.where(odd, second, first), jnp.where(odd, first, second)


def write_bulk(refs, modes, image_ref):
    modes_ref, outgoing_ref = refs
    modes_ref[...] = modes
    if image_ref is not None:
        outgoing_ref[...] = choose("tm", modes, image_ref[...])[0]
    else:
        part = outgoing_ref.shape[0]
        outgoing_ref[...] = choose("tm", modes[:part], modes[part:])[0]


def read_modes(came_ref, shared_ref, rows):
    first, second = choose("tm", came_ref[...], shared_ref[...])
    if first.shape[0] == rows:
        return first
    return jnp.concatenate([first, second], axis=0)


def first_merge_kernel(own_ref, other_ref, sketch_ref, halves_ref, slices_ref):
    width = own_ref.shape[1]
    own, other = own_ref[:width], other_ref[:width]
    even, odd = choose("tm", own, other)
    pair_gram = jnp.concatenate(choose("tm", own_ref[width:], other_ref[width:]), axis=0)
    cross = nt_full(nn_full(even, pair_gram), odd)
    cross_t = jnp.where(lax.axis_index("tm") % 2 == 1, cross, cross.T)
    half_own, half_other = merge(cross_t, sketch_ref)
    halves_ref[0] = half_own.astype(BF16)
    halves_ref[1] = half_other.astype(BF16)
    slices = choose("tm", nn_full(half_own, own), nn_full(half_other, other))
    slices_ref[:width] = slices[0]
    slices_ref[width:] = slices[1]


def write_probes(refs, slices, far_t, shared_t, image):
    probes_ref, second_ref, *image_ref = refs
    probes = jnp.concatenate(
        [dot_nn(far, image) for far in choose("tm", far_t[...], shared_t[...])], axis=0
    ).astype(BF16)
    probes_ref[...] = probes
    second_ref[...] = choose("tm", probes, slices)[0]
    if image_ref:
        image_ref[0][...] = image


def first_apply_kernel(slices_ref, image_own, image_other, far_t, shared_t, *refs):
    slices = slices_ref[...].astype(BF16)
    width = slices.shape[1]
    own, other = choose("tm", slices[:width], slices[width:])
    image = combined(image_own[...], image_other[...], own, other)
    write_probes(refs, slices, far_t, shared_t, image)


def pick_kernel(probes_ref, slices_ref, out_ref):
    out_ref[...] = choose("tm", probes_ref[...], slices_ref[...].astype(BF16))[0]


def first_modes_kernel(halves_ref, modes_own, modes_other, *refs):
    *image_ref, modes_ref, outgoing_ref = refs
    modes = combined(modes_own[...], modes_other[...], halves_ref[0], halves_ref[1])
    write_bulk((modes_ref, outgoing_ref), modes, image_ref[0] if image_ref else None)


def cross_of(total_rows, own_ref, one_ref, two_ref, shared_one, shared_two):
    first, second = choose("tm", one_ref[...], shared_one[...])
    third, slices = choose("tm", two_ref[...], shared_two[...])
    probes = (own_ref[...].astype(F32) + first.astype(F32)) + (
        second.astype(F32) + third.astype(F32)
    )
    high, low = split(probes / total_rows)
    width = slices.shape[1]
    left = jnp.concatenate([slices[:width], slices[width:]] * 2, axis=1)
    return dot_nn(left, jnp.concatenate([high, low], axis=0))


def write_coefficients(halves_ref, slices_ref, old_ref, half_own, half_other):
    halves_ref[0] = half_own.astype(BF16)
    halves_ref[1] = half_other.astype(BF16)
    width = old_ref.shape[1]
    slices_ref[:width] = nn_full(half_own, old_ref[:width])
    slices_ref[width:] = nn_full(half_own, old_ref[width:])


def near_merge_kernel(total_rows, *refs):
    *arrivals, sketch_ref, old_ref, halves_ref, slices_ref = refs
    half_own, half_other = merge(cross_of(total_rows, *arrivals), sketch_ref)
    write_coefficients(halves_ref, slices_ref, old_ref, half_own, half_other)


def merge_kernel(count, *refs):
    parts, (sketch_ref, old_ref, halves_ref, slices_ref) = refs[:count], refs[count:]
    half_own, half_other = merge(total_of(parts), sketch_ref)
    write_coefficients(halves_ref, slices_ref, old_ref, half_own, half_other)


def last_merge_kernel(count, *refs):
    parts, (sketch_ref, *kept, halves_ref, out_ref, sems) = refs[:count], refs[count:]
    copies = [
        pltpu.make_async_copy(modes_ref, out_ref.at[level], sems.at[level])
        for level, modes_ref in enumerate(kept)
    ]
    for copy in copies:
        copy.start()
    half_own, half_other = merge(total_of(parts), sketch_ref)
    halves_ref[0] = half_own.astype(BF16)
    halves_ref[1] = half_other.astype(BF16)
    for copy in copies:
        copy.wait()


def apply_kernel(halves_ref, slices_ref, image_own, came_ref, shared_ref, far_t, shared_t, *refs):
    image_other = choose("tm", came_ref[...], shared_ref[...])[1]
    image = combined(image_own[...], image_other, halves_ref[0], halves_ref[1])
    write_probes(refs, slices_ref[...].astype(BF16), far_t, shared_t, image)


def modes_kernel(halves_ref, modes_own, came_ref, shared_ref, *refs):
    *image_ref, modes_ref, outgoing_ref = refs
    modes_other = choose("tm", came_ref[...], shared_ref[...])[0]
    modes = combined(modes_own[...], modes_other, halves_ref[0], halves_ref[1])
    write_bulk((modes_ref, outgoing_ref), modes, image_ref[0] if image_ref else None)


def output_kernel(halves_ref, modes_own, came_ref, shared_ref, _, out_ref, modes_ref, sems):
    rows = modes_own.shape[0]
    modes_other = read_modes(came_ref, shared_ref, rows)
    part = rows // 2
    copies = []
    for half in range(2):
        span = slice(half * part, (half + 1) * part)
        modes_ref[span] = combined(
            modes_own[span], modes_other[span], halves_ref[0], halves_ref[1]
        )
        copies.append(
            pltpu.make_async_copy(
                modes_ref.at[pl.ds(half * part, part)],
                out_ref.at[out_ref.shape[0] - 1, pl.ds(half * part, part)],
                sems.at[half],
            )
        )
        copies[-1].start()
    for copy in copies:
        copy.wait()


def last_level(parts, sketch_t, kept, halves_shape):
    rows, width = kept[0].shape
    levels = len(kept)
    vmem = pl.BlockSpec(memory_space=pltpu.VMEM)
    hbm = pl.BlockSpec(memory_space=pltpu.HBM)
    return pl.pallas_call(
        functools.partial(last_merge_kernel, len(parts)),
        out_shape=[halves_shape, jax.ShapeDtypeStruct((levels + 1, rows, width), BF16)],
        in_specs=[vmem] * (len(parts) + 1 + levels),
        out_specs=[vmem, hbm],
        scratch_shapes=[pltpu.SemaphoreType.DMA((levels,))],
        compiler_params=PARAMS,
    )(*parts, sketch_t, *kept)


def last_modes(halves, modes, came, shared, out):
    vmem = pl.BlockSpec(memory_space=pltpu.VMEM)
    hbm = pl.BlockSpec(memory_space=pltpu.HBM)
    return pl.pallas_call(
        output_kernel,
        out_shape=jax.ShapeDtypeStruct(out.shape, BF16),
        in_specs=[vmem] * 4 + [hbm],
        out_specs=hbm,
        scratch_shapes=[pltpu.VMEM(modes.shape, BF16), pltpu.SemaphoreType.DMA((2,))],
        input_output_aliases={4: 0},
        compiler_params=PARAMS,
    )(halves, modes, came, shared, out)


def cross_kernel(total_rows, *refs):
    *arrivals, out_ref = refs
    out_ref[...] = cross_of(total_rows, *arrivals).astype(BF16)


def modes_of(snapshots, energy, neighbours, sketch):
    block_count, _, block_rows, _ = energy.shape
    rows_dev, width = snapshots.shape
    space = lax.axis_size("space")
    total_rows = rows_dev * space
    levels = sketch.shape[0]
    blocks = snapshots.reshape(block_count, block_rows, width)
    head, tail = blocks[:HB], blocks[block_count - HB :]
    odd = (lax.axis_index("space") & 1) == 1
    near = [(i, i ^ 1) for i in range(space)]
    wide = [(i, (i + 2 * (i % 2) - 1) % space) for i in range(space)]
    came_near = lax.ppermute(jnp.where(odd, head, tail), "space", near)
    came_wide = lax.ppermute(jnp.where(odd, tail, head), "space", wide)
    modes_shape = jax.ShapeDtypeStruct((rows_dev, width), BF16)
    half_shape = jax.ShapeDtypeStruct((rows_dev // 2, width), BF16)
    factor_shape = jax.ShapeDtypeStruct((width + width // 2, width), F32)
    half_square = jax.ShapeDtypeStruct((width, width), BF16)
    pair_square = jax.ShapeDtypeStruct((2 * width, width), BF16)
    slices_shape = jax.ShapeDtypeStruct((2 * width, width), F32)
    halves_shape = jax.ShapeDtypeStruct((2, width, width), BF16)

    inner, sketch_t, edges, blocks = interior_of(neighbours, energy, blocks, sketch)
    image, image_t, gram = edge_of(neighbours, edges, came_near, blocks, came_wide, inner)
    other_image = swap(image, "tm", 1)
    pair = run_kernel(
        pair_kernel,
        factor_shape, gram, image_t, other_image,
    )
    parts = summands(pair, "space", space, 4)
    far_images = [swap(image_t, "tm", 2**level) for level in range(1, levels)]
    factor = run_kernel(
        functools.partial(leaf_kernel, total_rows, len(parts)), factor_shape, *parts
    )
    other_factor = swap(factor, "tm", 1)
    modes = run_kernel(
        leaf_modes_kernel, modes_shape, blocks.reshape(rows_dev, width), factor
    )
    other = swap(modes, "tm", 1)
    kept = [modes]
    for level in range(levels):
        last = level + 1 == levels
        deep = level + 2 < levels
        probe_outs = [pair_square] * 2 + ([modes_shape] if deep else [])
        modes_outs = [modes_shape, modes_shape if deep else half_shape]
        if level > 0:
            quarter = space // 4
            if quarter > 1:
                parts = summands(probes, "space", quarter, 4)
                probes = run_kernel(add_kernel, pair_square, *parts)
                second = run_kernel(pick_kernel, pair_square, probes, slices)
            one = mixed_swap(probes, (0, quarter), (0, 2 * quarter))
            two = mixed_swap(second, (0, 3 * quarter), (2**level, 0))
            came = swap(outgoing, "tm", 2**level)
            shared = swap(came, "tm", 1)
            arrivals = [
                probes, one, two,
                swap(one, "tm", 1), swap(two, "tm", 1),
            ]
            if level > 1:
                cross = run_kernel(
                    functools.partial(cross_kernel, total_rows), half_square, *arrivals
                )
                parts = summands(cross, "tm", 2**level, 2, done=2)
        outs = [halves_shape, slices_shape]
        if level == 0:
            halves, slices = run_kernel(
                first_merge_kernel, outs, factor, other_factor, sketch_t[level]
            )
        elif last:
            halves, out = last_level(parts, sketch_t[level], kept, halves_shape)
        elif level == 1:
            halves, slices = run_kernel(
                functools.partial(near_merge_kernel, total_rows), outs,
                *arrivals, sketch_t[level], slices,
            )
        else:
            halves, slices = run_kernel(
                functools.partial(merge_kernel, len(parts)), outs,
                *parts, sketch_t[level], slices,
            )
        if last:
            out = last_modes(halves, modes, came, shared, out)
            break
        far = far_images[level]
        far_shared = swap(far, "tm", 1)
        if level == 0:
            probes, second, *image = run_kernel(
                first_apply_kernel, probe_outs,
                slices, image, other_image, far, far_shared,
            )
        else:
            probes, second, *image = run_kernel(
                apply_kernel, probe_outs,
                halves, slices, image[0], came, shared, far, far_shared,
            )
        if level == 0:
            modes, outgoing = run_kernel(
                first_modes_kernel, modes_outs, halves, modes, other, *image
            )
        else:
            modes, outgoing = run_kernel(
                modes_kernel, modes_outs, halves, modes, came, shared, *image
            )
        kept.append(modes)
    return out[:, None]


def solution(mesh):
    placed = (P("space", "tm"), P("space", None, None, None), P("space", None), P())
    return jax.shard_map(
        modes_of,
        mesh=mesh,
        in_specs=placed,
        out_specs=P(None, "tm", "space", None),
        check_vma=False,
    )
```

```python
import functools

import jax
import jax.numpy as jnp
from jax import lax
from jax.experimental import pallas as pl
from jax.experimental.pallas import tpu as pltpu
from jax.sharding import PartitionSpec as P


HB = 2
PANEL = 8
F32 = jnp.float32
BF16 = jnp.bfloat16
PARAMS = pltpu.CompilerParams(vmem_limit_bytes=16 * 1024 * 1024)


def swap(value, axis, mask):
    pairs = [(source, source ^ mask) for source in range(lax.axis_size(axis))]
    return lax.ppermute(value, axis, pairs)


def mixed_swap(value, even, odd):
    space = lax.axis_size("space")
    pairs = []
    for t in range(lax.axis_size("tm")):
        masks = odd if t % 2 else even
        for place in range(space):
            target = (t ^ masks[0]) * space + (place ^ masks[1])
            pairs.append((t * space + place, target))
    return lax.ppermute(value, ("tm", "space"), pairs)


def summands(value, axis, count, widest, done=1):
    parts = [value]
    while done < count:
        if len(parts) > 1:
            value = run_kernel(add_kernel, jax.ShapeDtypeStruct(value.shape, value.dtype), *parts)
        radix = 4 if widest == 4 and count // done % 4 == 0 else 2
        parts = [value]
        for step in range(1, radix):
            parts.append(swap(value, axis, step * done))
        done *= radix
    return parts


def add_kernel(*refs):
    refs[-1][...] = total_of(refs[:-1]).astype(refs[-1].dtype)


def total_of(parts):
    values = [part[...].astype(F32) for part in parts]
    while len(values) > 1:
        values = [a + b for a, b in zip(values[::2], values[1::2])]
    return values[0]


def dot_nn(a, b):
    return lax.dot_general(a, b, (((1,), (0,)), ((), ())), preferred_element_type=F32)


def dot_nt(a, b):
    return lax.dot_general(a, b, (((1,), (1,)), ((), ())), preferred_element_type=F32)


def split(value):
    high = value.astype(BF16)
    return high, (value - high.astype(F32)).astype(BF16)


def full(dot, axis, a, b):
    a_high, a_low = split(a)
    b_high, b_low = split(b)
    left = jnp.concatenate([a_high, a_high, a_low], axis=1)
    return dot(left, jnp.concatenate([b_high, b_low, b_high], axis=axis))


nn_full = functools.partial(full, dot_nn, 0)
nt_full = functools.partial(full, dot_nt, 1)


def inverse_factor(matrix, exact=False):
    size = matrix.shape[0]
    panels = size // PANEL
    shape = (PANEL, size)
    lane = lax.broadcasted_iota(jnp.int32, shape, 1)
    sub = lax.broadcasted_iota(jnp.int32, shape, 0)

    def column(rows, index):
        return jnp.broadcast_to(rows[:, index : index + 1], shape)

    def row(rows, index):
        return jnp.broadcast_to(rows[index : index + 1, :], shape)

    rows_of = [matrix[PANEL * i : PANEL * (i + 1), :] for i in range(panels)]
    zero = jnp.zeros(shape, F32)
    out = []
    block = [column(rows_of[0], j) for j in range(PANEL)]
    for k in range(panels):
        base = PANEL * k
        final = k + 1 == panels
        active = rows_of[k]
        here = (lane >= base) & (lane < base + PANEL)
        if not final:
            below = rows_of[k + 1]
            under = [column(below, base + j) for j in range(PANEL)]
            ahead = [column(active, base + PANEL + q) for q in range(PANEL)]
            following = [column(below, base + PANEL + q) for q in range(PANEL)]
            below = jnp.where(here, 0.0, below)
        active = jnp.where(here, jnp.where(lane == sub + base, 1.0, 0.0), active)
        kept = active
        pivots = block[0]
        for j in range(PANEL):
            pivot = row(block[j], j)
            inverse = 1.0 / pivot
            factor = jnp.where(sub == j, 0.0, block[j]) * inverse
            leading = row(active, j)
            kept = jnp.where(sub == j, active, kept)
            pivots = jnp.where(sub == j, pivot, pivots)
            active = active - factor * leading
            if not final:
                lower = under[j] * inverse
                below = below - lower * leading
            for q in range(j + 1, PANEL):
                item = row(block[q], j)
                block[q] = block[q] - factor * item
                if not final:
                    under[q] = under[q] - lower * item
            if not final:
                for q in range(PANEL):
                    item = row(ahead[q], j)
                    ahead[q] = ahead[q] - factor * item
                    following[q] = following[q] - lower * item
        out.append(jnp.where(lane < base + PANEL, kept * lax.rsqrt(pivots), 0.0))
        if final:
            break
        rows_of[k + 1] = below
        block = following
        if k + 2 < panels:
            solved = active * (1.0 / pivots)
            solved_rows = [row(solved, j) for j in range(PANEL)]
            for i in range(k + 2, panels if exact else k + 3):
                old = rows_of[i]
                new = jnp.where(here, 0.0, old)
                for j in range(PANEL):
                    new = new - column(old, base + j) * solved_rows[j]
                rows_of[i] = new
        if k + 3 < panels and not exact:
            rest = rows_of[k + 3 :]
            spread = jnp.concatenate([zero] * k + [solved] + [zero] * (panels - k - 1), axis=0)
            change = nn_full(jnp.concatenate(rest, axis=0), spread)
            for i, old in enumerate(rest):
                part = change[PANEL * i : PANEL * (i + 1)]
                rows_of[k + 3 + i] = jnp.where(here, 0.0, old) - part
    return jnp.concatenate(out, axis=0)


def run_kernel(body, outs, *operands):
    cost = pl.CostEstimate(flops=2_000_000_000, bytes_accessed=1_000_000, transcendentals=0)
    return pl.pallas_call(
        body, out_shape=outs, cost_estimate=cost, compiler_params=PARAMS
    )(*operands)


def coupled(energy_ref, place, slots, lookup):
    left = jnp.concatenate([energy_ref[place, slot] for slot in range(slots)], axis=1)
    right = jnp.concatenate([lookup(slot) for slot in range(slots)], axis=0)
    return dot_nn(left, right)


def interior_kernel(
    index_hbm, energy_hbm, blocks_hbm, sketch_hbm,
    image_ref, image_t_ref, gram_ref, sketch_out, edges_ref, blocks_ref,
    index_ref, energy_ref, sketch_ref, sems,
):
    count = blocks_ref.shape[0]
    inner, slots = energy_ref.shape[:2]
    width = sketch_out.shape[2]
    copies = [
        pltpu.make_async_copy(source, target, sems.at[place])
        for place, (source, target) in enumerate(
            [
                (index_hbm, index_ref),
                (blocks_hbm, blocks_ref),
                (energy_hbm.at[pl.ds(HB, inner)], energy_ref),
                (sketch_hbm, sketch_ref),
                (energy_hbm.at[pl.ds(0, HB)], edges_ref.at[0]),
                (energy_hbm.at[pl.ds(count - HB, HB)], edges_ref.at[1]),
            ]
        )
    ]
    for copy in copies:
        copy.start()
    first = lax.axis_index("space") * count
    window = lax.axis_index("tm")
    for copy in copies[:3]:
        copy.wait()
    for place in range(inner):
        b = HB + place
        value = 3.0 * blocks_ref[b].astype(F32) + coupled(
            energy_ref, place, slots, lambda slot: blocks_ref[index_ref[b, slot] - first]
        )
        image_ref[place] = value.astype(BF16)
    image = image_ref[...].reshape(image_t_ref.shape[1], image_t_ref.shape[0])
    image_t = image.T
    image_t_ref[...] = image_t
    gram_ref[...] = dot_nn(image_t, image)
    copies[3].wait()
    for level in range(sketch_ref.shape[0]):
        upper = window // 2**level % 2
        for half in range(2):
            start = pl.multiple_of((upper ^ half) * width, width)
            sketch_out[level, half] = sketch_ref[level, pl.ds(start, width), :].T
    for copy in copies[4:]:
        copy.wait()


def edge_kernel(
    index_ref, edges_ref, near_ref, blocks_ref, wide_ref, inner_ref, inner_t_ref, inner_gram_ref,
    image_ref, image_t_ref, gram_ref, padded_ref,
):
    slots = edges_ref.shape[2]
    blocks = blocks_ref.shape[0]
    before, after = choose("space", wide_ref[...], near_ref[...])
    padded_ref[0, :HB] = before
    padded_ref[0, HB:] = blocks_ref[: 2 * HB]
    padded_ref[1, : 2 * HB] = blocks_ref[blocks - 2 * HB :]
    padded_ref[1, 2 * HB :] = after
    image_ref[HB : blocks - HB] = inner_ref[...]
    width = gram_ref.shape[0]
    reach = HB * image_ref.shape[1]
    image_t_ref[:, reach : image_t_ref.shape[1] - reach] = inner_t_ref[...]
    gram = inner_gram_ref[...]
    for side in range(2):
        first = lax.axis_index("space") * blocks - HB + side * (blocks - HB)
        start = side * (blocks - HB)
        for place in range(HB):
            b = start + place
            value = 3.0 * blocks_ref[b].astype(F32) + coupled(
                edges_ref.at[side], place, slots,
                lambda slot: padded_ref[side, index_ref[b, slot] - first],
            )
            image_ref[b] = value.astype(BF16)
        image = image_ref[start : start + HB].reshape(reach, width)
        image_t = image.T
        offset = start * image_ref.shape[1]
        image_t_ref[:, offset : offset + reach] = image_t
        gram = gram + dot_nn(image_t, image)
    gram_ref[...] = gram


def interior_of(neighbours, energy, blocks, sketch):
    count, slots, rows, _ = energy.shape
    width = blocks.shape[2]
    levels = sketch.shape[0]
    inner = count - 2 * HB
    return pl.pallas_call(
        interior_kernel,
        out_shape=[
            jax.ShapeDtypeStruct((inner, rows, width), BF16),
            jax.ShapeDtypeStruct((width, inner * rows), BF16),
            jax.ShapeDtypeStruct((width, width), F32),
            jax.ShapeDtypeStruct((levels, 2, width, width), F32),
            jax.ShapeDtypeStruct((2, HB, slots, rows, rows), BF16),
            jax.ShapeDtypeStruct(blocks.shape, BF16),
        ],
        in_specs=[pl.BlockSpec(memory_space=pltpu.HBM)] * 4,
        scratch_shapes=[
            pltpu.SMEM(neighbours.shape, jnp.int32),
            pltpu.VMEM((inner, slots, rows, rows), BF16),
            pltpu.VMEM(sketch.shape, F32),
            pltpu.SemaphoreType.DMA((6,)),
        ],
        compiler_params=PARAMS,
    )(*[pltpu.with_memory_space_constraint(item, pltpu.HBM) for item in (neighbours, energy, blocks, sketch)])


def edge_of(neighbours, edges, came_near, blocks, came_wide, *inner):
    count, rows, width = blocks.shape
    image, image_t, gram = pl.pallas_call(
        edge_kernel,
        out_shape=[
            jax.ShapeDtypeStruct((count, rows, width), BF16),
            jax.ShapeDtypeStruct((width, count * rows), BF16),
            jax.ShapeDtypeStruct((width, width), F32),
        ],
        in_specs=[pl.BlockSpec(memory_space=pltpu.SMEM)]
        + [pl.BlockSpec(memory_space=pltpu.VMEM)] * 7,
        scratch_shapes=[pltpu.VMEM((2, 3 * HB, rows, width), BF16)],
        compiler_params=PARAMS,
    )(neighbours, edges, came_near, blocks, came_wide, *inner)
    return image.reshape(count * rows, width), image_t, gram


def pair_kernel(gram_ref, image_t_ref, other_ref, out_ref):
    width = gram_ref.shape[0]
    out_ref[:width] = gram_ref[...]
    cross = dot_nn(image_t_ref[...], other_ref[...])
    odd = lax.axis_index("tm") % 2 == 1
    out_ref[width:] = jnp.where(odd, cross.T[width // 2 :], cross[: width // 2])


def leaf_kernel(total_rows, count, *refs):
    parts, (factor_ref,) = refs[:count], refs[count:]
    width = factor_ref.shape[1]
    grams = total_of(parts) / total_rows
    factor_ref[width:] = grams[width:]
    inverse = inverse_factor(grams[:width], exact=True)
    factor_ref[:width] = inverse


def leaf_modes_kernel(snapshots_ref, factor_ref, modes_ref):
    inverse = factor_ref[: factor_ref.shape[1]]
    modes_ref[...] = dot_nt(snapshots_ref[...], inverse.astype(BF16)).astype(BF16)


def merge(cross_t, sketch_ref):
    sketch_own, sketch_other = sketch_ref[0], sketch_ref[1]
    columns_own = sketch_own + nn_full(sketch_other, cross_t)
    columns_other = nt_full(sketch_own, cross_t) + sketch_other
    image_own = columns_own + nn_full(columns_other, cross_t)
    image_other = nt_full(columns_own, cross_t) + columns_other
    inner = nt_full(
        jnp.concatenate([columns_own, columns_other], axis=1),
        jnp.concatenate([image_own, image_other], axis=1),
    )
    inverse = inverse_factor(inner)
    return nn_full(inverse, columns_own), nn_full(inverse, columns_other)


def combined(own, other, half_own, half_other):
    joined = jnp.concatenate([own, other], axis=1)
    halves = jnp.concatenate([half_own.astype(BF16), half_other.astype(BF16)], axis=1)
    return dot_nt(joined, halves).astype(BF16)


def choose(axis, first, second):
    odd = (lax.axis_index(axis) & 1) == 1
    return jnp.where(odd, second, first), jnp.where(odd, first, second)


def write_bulk(refs, modes, image_ref):
    modes_ref, outgoing_ref = refs
    modes_ref[...] = modes
    if image_ref is not None:
        outgoing_ref[...] = choose("tm", modes, image_ref[...])[0]
    else:
        part = outgoing_ref.shape[0]
        outgoing_ref[...] = choose("tm", modes[:part], modes[part:])[0]


def first_merge_kernel(own_ref, other_ref, sketch_ref, halves_ref, slices_ref):
    width = own_ref.shape[1]
    own, other = own_ref[:width], other_ref[:width]
    even, odd = choose("tm", own, other)
    pair_gram = jnp.concatenate(choose("tm", own_ref[width:], other_ref[width:]), axis=0)
    cross = nt_full(nn_full(even, pair_gram), odd)
    cross_t = jnp.where(lax.axis_index("tm") % 2 == 1, cross, cross.T)
    half_own, half_other = merge(cross_t, sketch_ref)
    halves_ref[0] = half_own.astype(BF16)
    halves_ref[1] = half_other.astype(BF16)
    slices = choose("tm", nn_full(half_own, own), nn_full(half_other, other))
    slices_ref[:width] = slices[0]
    slices_ref[width:] = slices[1]


def write_probes(refs, slices, far_t, shared_t, image):
    probes_ref, second_ref, *image_ref = refs
    probes = jnp.concatenate(
        [dot_nn(far, image) for far in choose("tm", far_t[...], shared_t[...])], axis=0
    ).astype(BF16)
    probes_ref[...] = probes
    second_ref[...] = choose("tm", probes, slices)[0]
    if image_ref:
        image_ref[0][...] = image


def first_apply_kernel(slices_ref, image_own, image_other, far_t, shared_t, *refs):
    slices = slices_ref[...].astype(BF16)
    width = slices.shape[1]
    own, other = choose("tm", slices[:width], slices[width:])
    image = combined(image_own[...], image_other[...], own, other)
    write_probes(refs, slices, far_t, shared_t, image)


def pick_kernel(probes_ref, slices_ref, out_ref):
    out_ref[...] = choose("tm", probes_ref[...], slices_ref[...].astype(BF16))[0]


def first_modes_kernel(halves_ref, modes_own, modes_other, *refs):
    *image_ref, modes_ref, outgoing_ref = refs
    modes = combined(modes_own[...], modes_other[...], halves_ref[0], halves_ref[1])
    write_bulk((modes_ref, outgoing_ref), modes, image_ref[0] if image_ref else None)


def cross_of(total_rows, own_ref, one_ref, two_ref, shared_one, shared_two):
    first, second = choose("tm", one_ref[...], shared_one[...])
    third, slices = choose("tm", two_ref[...], shared_two[...])
    probes = (own_ref[...].astype(F32) + first.astype(F32)) + (
        second.astype(F32) + third.astype(F32)
    )
    high, low = split(probes / total_rows)
    width = slices.shape[1]
    left = jnp.concatenate([slices[:width], slices[width:]] * 2, axis=1)
    return dot_nn(left, jnp.concatenate([high, low], axis=0))


def write_coefficients(halves_ref, slices_ref, old_ref, half_own, half_other):
    halves_ref[0] = half_own.astype(BF16)
    halves_ref[1] = half_other.astype(BF16)
    width = old_ref.shape[1]
    slices_ref[:width] = nn_full(half_own, old_ref[:width])
    slices_ref[width:] = nn_full(half_own, old_ref[width:])


def near_merge_kernel(total_rows, *refs):
    *arrivals, sketch_ref, old_ref, halves_ref, slices_ref = refs
    half_own, half_other = merge(cross_of(total_rows, *arrivals), sketch_ref)
    write_coefficients(halves_ref, slices_ref, old_ref, half_own, half_other)


def merge_kernel(count, *refs):
    parts, (sketch_ref, old_ref, halves_ref, slices_ref) = refs[:count], refs[count:]
    half_own, half_other = merge(total_of(parts), sketch_ref)
    write_coefficients(halves_ref, slices_ref, old_ref, half_own, half_other)


def last_merge_kernel(count, *refs):
    parts, (sketch_ref, *kept, halves_ref, out_ref, sems) = refs[:count], refs[count:]
    copies = [
        pltpu.make_async_copy(modes_ref, out_ref.at[level], sems.at[level])
        for level, modes_ref in enumerate(kept)
    ]
    for copy in copies:
        copy.start()
    half_own, half_other = merge(total_of(parts), sketch_ref)
    halves_ref[0] = half_own.astype(BF16)
    halves_ref[1] = half_other.astype(BF16)
    for copy in copies:
        copy.wait()


def apply_kernel(halves_ref, slices_ref, image_own, came_ref, shared_ref, far_t, shared_t, *refs):
    image_other = choose("tm", came_ref[...], shared_ref[...])[1]
    image = combined(image_own[...], image_other, halves_ref[0], halves_ref[1])
    write_probes(refs, slices_ref[...].astype(BF16), far_t, shared_t, image)


def modes_kernel(halves_ref, modes_own, came_ref, shared_ref, *refs):
    *image_ref, modes_ref, outgoing_ref = refs
    modes_other = choose("tm", came_ref[...], shared_ref[...])[0]
    modes = combined(modes_own[...], modes_other, halves_ref[0], halves_ref[1])
    write_bulk((modes_ref, outgoing_ref), modes, image_ref[0] if image_ref else None)


def output_kernel(side, halves_ref, modes_own, modes_other, _, out_ref, modes_ref, sem):
    part = modes_other.shape[0]
    start = pl.multiple_of((lax.axis_index("tm") + side) % 2 * part, part)
    modes_ref[...] = combined(
        modes_own[pl.ds(start, part)], modes_other[...], halves_ref[0], halves_ref[1]
    )
    copy = pltpu.make_async_copy(
        modes_ref, out_ref.at[out_ref.shape[0] - 1, pl.ds(start, part)], sem
    )
    copy.start()
    copy.wait()


def last_level(parts, sketch_t, kept, halves_shape):
    rows, width = kept[0].shape
    levels = len(kept)
    vmem = pl.BlockSpec(memory_space=pltpu.VMEM)
    hbm = pl.BlockSpec(memory_space=pltpu.HBM)
    return pl.pallas_call(
        functools.partial(last_merge_kernel, len(parts)),
        out_shape=[halves_shape, jax.ShapeDtypeStruct((levels + 1, rows, width), BF16)],
        in_specs=[vmem] * (len(parts) + 1 + levels),
        out_specs=[vmem, hbm],
        scratch_shapes=[pltpu.SemaphoreType.DMA((levels,))],
        compiler_params=PARAMS,
    )(*parts, sketch_t, *kept)


def last_modes(side, halves, modes, came, out):
    vmem = pl.BlockSpec(memory_space=pltpu.VMEM)
    hbm = pl.BlockSpec(memory_space=pltpu.HBM)
    return pl.pallas_call(
        functools.partial(output_kernel, side),
        out_shape=jax.ShapeDtypeStruct(out.shape, BF16),
        in_specs=[vmem] * 3 + [hbm],
        out_specs=hbm,
        scratch_shapes=[pltpu.VMEM(came.shape, BF16), pltpu.SemaphoreType.DMA],
        input_output_aliases={3: 0},
        compiler_params=PARAMS,
    )(halves, modes, came, out)


def cross_kernel(total_rows, *refs):
    *arrivals, out_ref = refs
    out_ref[...] = cross_of(total_rows, *arrivals).astype(BF16)


def modes_of(snapshots, energy, neighbours, sketch):
    block_count, _, block_rows, _ = energy.shape
    rows_dev, width = snapshots.shape
    space = lax.axis_size("space")
    total_rows = rows_dev * space
    levels = sketch.shape[0]
    blocks = snapshots.reshape(block_count, block_rows, width)
    head, tail = blocks[:HB], blocks[block_count - HB :]
    odd = (lax.axis_index("space") & 1) == 1
    near = [(i, i ^ 1) for i in range(space)]
    wide = [(i, (i + 2 * (i % 2) - 1) % space) for i in range(space)]
    came_near = lax.ppermute(jnp.where(odd, head, tail), "space", near)
    came_wide = lax.ppermute(jnp.where(odd, tail, head), "space", wide)
    modes_shape = jax.ShapeDtypeStruct((rows_dev, width), BF16)
    half_shape = jax.ShapeDtypeStruct((rows_dev // 2, width), BF16)
    factor_shape = jax.ShapeDtypeStruct((width + width // 2, width), F32)
    half_square = jax.ShapeDtypeStruct((width, width), BF16)
    pair_square = jax.ShapeDtypeStruct((2 * width, width), BF16)
    slices_shape = jax.ShapeDtypeStruct((2 * width, width), F32)
    halves_shape = jax.ShapeDtypeStruct((2, width, width), BF16)

    *inner, sketch_t, edges, blocks = interior_of(neighbours, energy, blocks, sketch)
    image, image_t, gram = edge_of(neighbours, edges, came_near, blocks, came_wide, *inner)
    other_image = swap(image, "tm", 1)
    pair = run_kernel(
        pair_kernel,
        factor_shape, gram, image_t, other_image,
    )
    parts = summands(pair, "space", space, 4)
    far_images = [swap(image_t, "tm", 2**level) for level in range(1, levels)]
    factor = run_kernel(
        functools.partial(leaf_kernel, total_rows, len(parts)), factor_shape, *parts
    )
    other_factor = swap(factor, "tm", 1)
    modes = run_kernel(
        leaf_modes_kernel, modes_shape, blocks.reshape(rows_dev, width), factor
    )
    other = swap(modes, "tm", 1)
    kept = [modes]
    for level in range(levels):
        last = level + 1 == levels
        deep = level + 2 < levels
        probe_outs = [pair_square] * 2 + ([modes_shape] if deep else [])
        modes_outs = [modes_shape, modes_shape if deep else half_shape]
        if level > 0:
            quarter = space // 4
            if quarter > 1:
                parts = summands(probes, "space", quarter, 4)
                probes = run_kernel(add_kernel, pair_square, *parts)
                second = run_kernel(pick_kernel, pair_square, probes, slices)
            one = mixed_swap(probes, (0, quarter), (0, 2 * quarter))
            two = mixed_swap(second, (0, 3 * quarter), (2**level, 0))
            came = swap(outgoing, "tm", 2**level)
            shared = swap(came, "tm", 1)
            arrivals = [
                probes, one, two,
                swap(one, "tm", 1), swap(two, "tm", 1),
            ]
            if level > 1:
                cross = run_kernel(
                    functools.partial(cross_kernel, total_rows), half_square, *arrivals
                )
                parts = summands(cross, "tm", 2**level, 2, done=2)
        outs = [halves_shape, slices_shape]
        if level == 0:
            halves, slices = run_kernel(
                first_merge_kernel, outs, factor, other_factor, sketch_t[level]
            )
        elif last:
            halves, out = last_level(parts, sketch_t[level], kept, halves_shape)
        elif level == 1:
            halves, slices = run_kernel(
                functools.partial(near_merge_kernel, total_rows), outs,
                *arrivals, sketch_t[level], slices,
            )
        else:
            halves, slices = run_kernel(
                functools.partial(merge_kernel, len(parts)), outs,
                *parts, sketch_t[level], slices,
            )
        if last:
            out = last_modes(0, halves, modes, came, out)
            out = last_modes(1, halves, modes, shared, out)
            break
        far = far_images[level]
        far_shared = swap(far, "tm", 1)
        if level == 0:
            probes, second, *image = run_kernel(
                first_apply_kernel, probe_outs,
                slices, image, other_image, far, far_shared,
            )
        else:
            probes, second, *image = run_kernel(
                apply_kernel, probe_outs,
                halves, slices, image[0], came, shared, far, far_shared,
            )
        if level == 0:
            modes, outgoing = run_kernel(
                first_modes_kernel, modes_outs, halves, modes, other, *image
            )
        else:
            modes, outgoing = run_kernel(
                modes_kernel, modes_outs, halves, modes, came, shared, *image
            )
        kept.append(modes)
    return out[:, None]


def solution(mesh):
    placed = (P("space", "tm"), P("space", None, None, None), P("space", None), P())
    return jax.shard_map(
        modes_of,
        mesh=mesh,
        in_specs=placed,
        out_specs=P(None, "tm", "space", None),
        check_vma=False,
    )
```

```python
import functools

import jax
import jax.numpy as jnp
from jax import lax
from jax.experimental import pallas as pl
from jax.experimental.pallas import tpu as pltpu
from jax.sharding import PartitionSpec as P


HB = 2
PANEL = 8
F32 = jnp.float32
BF16 = jnp.bfloat16
PARAMS = pltpu.CompilerParams(vmem_limit_bytes=16 * 1024 * 1024)


def swap(value, axis, mask):
    pairs = [(source, source ^ mask) for source in range(lax.axis_size(axis))]
    return lax.ppermute(value, axis, pairs)


def mixed_swap(value, even, odd):
    space = lax.axis_size("space")
    pairs = []
    for t in range(lax.axis_size("tm")):
        masks = odd if t % 2 else even
        for place in range(space):
            target = (t ^ masks[0]) * space + (place ^ masks[1])
            pairs.append((t * space + place, target))
    return lax.ppermute(value, ("tm", "space"), pairs)


def summands(value, axis, count, widest, done=1):
    parts = [value]
    while done < count:
        if len(parts) > 1:
            value = run_kernel(add_kernel, jax.ShapeDtypeStruct(value.shape, value.dtype), *parts)
        radix = 4 if widest == 4 and count // done % 4 == 0 else 2
        parts = [value]
        for step in range(1, radix):
            parts.append(swap(value, axis, step * done))
        done *= radix
    return parts


def add_kernel(*refs):
    refs[-1][...] = total_of(refs[:-1]).astype(refs[-1].dtype)


def total_of(parts):
    values = [part[...].astype(F32) for part in parts]
    while len(values) > 1:
        values = [a + b for a, b in zip(values[::2], values[1::2])]
    return values[0]


def dot_nn(a, b):
    return lax.dot_general(a, b, (((1,), (0,)), ((), ())), preferred_element_type=F32)


def dot_nt(a, b):
    return lax.dot_general(a, b, (((1,), (1,)), ((), ())), preferred_element_type=F32)


def split(value):
    high = value.astype(BF16)
    return high, (value - high.astype(F32)).astype(BF16)


def full(dot, axis, a, b):
    a_high, a_low = split(a)
    b_high, b_low = split(b)
    left = jnp.concatenate([a_high, a_high, a_low], axis=1)
    return dot(left, jnp.concatenate([b_high, b_low, b_high], axis=axis))


nn_full = functools.partial(full, dot_nn, 0)
nt_full = functools.partial(full, dot_nt, 1)


def inverse_factor(matrix, exact=False):
    size = matrix.shape[0]
    panels = size // PANEL
    shape = (PANEL, size)
    lane = lax.broadcasted_iota(jnp.int32, shape, 1)
    sub = lax.broadcasted_iota(jnp.int32, shape, 0)

    def column(rows, index):
        return jnp.broadcast_to(rows[:, index : index + 1], shape)

    def row(rows, index):
        return jnp.broadcast_to(rows[index : index + 1, :], shape)

    rows_of = [matrix[PANEL * i : PANEL * (i + 1), :] for i in range(panels)]
    zero = jnp.zeros(shape, F32)
    out = []
    block = [column(rows_of[0], j) for j in range(PANEL)]
    for k in range(panels):
        base = PANEL * k
        final = k + 1 == panels
        active = rows_of[k]
        here = (lane >= base) & (lane < base + PANEL)
        if not final:
            below = rows_of[k + 1]
            under = [column(below, base + j) for j in range(PANEL)]
            ahead = [column(active, base + PANEL + q) for q in range(PANEL)]
            following = [column(below, base + PANEL + q) for q in range(PANEL)]
            below = jnp.where(here, 0.0, below)
        active = jnp.where(here, jnp.where(lane == sub + base, 1.0, 0.0), active)
        kept = active
        pivots = block[0]
        for j in range(PANEL):
            pivot = row(block[j], j)
            inverse = 1.0 / pivot
            factor = jnp.where(sub == j, 0.0, block[j]) * inverse
            leading = row(active, j)
            kept = jnp.where(sub == j, active, kept)
            pivots = jnp.where(sub == j, pivot, pivots)
            active = active - factor * leading
            if not final:
                lower = under[j] * inverse
                below = below - lower * leading
            for q in range(j + 1, PANEL):
                item = row(block[q], j)
                block[q] = block[q] - factor * item
                if not final:
                    under[q] = under[q] - lower * item
            if not final:
                for q in range(PANEL):
                    item = row(ahead[q], j)
                    ahead[q] = ahead[q] - factor * item
                    following[q] = following[q] - lower * item
        out.append(jnp.where(lane < base + PANEL, kept * lax.rsqrt(pivots), 0.0))
        if final:
            break
        rows_of[k + 1] = below
        block = following
        if k + 2 < panels:
            solved = active * (1.0 / pivots)
            solved_rows = [row(solved, j) for j in range(PANEL)]
            for i in range(k + 2, panels if exact else k + 3):
                old = rows_of[i]
                new = jnp.where(here, 0.0, old)
                for j in range(PANEL):
                    new = new - column(old, base + j) * solved_rows[j]
                rows_of[i] = new
        if k + 3 < panels and not exact:
            rest = rows_of[k + 3 :]
            spread = jnp.concatenate([zero] * k + [solved] + [zero] * (panels - k - 1), axis=0)
            change = nn_full(jnp.concatenate(rest, axis=0), spread)
            for i, old in enumerate(rest):
                part = change[PANEL * i : PANEL * (i + 1)]
                rows_of[k + 3 + i] = jnp.where(here, 0.0, old) - part
    return jnp.concatenate(out, axis=0)


def run_kernel(body, outs, *operands):
    cost = pl.CostEstimate(flops=2_000_000_000, bytes_accessed=1_000_000, transcendentals=0)
    return pl.pallas_call(
        body, out_shape=outs, cost_estimate=cost, compiler_params=PARAMS
    )(*operands)


def coupled(energy_ref, place, slots, lookup):
    left = jnp.concatenate([energy_ref[place, slot] for slot in range(slots)], axis=1)
    right = jnp.concatenate([lookup(slot) for slot in range(slots)], axis=0)
    return dot_nn(left, right)


def interior_kernel(
    index_hbm, energy_hbm, blocks_hbm, sketch_hbm,
    image_ref, sketch_out, edges_ref, blocks_ref, index_ref, energy_ref, sketch_ref, sems,
):
    count = blocks_ref.shape[0]
    inner, slots = energy_ref.shape[:2]
    width = sketch_out.shape[2]
    copies = [
        pltpu.make_async_copy(source, target, sems.at[place])
        for place, (source, target) in enumerate(
            [
                (index_hbm, index_ref),
                (blocks_hbm, blocks_ref),
                (energy_hbm.at[pl.ds(HB, inner)], energy_ref),
                (sketch_hbm, sketch_ref),
                (energy_hbm.at[pl.ds(0, HB)], edges_ref.at[0]),
                (energy_hbm.at[pl.ds(count - HB, HB)], edges_ref.at[1]),
            ]
        )
    ]
    for copy in copies:
        copy.start()
    first = lax.axis_index("space") * count
    window = lax.axis_index("tm")
    for copy in copies[:3]:
        copy.wait()
    for place in range(inner):
        b = HB + place
        value = 3.0 * blocks_ref[b].astype(F32) + coupled(
            energy_ref, place, slots, lambda slot: blocks_ref[index_ref[b, slot] - first]
        )
        image_ref[place] = value.astype(BF16)
    copies[3].wait()
    for level in range(sketch_ref.shape[0]):
        upper = window // 2**level % 2
        for half in range(2):
            start = pl.multiple_of((upper ^ half) * width, width)
            sketch_out[level, half] = sketch_ref[level, pl.ds(start, width), :].T
    for copy in copies[4:]:
        copy.wait()


def edge_kernel(
    index_ref, edges_ref, near_ref, blocks_ref, wide_ref, inner_ref,
    image_ref, image_t_ref, gram_ref, padded_ref,
):
    slots = edges_ref.shape[2]
    blocks = blocks_ref.shape[0]
    before, after = choose("space", wide_ref[...], near_ref[...])
    padded_ref[0, :HB] = before
    padded_ref[0, HB:] = blocks_ref[: 2 * HB]
    padded_ref[1, : 2 * HB] = blocks_ref[blocks - 2 * HB :]
    padded_ref[1, 2 * HB :] = after
    image_ref[HB : blocks - HB] = inner_ref[...]
    for side in range(2):
        first = lax.axis_index("space") * blocks - HB + side * (blocks - HB)
        for place in range(HB):
            b = side * (blocks - HB) + place
            value = 3.0 * blocks_ref[b].astype(F32) + coupled(
                edges_ref.at[side], place, slots,
                lambda slot: padded_ref[side, index_ref[b, slot] - first],
            )
            image_ref[b] = value.astype(BF16)
    image = image_ref[...].reshape(image_t_ref.shape[1], image_t_ref.shape[0])
    image_t = image.T
    image_t_ref[...] = image_t
    gram_ref[...] = dot_nn(image_t, image)


def interior_of(neighbours, energy, blocks, sketch):
    count, slots, rows, _ = energy.shape
    width = blocks.shape[2]
    levels = sketch.shape[0]
    inner = count - 2 * HB
    return pl.pallas_call(
        interior_kernel,
        out_shape=[
            jax.ShapeDtypeStruct((inner, rows, width), BF16),
            jax.ShapeDtypeStruct((levels, 2, width, width), F32),
            jax.ShapeDtypeStruct((2, HB, slots, rows, rows), BF16),
            jax.ShapeDtypeStruct(blocks.shape, BF16),
        ],
        in_specs=[pl.BlockSpec(memory_space=pltpu.HBM)] * 4,
        scratch_shapes=[
            pltpu.SMEM(neighbours.shape, jnp.int32),
            pltpu.VMEM((inner, slots, rows, rows), BF16),
            pltpu.VMEM(sketch.shape, F32),
            pltpu.SemaphoreType.DMA((6,)),
        ],
        compiler_params=PARAMS,
    )(*[pltpu.with_memory_space_constraint(item, pltpu.HBM) for item in (neighbours, energy, blocks, sketch)])


def edge_of(neighbours, edges, came_near, blocks, came_wide, inner):
    count, rows, width = blocks.shape
    image, image_t, gram = pl.pallas_call(
        edge_kernel,
        out_shape=[
            jax.ShapeDtypeStruct((count, rows, width), BF16),
            jax.ShapeDtypeStruct((width, count * rows), BF16),
            jax.ShapeDtypeStruct((width, width), F32),
        ],
        in_specs=[pl.BlockSpec(memory_space=pltpu.SMEM)]
        + [pl.BlockSpec(memory_space=pltpu.VMEM)] * 5,
        scratch_shapes=[pltpu.VMEM((2, 3 * HB, rows, width), BF16)],
        compiler_params=PARAMS,
    )(neighbours, edges, came_near, blocks, came_wide, inner)
    return image.reshape(count * rows, width), image_t, gram


def pair_kernel(gram_ref, image_t_ref, other_ref, out_ref):
    width = gram_ref.shape[0]
    out_ref[:width] = gram_ref[...]
    cross = dot_nn(image_t_ref[...], other_ref[...])
    odd = lax.axis_index("tm") % 2 == 1
    out_ref[width:] = jnp.where(odd, cross.T[width // 2 :], cross[: width // 2])


def leaf_kernel(total_rows, count, *refs):
    parts, (factor_ref,) = refs[:count], refs[count:]
    width = factor_ref.shape[1]
    grams = total_of(parts) / total_rows
    factor_ref[width:] = grams[width:]
    inverse = inverse_factor(grams[:width], exact=True)
    factor_ref[:width] = inverse


def leaf_modes_kernel(snapshots_ref, factor_ref, modes_ref):
    inverse = factor_ref[: factor_ref.shape[1]]
    modes_ref[...] = dot_nt(snapshots_ref[...], inverse.astype(BF16)).astype(BF16)


def merge(cross_t, sketch_ref):
    sketch_own, sketch_other = sketch_ref[0], sketch_ref[1]
    columns_own = sketch_own + nn_full(sketch_other, cross_t)
    columns_other = nt_full(sketch_own, cross_t) + sketch_other
    image_own = columns_own + nn_full(columns_other, cross_t)
    image_other = nt_full(columns_own, cross_t) + columns_other
    inner = nt_full(
        jnp.concatenate([columns_own, columns_other], axis=1),
        jnp.concatenate([image_own, image_other], axis=1),
    )
    inverse = inverse_factor(inner)
    return nn_full(inverse, columns_own), nn_full(inverse, columns_other)


def combined(own, other, half_own, half_other):
    joined = jnp.concatenate([own, other], axis=1)
    halves = jnp.concatenate([half_own.astype(BF16), half_other.astype(BF16)], axis=1)
    return dot_nt(joined, halves).astype(BF16)


def choose(axis, first, second):
    odd = (lax.axis_index(axis) & 1) == 1
    return jnp.where(odd, second, first), jnp.where(odd, first, second)


def write_bulk(refs, modes, image_ref):
    modes_ref, outgoing_ref = refs
    modes_ref[...] = modes
    if image_ref is not None:
        outgoing_ref[...] = choose("tm", modes, image_ref[...])[0]
    else:
        part = outgoing_ref.shape[0]
        half = jnp.where(upper_chip(), modes[2 * part :], modes[: 2 * part])
        outgoing_ref[...] = choose("tm", half[:part], half[part:])[0]


def upper_chip():
    return (lax.axis_index("tm") & 2) == 2


def read_modes(came_ref, shared_ref, far_ref, far_shared_ref):
    near = jnp.concatenate(choose("tm", came_ref[...], shared_ref[...]), axis=0)
    far = jnp.concatenate(choose("tm", far_ref[...], far_shared_ref[...]), axis=0)
    upper = upper_chip()
    return jnp.concatenate([jnp.where(upper, far, near), jnp.where(upper, near, far)], axis=0)


def first_merge_kernel(own_ref, other_ref, sketch_ref, halves_ref, slices_ref):
    width = own_ref.shape[1]
    own, other = own_ref[:width], other_ref[:width]
    even, odd = choose("tm", own, other)
    pair_gram = jnp.concatenate(choose("tm", own_ref[width:], other_ref[width:]), axis=0)
    cross = nt_full(nn_full(even, pair_gram), odd)
    cross_t = jnp.where(lax.axis_index("tm") % 2 == 1, cross, cross.T)
    half_own, half_other = merge(cross_t, sketch_ref)
    halves_ref[0] = half_own.astype(BF16)
    halves_ref[1] = half_other.astype(BF16)
    slices = choose("tm", nn_full(half_own, own), nn_full(half_other, other))
    slices_ref[:width] = slices[0]
    slices_ref[width:] = slices[1]


def write_probes(refs, slices, far_t, shared_t, image):
    probes_ref, second_ref, *image_ref = refs
    probes = jnp.concatenate(
        [dot_nn(far, image) for far in choose("tm", far_t[...], shared_t[...])], axis=0
    ).astype(BF16)
    probes_ref[...] = probes
    second_ref[...] = choose("tm", probes, slices)[0]
    if image_ref:
        image_ref[0][...] = image


def first_apply_kernel(slices_ref, image_own, image_other, far_t, shared_t, *refs):
    slices = slices_ref[...].astype(BF16)
    width = slices.shape[1]
    own, other = choose("tm", slices[:width], slices[width:])
    image = combined(image_own[...], image_other[...], own, other)
    write_probes(refs, slices, far_t, shared_t, image)


def pick_kernel(probes_ref, slices_ref, out_ref):
    out_ref[...] = choose("tm", probes_ref[...], slices_ref[...].astype(BF16))[0]


def first_modes_kernel(halves_ref, modes_own, modes_other, *refs):
    *image_ref, modes_ref, outgoing_ref = refs
    modes = combined(modes_own[...], modes_other[...], halves_ref[0], halves_ref[1])
    write_bulk((modes_ref, outgoing_ref), modes, image_ref[0] if image_ref else None)


def cross_of(total_rows, own_ref, one_ref, two_ref, shared_one, shared_two):
    first, second = choose("tm", one_ref[...], shared_one[...])
    third, slices = choose("tm", two_ref[...], shared_two[...])
    probes = (own_ref[...].astype(F32) + first.astype(F32)) + (
        second.astype(F32) + third.astype(F32)
    )
    high, low = split(probes / total_rows)
    width = slices.shape[1]
    left = jnp.concatenate([slices[:width], slices[width:]] * 2, axis=1)
    return dot_nn(left, jnp.concatenate([high, low], axis=0))


def write_coefficients(halves_ref, slices_ref, old_ref, half_own, half_other):
    halves_ref[0] = half_own.astype(BF16)
    halves_ref[1] = half_other.astype(BF16)
    width = old_ref.shape[1]
    slices_ref[:width] = nn_full(half_own, old_ref[:width])
    slices_ref[width:] = nn_full(half_own, old_ref[width:])


def near_merge_kernel(total_rows, *refs):
    *arrivals, sketch_ref, old_ref, halves_ref, slices_ref = refs
    half_own, half_other = merge(cross_of(total_rows, *arrivals), sketch_ref)
    write_coefficients(halves_ref, slices_ref, old_ref, half_own, half_other)


def merge_kernel(count, *refs):
    parts, (sketch_ref, old_ref, halves_ref, slices_ref) = refs[:count], refs[count:]
    half_own, half_other = merge(total_of(parts), sketch_ref)
    write_coefficients(halves_ref, slices_ref, old_ref, half_own, half_other)


def last_merge_kernel(count, *refs):
    parts, (sketch_ref, *kept, halves_ref, out_ref, sems) = refs[:count], refs[count:]
    copies = [
        pltpu.make_async_copy(modes_ref, out_ref.at[level], sems.at[level])
        for level, modes_ref in enumerate(kept)
    ]
    for copy in copies:
        copy.start()
    half_own, half_other = merge(total_of(parts), sketch_ref)
    halves_ref[0] = half_own.astype(BF16)
    halves_ref[1] = half_other.astype(BF16)
    for copy in copies:
        copy.wait()


def apply_kernel(halves_ref, slices_ref, image_own, came_ref, shared_ref, far_t, shared_t, *refs):
    image_other = choose("tm", came_ref[...], shared_ref[...])[1]
    image = combined(image_own[...], image_other, halves_ref[0], halves_ref[1])
    write_probes(refs, slices_ref[...].astype(BF16), far_t, shared_t, image)


def modes_kernel(halves_ref, modes_own, came_ref, shared_ref, *refs):
    *image_ref, modes_ref, outgoing_ref = refs
    modes_other = choose("tm", came_ref[...], shared_ref[...])[0]
    modes = combined(modes_own[...], modes_other, halves_ref[0], halves_ref[1])
    write_bulk((modes_ref, outgoing_ref), modes, image_ref[0] if image_ref else None)


def output_kernel(halves_ref, modes_own, *refs):
    *quarters, _, out_ref, modes_ref, sems = refs
    rows = modes_own.shape[0]
    modes_other = read_modes(*quarters)
    part = rows // 2
    copies = []
    for half in range(2):
        span = slice(half * part, (half + 1) * part)
        modes_ref[span] = combined(
            modes_own[span], modes_other[span], halves_ref[0], halves_ref[1]
        )
        copies.append(
            pltpu.make_async_copy(
                modes_ref.at[pl.ds(half * part, part)],
                out_ref.at[out_ref.shape[0] - 1, pl.ds(half * part, part)],
                sems.at[half],
            )
        )
        copies[-1].start()
    for copy in copies:
        copy.wait()


def last_level(parts, sketch_t, kept, halves_shape):
    rows, width = kept[0].shape
    levels = len(kept)
    vmem = pl.BlockSpec(memory_space=pltpu.VMEM)
    hbm = pl.BlockSpec(memory_space=pltpu.HBM)
    return pl.pallas_call(
        functools.partial(last_merge_kernel, len(parts)),
        out_shape=[halves_shape, jax.ShapeDtypeStruct((levels + 1, rows, width), BF16)],
        in_specs=[vmem] * (len(parts) + 1 + levels),
        out_specs=[vmem, hbm],
        scratch_shapes=[pltpu.SemaphoreType.DMA((levels,))],
        compiler_params=PARAMS,
    )(*parts, sketch_t, *kept)


def last_modes(halves, modes, quarters, out):
    vmem = pl.BlockSpec(memory_space=pltpu.VMEM)
    hbm = pl.BlockSpec(memory_space=pltpu.HBM)
    return pl.pallas_call(
        output_kernel,
        out_shape=jax.ShapeDtypeStruct(out.shape, BF16),
        in_specs=[vmem] * 6 + [hbm],
        out_specs=hbm,
        scratch_shapes=[pltpu.VMEM(modes.shape, BF16), pltpu.SemaphoreType.DMA((2,))],
        input_output_aliases={6: 0},
        compiler_params=PARAMS,
    )(halves, modes, *quarters, out)


def cross_kernel(total_rows, *refs):
    *arrivals, out_ref = refs
    out_ref[...] = cross_of(total_rows, *arrivals).astype(BF16)


def modes_of(snapshots, energy, neighbours, sketch):
    block_count, _, block_rows, _ = energy.shape
    rows_dev, width = snapshots.shape
    space = lax.axis_size("space")
    total_rows = rows_dev * space
    levels = sketch.shape[0]
    blocks = snapshots.reshape(block_count, block_rows, width)
    head, tail = blocks[:HB], blocks[block_count - HB :]
    odd = (lax.axis_index("space") & 1) == 1
    near = [(i, i ^ 1) for i in range(space)]
    wide = [(i, (i + 2 * (i % 2) - 1) % space) for i in range(space)]
    came_near = lax.ppermute(jnp.where(odd, head, tail), "space", near)
    came_wide = lax.ppermute(jnp.where(odd, tail, head), "space", wide)
    modes_shape = jax.ShapeDtypeStruct((rows_dev, width), BF16)
    quarter_shape = jax.ShapeDtypeStruct((rows_dev // 4, width), BF16)
    factor_shape = jax.ShapeDtypeStruct((width + width // 2, width), F32)
    half_square = jax.ShapeDtypeStruct((width, width), BF16)
    pair_square = jax.ShapeDtypeStruct((2 * width, width), BF16)
    slices_shape = jax.ShapeDtypeStruct((2 * width, width), F32)
    halves_shape = jax.ShapeDtypeStruct((2, width, width), BF16)

    inner, sketch_t, edges, blocks = interior_of(neighbours, energy, blocks, sketch)
    image, image_t, gram = edge_of(neighbours, edges, came_near, blocks, came_wide, inner)
    other_image = swap(image, "tm", 1)
    pair = run_kernel(
        pair_kernel,
        factor_shape, gram, image_t, other_image,
    )
    parts = summands(pair, "space", space, 4)
    far_images = [swap(image_t, "tm", 2**level) for level in range(1, levels)]
    factor = run_kernel(
        functools.partial(leaf_kernel, total_rows, len(parts)), factor_shape, *parts
    )
    other_factor = swap(factor, "tm", 1)
    modes = run_kernel(
        leaf_modes_kernel, modes_shape, blocks.reshape(rows_dev, width), factor
    )
    other = swap(modes, "tm", 1)
    kept = [modes]
    for level in range(levels):
        last = level + 1 == levels
        deep = level + 2 < levels
        probe_outs = [pair_square] * 2 + ([modes_shape] if deep else [])
        modes_outs = [modes_shape, modes_shape if deep else quarter_shape]
        if level > 0:
            quarter = space // 4
            if quarter > 1:
                parts = summands(probes, "space", quarter, 4)
                probes = run_kernel(add_kernel, pair_square, *parts)
                second = run_kernel(pick_kernel, pair_square, probes, slices)
            one = mixed_swap(probes, (0, quarter), (0, 2 * quarter))
            two = mixed_swap(second, (0, 3 * quarter), (2**level, 0))
            came = swap(outgoing, "tm", 2**level)
            shared = swap(came, "tm", 1)
            arrivals = [
                probes, one, two,
                swap(one, "tm", 1), swap(two, "tm", 1),
            ]
            if level > 1:
                cross = run_kernel(
                    functools.partial(cross_kernel, total_rows), half_square, *arrivals
                )
                parts = summands(cross, "tm", 2**level, 2, done=2)
        outs = [halves_shape, slices_shape]
        if level == 0:
            halves, slices = run_kernel(
                first_merge_kernel, outs, factor, other_factor, sketch_t[level]
            )
        elif last:
            halves, out = last_level(parts, sketch_t[level], kept, halves_shape)
        elif level == 1:
            halves, slices = run_kernel(
                functools.partial(near_merge_kernel, total_rows), outs,
                *arrivals, sketch_t[level], slices,
            )
        else:
            halves, slices = run_kernel(
                functools.partial(merge_kernel, len(parts)), outs,
                *parts, sketch_t[level], slices,
            )
        if last:
            far_quarters = [swap(came, "tm", 2), swap(came, "tm", 3)]
            out = last_modes(halves, modes, [came, shared, *far_quarters], out)
            break
        far = far_images[level]
        far_shared = swap(far, "tm", 1)
        if level == 0:
            probes, second, *image = run_kernel(
                first_apply_kernel, probe_outs,
                slices, image, other_image, far, far_shared,
            )
        else:
            probes, second, *image = run_kernel(
                apply_kernel, probe_outs,
                halves, slices, image[0], came, shared, far, far_shared,
            )
        if level == 0:
            modes, outgoing = run_kernel(
                first_modes_kernel, modes_outs, halves, modes, other, *image
            )
        else:
            modes, outgoing = run_kernel(
                modes_kernel, modes_outs, halves, modes, came, shared, *image
            )
        kept.append(modes)
    return out[:, None]


def solution(mesh):
    placed = (P("space", "tm"), P("space", None, None, None), P("space", None), P())
    return jax.shard_map(
        modes_of,
        mesh=mesh,
        in_specs=placed,
        out_specs=P(None, "tm", "space", None),
        check_vma=False,
    )
```
